32 devices in a mesh: row: 8 (over z, y), col: 4 (over x, core).
Axes of the slice: x: 2, y: 2, z: 4, core: 2. Of those that a mesh axis runs over, the one named last changes fastest.
Arguments:
- current_image: float32 [16, 1024, 1024], P(None, 'row', 'col'), may hold values from -6 to 6
- measured: float32 [16, 8, 16, 128], P('col', 'row'), may hold values from -6 to 6
- ray_weight: float32 [16, 8, 128], P('col', 'row'), may hold values from 0.25 to 4
- angle_ids: int32 [16], replicated, may hold values from 0 to 255, as said below
- shadow_start: int32 [8, 8, 16], replicated, may hold values from 0 to 896, as said below
Outputs:
- smoothed_image: float32 [16, 1024, 1024], P(None, 'row', 'col')
The draws below stay inside these ranges and needn't reach their ends.
Inputs may be any that keep to these rules, and one draw needn't show every extreme that they name: `angle_ids`: distinct angle numbers. `shadow_start`: the shadow of a tile covers the 128 detector bins from this bin on, so it touches one or two detector blocks.
All inputs are finite; a program needn't handle non-finite values.
Results may differ from the reference program's by a relative error of at most 0.0033.
Values may be sent and summed in bfloat16 or wider, within the bound.
A program may use at most 64 MiB of HBM per device.

```python
import math
import jax
import jax.numpy as jnp
from jax import lax

TILE = 128
SLICES = 16
ANGLES = 16
ALL_ANGLES = 256
TV_STEPS = 4
SIDE_TILES = 8
IMG = 1024
BLOCKS = 8
DET = 1024
N_ROW = 8


def angle_helper(key):
    stride = ALL_ANGLES // ANGLES
    offset = jax.random.randint(jax.random.fold_in(key, 11), (), 0, stride)
    return (offset + stride * jnp.arange(ANGLES, dtype=jnp.int32)).astype(jnp.int32)


def draw_angle_ids(key, part):
    return angle_helper(key)


def draw_shadow_start(key, part):
    total = SIDE_TILES * SIDE_TILES * ANGLES
    starts = jax.random.randint(jax.random.fold_in(key, 23), (total,), 0, DET - TILE + 1)
    places = jax.random.permutation(jax.random.fold_in(key, 29), total)
    starts = starts.at[places[0]].set(0)
    starts = starts.at[places[1]].set(DET - TILE)
    return starts.reshape(SIDE_TILES, SIDE_TILES, ANGLES).astype(jnp.int32)


def shard_levels(own_key, extent, pieces, low, high):
    factor_of, own = 1.0, jax.random.fold_in(own_key, 6)
    for axis_at, blocks in pieces:
        draws = jnp.exp(jax.random.uniform(jax.random.fold_in(own, axis_at), (blocks,), jnp.float32, low / len(pieces), high / len(pieces)))
        factor_of = factor_of * jnp.repeat(draws, extent[axis_at] // blocks).reshape([-1 if axis == axis_at else 1 for axis in range(len(extent))])
    return factor_of


def bell_draw(own_key, extent, scale, limit, split=(), held_as=jnp.bfloat16):
    values = scale * jax.random.normal(own_key, extent, jnp.float32)
    if split:
        values = values * shard_levels(own_key, extent, split, -0.22, 0.18)
    return jnp.clip(values, -limit, limit).astype(held_as)


def setup_inputs(seed: int = 0) -> dict:
    arg_keys = jax.random.split(jax.random.key(seed), 6)
    return {
        "current_image": bell_draw(arg_keys[0], (SLICES, IMG, IMG), 1.0, 6.0, ((1, 8), (2, 4)), jnp.float32),
        "measured": bell_draw(arg_keys[1], (ANGLES, BLOCKS, SLICES, TILE), 1.0, 6.0, ((0, 4), (1, 8)), jnp.float32),
        "ray_weight": jnp.clip(jnp.exp(math.log(4.0) - 2.7725887 * jax.random.uniform(arg_keys[2], (ANGLES, BLOCKS, TILE), jnp.float32) ** shard_levels(arg_keys[2], (ANGLES, BLOCKS, TILE), ((0, 4), (1, 8)), -0.2, 0.2)), 0.25, 4.0),
        "angle_ids": draw_angle_ids(jax.random.fold_in(arg_keys[5], 71), 0),
        "shadow_start": draw_shadow_start(jax.random.fold_in(arg_keys[5], 71), 0),
    }


inverse_root = 0.7071067811865476
proj_scale = 0.03125
relaxation = 8.0
smoothing = 0.25
descent_step = 0.05

def tile_weights(angle_number):
    radians = angle_number.astype(jnp.float32) * (math.pi / ALL_ANGLES)
    cosine = jnp.cos(radians)
    sine_value = jnp.sin(radians)
    centre = (TILE - 1) / 2.0
    position = jnp.arange(TILE, dtype=jnp.float32) - centre
    along_bins = TILE / 2.0 + (position[:, None] * cosine + position[None, :] * sine_value) * inverse_root
    centres = jnp.arange(TILE, dtype=jnp.float32) + 0.5
    hat_values = jnp.maximum(0.0, 1.0 - jnp.abs(along_bins.reshape(-1, 1) - centres[None, :]))
    return (hat_values * proj_scale).astype(jnp.bfloat16)

def ramp(offset):
    is_odd = offset % 2 != 0
    nonzero = jnp.where(offset == 0, 1, offset).astype(jnp.float32)
    values = jnp.where(is_odd, -1.0 / (math.pi * math.pi * nonzero * nonzero), 0.0)
    values = jnp.where(offset == 0, 0.25, values)
    return jnp.where(jnp.abs(offset) < TILE, values, 0.0).astype(jnp.float32)

def tv_gradient(padded):
    corner = padded[:, :-1, :-1]
    step_down = padded[:, 1:, :-1] - corner
    step_right = padded[:, :-1, 1:] - corner
    magnitude = jnp.sqrt(smoothing * smoothing + step_down * step_down + step_right * step_right)
    flow_down = step_down / magnitude
    flow_right = step_right / magnitude
    return flow_down[:, :-1, 1:] - flow_down[:, 1:, 1:] + flow_right[:, 1:, :-1] - flow_right[:, 1:, 1:]

def reference(current_image, measured, ray_weight, angle_ids, shadow_start):
    count = N_ROW * N_ROW
    tile_data = current_image.reshape(SLICES, N_ROW, TILE, N_ROW, TILE).transpose(1, 3, 0, 2, 4)
    tile_data = tile_data.reshape(count * SLICES, TILE * TILE).astype(jnp.bfloat16).astype(jnp.float32)
    starts = shadow_start.reshape(count, ANGLES)
    offsets = jnp.arange(TILE, dtype=jnp.int32)

    def project(angle_index):
        weights = tile_weights(angle_ids[angle_index]).astype(jnp.float32)
        partial_value = jnp.dot(tile_data, weights, precision=lax.Precision.HIGHEST)
        partial_value = partial_value.reshape(count, SLICES, TILE).transpose(1, 0, 2).reshape(SLICES, count * TILE)
        bin_index = (starts[:, angle_index][:, None] + offsets[None, :]).reshape(-1)
        return jnp.zeros((SLICES, DET), jnp.float32).at[:, bin_index].add(partial_value)
    ray_sums = lax.map(project, jnp.arange(ANGLES, dtype=jnp.int32))
    natural = measured.transpose(0, 2, 1, 3).reshape(ANGLES, SLICES, DET)
    weight_rows = ray_weight.reshape(ANGLES, 1, DET)
    residual = weight_rows * (natural - ray_sums)
    detector = jnp.arange(DET, dtype=jnp.int32)
    ramp_table = ramp(detector[None, :] - detector[:, None])
    filtered = jnp.einsum('asi,ij->asj', residual, ramp_table, precision=lax.Precision.HIGHEST)
    filtered = filtered.astype(jnp.bfloat16).astype(jnp.float32)

    def accumulate(angle_index, running):
        weights = tile_weights(angle_ids[angle_index]).astype(jnp.float32)
        bin_index = starts[:, angle_index][:, None] + offsets[None, :]
        shadow = filtered[angle_index][:, bin_index]
        shadow = shadow.transpose(1, 0, 2).reshape(count * SLICES, TILE)
        return running + jnp.dot(shadow, weights.T, precision=lax.Precision.HIGHEST)
    update = lax.fori_loop(0, ANGLES, accumulate, jnp.zeros((count * SLICES, TILE * TILE), jnp.float32))
    update = update.reshape(N_ROW, N_ROW, SLICES, TILE, TILE).transpose(2, 0, 3, 1, 4).reshape(SLICES, IMG, IMG)
    current = current_image + relaxation * update
    for repeat in range(TV_STEPS):
        padded = jnp.pad(current, ((0, 0), (1, 1), (1, 1)))
        current = current - descent_step * tv_gradient(padded)
    return current
```

```python
import math

import jax
import jax.numpy as jnp
import numpy as np
from jax import lax
from jax.experimental import pallas as pl
from jax.experimental.pallas import tpu as pltpu
from jax.sharding import PartitionSpec as P

TILE = 128
ANGLES = 16
ALL_ANGLES = 256
TV_STEPS = 4
PACK = TILE // TV_STEPS

HIGH = 8
WIDE = 16
BINS = 16
MARGIN = 8
DEPTH = MARGIN + TILE + BINS
GROUPS = 4
GROUP_ROWS = TILE // GROUPS
DOWN = GROUP_ROWS // HIGH
RIGHT = TILE // WIDE
QUAD = 4

inverse_root = 0.7071067811865476
proj_scale = 0.03125
relaxation = 8.0
smoothing = 0.25
descent_step = 0.05

MESH = pl.DeviceIdType.MESH
SMEM = pl.BlockSpec(memory_space=pltpu.SMEM)
VMEM = pl.BlockSpec(memory_space=pltpu.VMEM)
ANY = pl.BlockSpec(memory_space=pl.ANY)


def lookup(table, index):
    return jnp.take_along_axis(table, index, axis=1, mode="promise_in_bounds")


def lane_iota():
    return lax.broadcasted_iota(jnp.int32, (8, TILE), 1)


def row_iota():
    return lax.broadcasted_iota(jnp.int32, (8, TILE), 0)


def geometry(angle_ids):
    radians = angle_ids.astype(jnp.float32) * (math.pi / ALL_ANGLES)
    down = jnp.cos(radians) * inverse_root
    right = jnp.sin(radians) * inverse_root
    centre = (TILE - 1) / 2.0
    row = jnp.arange(DOWN)[:, None] * HIGH + jnp.arange(GROUPS)[None, :] * GROUP_ROWS
    row = (row.astype(jnp.float32) - centre)[:, None, :, None]
    column = (jnp.arange(RIGHT) * WIDE).astype(jnp.float32)[None, :, None, None] - centre
    place = TILE / 2.0 + row * down + column * right
    lowest = place + jnp.minimum(0.0, (HIGH - 1) * down) + jnp.minimum(0.0, (WIDE - 1) * right)
    first = jnp.floor(lowest - 0.5)
    offset = place - first - 0.5
    shape = (DOWN * RIGHT, GROUPS * ANGLES)
    first = first.astype(jnp.int32) + MARGIN
    return jnp.stack([down, right]), first.reshape(shape), offset.reshape(shape)


def lane_orders(angles_here, slices_here, slices, across):
    rows = slices // slices_here
    to_owner = []
    for sub in range(QUAD // angles_here):
        for r in range(rows):
            for t in range(across):
                for a in range(angles_here):
                    for s in range(slices_here):
                        angle = sub * angles_here + a
                        to_owner.append((angle * across + t) * slices + r * slices_here + s)
    to_owner = np.array(to_owner, np.int32)
    back = np.argsort(to_owner).astype(np.int32)
    return to_owner, back


def row_shifts(shift_ref, quad, to_owner, slices, across, eight):
    rows = row_iota()
    keys = [int(to_owner[eight * 8 + r]) // slices for r in range(8)]
    result = jnp.full((8, TILE), shift_ref[quad * QUAD + keys[0] // across, keys[0] % across], jnp.int32)
    for r in range(1, 8):
        if keys[r] != keys[r - 1]:
            value = shift_ref[quad * QUAD + keys[r] // across, keys[r] % across]
            result = jnp.where(rows >= r, value, result)
    return result


def hat(distance):
    return jnp.maximum(1.0 - jnp.abs(distance), 0.0).astype(jnp.bfloat16)


def to_pixels(z_ref, ur, across, slices):
    parts = []
    for g in range(GROUPS):
        for t in range(across):
            for s in range(0, slices, 8):
                start = s * TILE + g * GROUP_ROWS + ur
                parts.append(z_ref[t, pl.ds(start, 8, stride=TILE), :])
    return jnp.concatenate(parts, axis=0).T


def forward_kernel(
    first_ref, offset_ref, slope_ref, shift_ref, order_ref, x_ref, out_ref, xt_ref,
    z_ref, xb_ref, acc_ref, q_ref, sems,
    *, slices, across, angles_here, slices_here, tile_rows,
):
    copies = [
        pltpu.make_async_copy(
            x_ref.at[:, pl.ds(t * TILE, TILE)], z_ref.at[t], sems.at[t]
        )
        for t in range(across)
    ]
    for copy in copies:
        copy.start()

    pixel = lax.broadcasted_iota(jnp.int32, (BINS, TILE), 1)
    bins = lax.broadcasted_iota(jnp.int32, (BINS, TILE), 0).astype(jnp.float32)
    pixel_row = (pixel // WIDE).astype(jnp.float32)
    pixel_column = (pixel % WIDE).astype(jnp.float32)
    for a in range(ANGLES):
        q_ref[a] = pixel_row * slope_ref[0, a] + pixel_column * slope_ref[1, a] - bins

    def clear(k, carry):
        acc_ref[k] = jnp.zeros((DEPTH, TILE), jnp.float32)
        return carry

    lax.fori_loop(0, GROUPS * ANGLES, clear, jnp.int32(0))
    for copy in copies:
        copy.wait()

    def turn(ur, carry):
        value = to_pixels(z_ref, ur, across, slices)
        xt_ref[ur] = value
        xb_ref[ur] = value.astype(jnp.bfloat16)
        return carry

    lax.fori_loop(0, GROUP_ROWS, turn, jnp.int32(0), unroll=2)

    def block(i, carry):
        top = (i // RIGHT) * HIGH
        left = pl.multiple_of((i % RIGHT) * WIDE, WIDE)
        pixels = jnp.concatenate(
            [xb_ref[top + k, pl.ds(left, WIDE), :] for k in range(HIGH)], axis=0
        )
        for g in range(GROUPS):
            weights = jnp.concatenate(
                [hat(q_ref[a] + offset_ref[i, g * ANGLES + a]) for a in range(ANGLES)], axis=0
            )
            shadow = jnp.dot(weights, pixels, preferred_element_type=jnp.float32)
            for a in range(ANGLES):
                span = pl.ds(first_ref[i, g * ANGLES + a], BINS)
                k = g * ANGLES + a
                acc_ref[k, span, :] = acc_ref[k, span, :] + shadow[a * BINS : (a + 1) * BINS]
        return carry

    lax.fori_loop(0, DOWN * RIGHT, block, jnp.int32(0))

    width = TILE // GROUPS
    lanes = lane_iota()
    group = lanes // width
    to_owner, back = lane_orders(angles_here, slices_here, slices, across)
    order = order_ref[...]
    per_owner = across * angles_here * slices_here
    per_tile = angles_here * slices_here
    owners = slices // slices_here
    cols = ANGLES // angles_here
    for quad in range(ANGLES // QUAD):
        pieces = []
        for b in range(TILE // 8):
            span = slice(MARGIN + b * 8, MARGIN + b * 8 + 8)
            total = None
            for k in range(GROUPS):
                part = None
                for g in range(GROUPS):
                    angle = quad * QUAD + (g + k) % GROUPS
                    value = acc_ref[g * ANGLES + angle, span, :]
                    part = value if part is None else jnp.where(group == g, value, part)
                if k:
                    part = pltpu.roll(part, width * k, 1)
                total = part if total is None else total + part
            pieces.append(lookup(total, order))
        rows = jnp.concatenate(pieces, axis=0).T
        sent = []
        for e in range(TILE // 8):
            shift = row_shifts(shift_ref, quad, to_owner, slices, across, e)
            value = lookup(rows[e * 8 : e * 8 + 8], (lanes - shift) & (TILE - 1))
            sent.append(value * proj_scale)
        flat = jnp.concatenate(sent, axis=0)
        for sub in range(QUAD // angles_here):
            col = quad * (QUAD // angles_here) + sub
            for r in range(owners):
                at = (sub * owners + r) * per_owner
                parts = []
                for t in range(across):
                    parts.append(flat[at + t * per_tile : at + (t + 1) * per_tile])
                    if tile_rows > per_tile:
                        parts.append(jnp.zeros((tile_rows - per_tile, TILE), jnp.float32))
                message = jnp.concatenate(parts, axis=0)
                out_ref[r * cols + col] = message.astype(jnp.bfloat16)


def tile_rows_of(angles_here, slices_here):
    return pl.cdiv(angles_here * slices_here, 8) * 8


def project(image, first, offset, slopes, shift):
    row_count = lax.axis_size("row")
    col_count = lax.axis_size("col")
    slices, height, width = image.shape
    across = width // TILE
    angles_here = ANGLES // col_count
    slices_here = slices // row_count
    tile_rows = tile_rows_of(angles_here, slices_here)
    order = np.broadcast_to(lane_orders(angles_here, slices_here, slices, across)[0], (8, TILE))
    kernel = lambda *refs: forward_kernel(
        *refs, slices=slices, across=across, angles_here=angles_here,
        slices_here=slices_here, tile_rows=tile_rows,
    )
    return pl.pallas_call(
        kernel,
        out_shape=[
            jax.ShapeDtypeStruct((row_count * col_count, across * tile_rows, TILE), jnp.bfloat16),
            jax.ShapeDtypeStruct((GROUP_ROWS, TILE, TILE), jnp.float32),
        ],
        in_specs=[SMEM] * 4 + [VMEM, ANY],
        out_specs=[VMEM, VMEM],
        scratch_shapes=[
            pltpu.VMEM((across, slices * height, TILE), jnp.float32),
            pltpu.VMEM((GROUP_ROWS, TILE, TILE), jnp.bfloat16),
            pltpu.VMEM((GROUPS * ANGLES, DEPTH, TILE), jnp.float32),
            pltpu.VMEM((ANGLES, BINS, TILE), jnp.float32),
            pltpu.SemaphoreType.DMA((across,)),
        ],
        compiler_params=pltpu.CompilerParams(vmem_limit_bytes=48 << 20),
        name="project",
    )(first, offset, slopes, shift, jnp.asarray(order), image.reshape(slices * height, width))


def ramp_table():
    bins = np.arange(TILE)
    tables = []
    for n in (-1, 0, 1):
        gap = bins[None, :] - bins[:, None] - n * TILE
        nonzero = np.where(gap == 0, 1, gap).astype(np.float64)
        value = np.where(gap % 2 != 0, -1.0 / (math.pi * math.pi * nonzero * nonzero), 0.0)
        value = np.where(gap == 0, 0.25, value)
        tables.append(np.where(np.abs(gap) < TILE, value, 0.0))
    return np.concatenate(tables, axis=0).astype(np.float32)


def exchange_kernel(
    starts_ref, sent_ref, measured_ref, ramp_ref, out_ref,
    landed, scan, target_ref, outgoing, returned,
    shadow_sems, scan_sems, window_sems,
    *, angles_here, slices_here, across, tile_rows,
):
    rows = lax.axis_size("row")
    cols = lax.axis_size("col")
    row = lax.axis_index("row")
    col = lax.axis_index("col")
    count = rows * cols
    me = row * cols + col

    def send(src, dst, sems, k, to):
        return pltpu.make_async_remote_copy(
            src_ref=src, dst_ref=dst, send_sem=sems.at[0, k], recv_sem=sems.at[1, k],
            device_id=(to // cols, to % cols), device_id_type=MESH,
        )

    barrier = pltpu.get_barrier_semaphore()

    def greet(k, carry):
        to = lax.rem(me + k, count)
        pl.semaphore_signal(barrier, inc=1, device_id=(to // cols, to % cols), device_id_type=MESH)
        return carry

    lax.fori_loop(1, count, greet, jnp.int32(0))

    lanes = lane_iota()
    sublanes = row_iota()

    def aim(k, carry):
        peer = lax.rem(me + k, count)
        down, right = peer // cols, peer % cols
        for t in range(across):
            start = jnp.zeros((8, TILE), jnp.int32)
            for a in range(angles_here):
                value = starts_ref[down, (right * across + t) * ANGLES + col * angles_here + a]
                start = jnp.where(sublanes >= a * slices_here, value, start)
            block = (start >> 7) + jnp.where(lanes < (start & (TILE - 1)), 1, 0)
            target_ref[k, t] = block
        return carry

    lax.fori_loop(0, count, aim, jnp.int32(0), unroll=2)
    pl.semaphore_wait(barrier, count - 1)

    def shadow_copy(k):
        to = lax.rem(me + k, count)
        return send(sent_ref.at[to], landed.at[k], shadow_sems, k, to)

    def scan_copy(k):
        down = lax.rem(row + k, rows)
        return send(measured_ref.at[down], scan.at[k], scan_sems, k, down * cols + col)

    def start(copy):
        def body(k, carry):
            copy(k).start()
            return carry

        return body

    lax.fori_loop(1, count, start(shadow_copy), jnp.int32(0))
    lax.fori_loop(1, rows, start(scan_copy), jnp.int32(0))
    landed[0] = sent_ref[me]
    scan[0] = measured_ref[row]

    def add(k, sums):
        other = lax.rem(count - k, count)
        message = landed[k].astype(jnp.float32)
        for t in range(across):
            value = message[t * tile_rows : (t + 1) * tile_rows]
            target = target_ref[other, t]
            sums = tuple(
                total + jnp.where(target == b, value, 0.0) for b, total in enumerate(sums)
            )
        return sums

    zero = jnp.zeros((tile_rows, TILE), jnp.float32)
    sums = add(0, (zero,) * rows)

    def add_next(k, sums):
        shadow_copy(k).wait_recv()
        return add(k, sums)

    sums = lax.fori_loop(1, count, add_next, sums)

    def wait_scan(k, carry):
        scan_copy(k).wait_recv()
        return carry

    lax.fori_loop(1, rows, wait_scan, jnp.int32(0))
    residual = []
    for b in range(rows):
        here = scan[lax.rem(row - b + rows, rows)]
        residual.append(here[tile_rows:] * (here[:tile_rows] - sums[b]))
    stacked = jnp.concatenate(
        [
            jnp.concatenate([zero] + residual[:-1], axis=0),
            jnp.concatenate(residual, axis=0),
            jnp.concatenate(residual[1:] + [zero], axis=0),
        ],
        axis=1,
    )
    filtered = jnp.dot(
        stacked, ramp_ref[...], precision=lax.Precision.HIGHEST,
        preferred_element_type=jnp.float32,
    )
    blocks = tuple(filtered[b * tile_rows : (b + 1) * tile_rows] for b in range(rows))

    def window(k):
        parts = []
        for t in range(across):
            target = target_ref[k, t]
            value = zero
            for b in range(rows):
                value = jnp.where(target == b, blocks[b], value)
            parts.append(value)
        return jnp.concatenate(parts, axis=0).astype(jnp.bfloat16)

    def window_copy(k):
        to = lax.rem(me + k, count)
        return send(outgoing.at[k], returned.at[me], window_sems, k, to)

    def reply(k, carry):
        outgoing[k] = window(k)
        window_copy(k).start()
        return carry

    lax.fori_loop(1, count, reply, jnp.int32(0))
    returned[me] = window(0)

    def finish(k, carry):
        window_copy(k).wait_recv()
        return carry

    lax.fori_loop(1, count, finish, jnp.int32(0))
    out_ref[...] = returned[...]

    def settle(k, carry):
        shadow_copy(k).wait_send()
        window_copy(k).wait_send()
        return carry

    lax.fori_loop(1, count, settle, jnp.int32(0))

    def settle_scan(k, carry):
        scan_copy(k).wait_send()
        return carry

    lax.fori_loop(1, rows, settle_scan, jnp.int32(0))


def exchange(sent, measured, ray_weight, shadow_start, slices):
    rows = lax.axis_size("row")
    cols = lax.axis_size("col")
    angles_here = ANGLES // cols
    slices_here = slices // rows
    tile_rows = tile_rows_of(angles_here, slices_here)
    count, depth, unused = sent.shape
    across = depth // tile_rows
    per_tile = angles_here * slices_here
    natural = measured.reshape(angles_here, rows, slices_here, TILE).transpose(1, 0, 2, 3)
    weight = jnp.broadcast_to(ray_weight.reshape(1, angles_here, 1, TILE), natural.shape)
    scan = jnp.stack([natural, weight], axis=1).reshape(rows, 2, per_tile, TILE)
    scan = jnp.pad(scan, ((0, 0), (0, 0), (0, tile_rows - per_tile), (0, 0)))
    scan = scan.reshape(rows, 2 * tile_rows, TILE)
    dma = pltpu.SemaphoreType.DMA
    kernel = lambda *refs: exchange_kernel(
        *refs, angles_here=angles_here, slices_here=slices_here, across=across, tile_rows=tile_rows
    )
    return pl.pallas_call(
        kernel,
        out_shape=jax.ShapeDtypeStruct(sent.shape, jnp.bfloat16),
        in_specs=[SMEM, VMEM, VMEM, VMEM],
        out_specs=VMEM,
        scratch_shapes=[
            pltpu.VMEM(sent.shape, jnp.bfloat16),
            pltpu.VMEM(scan.shape, jnp.float32),
            pltpu.VMEM((count, across, tile_rows, TILE), jnp.int32),
            pltpu.VMEM(sent.shape, jnp.bfloat16),
            pltpu.VMEM(sent.shape, jnp.bfloat16),
            dma((2, count)),
            dma((2, rows)),
            dma((2, count)),
        ],
        compiler_params=pltpu.CompilerParams(collective_id=0, has_side_effects=True),
        name="exchange",
    )(shadow_start.reshape(rows, -1), sent, scan, jnp.asarray(ramp_table()))


def backward_kernel(
    first_ref, slope_ref, shift_ref, order_ref, offset_ref, shadow_ref, x_ref, out_ref,
    row_edge_ref, col_edge_ref, store_ref, q_ref,
    *, slices, across, angles_here, slices_here, tile_rows,
):
    width = TILE // GROUPS
    lanes = lane_iota()
    group = lanes // width
    to_owner, back = lane_orders(angles_here, slices_here, slices, across)
    order = order_ref[...]
    per_owner = across * angles_here * slices_here
    per_tile = angles_here * slices_here
    owners = slices // slices_here
    cols = ANGLES // angles_here
    for k in range(GROUPS * ANGLES):
        store_ref[k, 0:MARGIN, :] = jnp.zeros((MARGIN, TILE), jnp.float32)
        store_ref[k, MARGIN + TILE :, :] = jnp.zeros((DEPTH - MARGIN - TILE, TILE), jnp.float32)
    pixel = lax.broadcasted_iota(jnp.int32, (TILE, 1), 0)
    pixel_row = (pixel // WIDE).astype(jnp.float32)
    pixel_column = (pixel % WIDE).astype(jnp.float32)
    full = ANGLES * BINS
    bins = (lax.broadcasted_iota(jnp.int32, (1, full), 1) % BINS).astype(jnp.float32)
    q_ref[...] = pixel_row * slope_ref[0:1, :] + pixel_column * slope_ref[1:2, :] - bins

    for quad in range(ANGLES // QUAD):
        parts = []
        for sub in range(QUAD // angles_here):
            col = quad * (QUAD // angles_here) + sub
            for r in range(owners):
                message = shadow_ref[r * cols + col].astype(jnp.float32)
                for t in range(across):
                    parts.append(message[t * tile_rows : t * tile_rows + per_tile])
        flat = jnp.concatenate(parts, axis=0)
        turned = []
        for e in range(TILE // 8):
            shift = row_shifts(shift_ref, quad, to_owner, slices, across, e)
            turned.append(lookup(flat[e * 8 : e * 8 + 8], (lanes + shift) & (TILE - 1)))
        rows = jnp.concatenate(turned, axis=0).T
        for b in range(TILE // 8):
            span = slice(MARGIN + b * 8, MARGIN + b * 8 + 8)
            value = lookup(rows[b * 8 : b * 8 + 8], order)
            for k in range(GROUPS):
                moved = pltpu.roll(value, width * k, 1) if k else value
                for a in range(QUAD):
                    g = (a + k) % GROUPS
                    store_ref[g * ANGLES + quad * QUAD + a, span, :] = jnp.where(
                        group == g, moved, 0.0
                    )

    def block(i, carry):
        top = (i // RIGHT) * HIGH
        left = pl.multiple_of((i % RIGHT) * WIDE, WIDE)
        total = None
        for g in range(GROUPS):
            shadows = jnp.concatenate(
                [
                    store_ref[g * ANGLES + a, pl.ds(first_ref[i, g * ANGLES + a], BINS), :]
                    for a in range(ANGLES)
                ],
                axis=0,
            ).astype(jnp.bfloat16)
            weights = hat(q_ref[...] + offset_ref[pl.ds(i * GROUPS + g, 1), :])
            part = jnp.dot(weights, shadows, preferred_element_type=jnp.float32)
            total = part if total is None else total + part
        total = total * (relaxation * proj_scale)
        for k in range(HIGH):
            out_ref[top + k, pl.ds(left, WIDE), :] = (
                x_ref[top + k, pl.ds(left, WIDE), :] + total[k * WIDE : (k + 1) * WIDE]
            )
        return carry

    lax.fori_loop(0, DOWN * RIGHT, block, jnp.int32(0))
    pack_edges(out_ref, row_edge_ref, col_edge_ref, slices)


def back_project(shadows, x, first, offset, slopes, shift, slices):
    row_count = lax.axis_size("row")
    col_count = lax.axis_size("col")
    across = shift.shape[1]
    angles_here = ANGLES // col_count
    slices_here = slices // row_count
    tile_rows = tile_rows_of(angles_here, slices_here)
    order = np.broadcast_to(lane_orders(angles_here, slices_here, slices, across)[1], (8, TILE))
    kernel = lambda *refs: backward_kernel(
        *refs, slices=slices, across=across, angles_here=angles_here,
        slices_here=slices_here, tile_rows=tile_rows,
    )
    wide = jnp.repeat(offset.reshape(DOWN * RIGHT * GROUPS, ANGLES), BINS, axis=1)
    return pl.pallas_call(
        kernel,
        out_shape=[
            jax.ShapeDtypeStruct(x.shape, jnp.float32),
            jax.ShapeDtypeStruct((2, TILE, TILE), jnp.bfloat16),
            jax.ShapeDtypeStruct((2, GROUP_ROWS // 4, 16, TILE), jnp.bfloat16),
        ],
        in_specs=[SMEM, VMEM, SMEM] + [VMEM] * 4,
        out_specs=[VMEM] * 3,
        scratch_shapes=[
            pltpu.VMEM((GROUPS * ANGLES, DEPTH, TILE), jnp.float32),
            pltpu.VMEM((TILE, ANGLES * BINS), jnp.float32),
        ],
        compiler_params=pltpu.CompilerParams(vmem_limit_bytes=48 << 20),
        name="back_project",
    )(first, jnp.repeat(slopes, BINS, axis=1), shift, jnp.asarray(order), wide, shadows, x)


def pack_edges(y_ref, row_edge_ref, col_edge_ref, slices):
    width = TILE // GROUPS
    lanes = lane_iota()
    group = lanes // width
    first_tile = lanes % width < slices
    for b in range(0, TILE, 16):
        for side in range(2):
            halves = []
            for half in range(2):
                span = slice(b + half * 8, b + half * 8 + 8)
                packed = None
                for i in range(TV_STEPS):
                    row = i if side == 0 else GROUP_ROWS - TV_STEPS + i
                    home = 0 if side == 0 else GROUPS - 1
                    value = pltpu.roll(y_ref[row, span, :], (width * (i - home)) % TILE, 1)
                    packed = value if packed is None else jnp.where(group == i, value, packed)
                halves.append(packed)
            row_edge_ref[side, b : b + 16, :] = jnp.concatenate(halves, axis=0).astype(jnp.bfloat16)
    half_rows = GROUP_ROWS // 2
    for j in range(0, half_rows, 2):
        for side in range(2):
            span = slice(0, 8) if side == 0 else slice(TILE - 8, TILE)
            parts = []
            for k in (j, j + 1):
                near, far = y_ref[k, span, :], y_ref[k + half_rows, span, :]
                if side == 0:
                    far = pltpu.roll(far, slices, 1)
                else:
                    near = pltpu.roll(near, TILE - slices, 1)
                parts.append(jnp.where(first_tile, near, far))
            col_edge_ref[side, j // 2] = jnp.concatenate(parts, axis=0).astype(jnp.bfloat16)


def edges_kernel(row_edge, col_edge, row_out, col_out, corner_out, row_halo, col_halo, corner, sems):
    row_count = lax.axis_size("row")
    col_count = lax.axis_size("col")
    row = lax.axis_index("row")
    col = lax.axis_index("col")
    low, high = pl.ds(0, 16), pl.ds(TILE - 16, 16)
    routes = (
        (-1, 0, row_edge.at[0], row_halo.at[1]),
        (1, 0, row_edge.at[1], row_halo.at[0]),
        (0, -1, col_edge.at[0], col_halo.at[1]),
        (0, 1, col_edge.at[1], col_halo.at[0]),
        (-1, -1, row_edge.at[0, low], corner.at[1, 1]),
        (-1, 1, row_edge.at[0, high], corner.at[1, 0]),
        (1, -1, row_edge.at[1, low], corner.at[0, 1]),
        (1, 1, row_edge.at[1, high], corner.at[0, 0]),
    )

    def exists(down, right):
        to_row, to_col = row + down, col + right
        return (to_row >= 0) & (to_row < row_count) & (to_col >= 0) & (to_col < col_count)

    row_halo[...] = jnp.zeros(row_halo.shape, row_halo.dtype)
    col_halo[...] = jnp.zeros(col_halo.shape, col_halo.dtype)
    corner[...] = jnp.zeros(corner.shape, corner.dtype)
    barrier = pltpu.get_barrier_semaphore()
    for down, right, src, dst in routes:

        @pl.when(exists(down, right))
        def _(down=down, right=right):
            pl.semaphore_signal(
                barrier, inc=1, device_id=(row + down, col + right), device_id_type=MESH
            )

    rows_near = jnp.where(row > 0, 1, 0) + jnp.where(row < row_count - 1, 1, 0)
    cols_near = jnp.where(col > 0, 1, 0) + jnp.where(col < col_count - 1, 1, 0)
    pl.semaphore_wait(barrier, (rows_near + 1) * (cols_near + 1) - 1)

    copies = []
    for k, (down, right, src, dst) in enumerate(routes):
        copy = pltpu.make_async_remote_copy(
            src_ref=src,
            dst_ref=dst,
            send_sem=sems.at[0, k],
            recv_sem=sems.at[1, k],
            device_id=(row + down, col + right),
            device_id_type=MESH,
        )
        copies.append((down, right, copy))
        pl.when(exists(down, right))(copy.start)
    for down, right, copy in copies:
        pl.when(exists(-down, -right))(copy.wait_recv)
    row_out[...] = row_halo[...]
    col_out[...] = col_halo[...]
    corner_out[...] = corner[...]
    for down, right, copy in copies:
        pl.when(exists(down, right))(copy.wait_send)


def exchange_edges(row_edge, col_edge):
    corner = jax.ShapeDtypeStruct((2, 2, 16, TILE), row_edge.dtype)
    shapes = [jax.ShapeDtypeStruct(e.shape, e.dtype) for e in (row_edge, col_edge)] + [corner]
    return pl.pallas_call(
        edges_kernel,
        out_shape=shapes,
        in_specs=[VMEM] * 2,
        out_specs=[VMEM] * 3,
        scratch_shapes=[pltpu.VMEM(s.shape, s.dtype) for s in shapes]
        + [pltpu.SemaphoreType.DMA((2, 8))],
        compiler_params=pltpu.CompilerParams(collective_id=1, has_side_effects=True),
        name="exchange_edges",
    )(row_edge, col_edge)


EXTRA = 8
SPAN = TILE + 2 * EXTRA
ROWS = GROUP_ROWS + 2 * TV_STEPS


def smooth_kernel(near_ref, y_ref, row_halo, col_halo, corner, out_ref, p_ref, z_ref, sems, *, slices, across):
    width = TILE // GROUPS
    lanes = lane_iota()
    group = lanes // width
    first_tile = lanes % width < slices
    inner = slice(EXTRA, EXTRA + TILE)
    half_rows = GROUP_ROWS // 2

    def shift(value, by):
        by = by % TILE
        return pltpu.roll(value, by, 1) if by else value

    def fill(ur, carry):
        p_ref[TV_STEPS + ur, inner, :] = y_ref[ur]
        return carry

    lax.fori_loop(0, GROUP_ROWS, fill, jnp.int32(0), unroll=2)

    for i in range(TV_STEPS):
        for b in range(0, TILE, 16):
            above = row_halo[0, b : b + 16, :].astype(jnp.float32)
            below = row_halo[1, b : b + 16, :].astype(jnp.float32)
            for half in range(2):
                at = slice(b + half * 8, b + half * 8 + 8)
                to = slice(EXTRA + b + half * 8, EXTRA + b + half * 8 + 8)
                piece = slice(half * 8, half * 8 + 8)
                p_ref[i, to, :] = jnp.where(
                    group == 0,
                    shift(above[piece], -width * i),
                    shift(y_ref[GROUP_ROWS - TV_STEPS + i, at, :], width),
                )
                p_ref[TV_STEPS + GROUP_ROWS + i, to, :] = jnp.where(
                    group == GROUPS - 1,
                    shift(below[piece], width * (GROUPS - 1 - i)),
                    shift(y_ref[i, at, :], -width),
                )

    left, right = [], []
    for j in range(half_rows):
        piece = slice((j % 2) * 8, (j % 2) * 8 + 8)
        left.append(col_halo[0, j // 2].astype(jnp.float32)[piece])
        right.append(col_halo[1, j // 2].astype(jnp.float32)[piece])

    def from_left(ur):
        return left[ur] if ur < half_rows else shift(left[ur - half_rows], -slices)

    def from_right(ur):
        return shift(right[ur], slices) if ur < half_rows else right[ur - half_rows]

    def corner_of(down, side):
        value = corner[down, side].astype(jnp.float32)
        return value[8:16] if side == 0 else value[0:8]

    for r in range(ROWS):
        ur = r - TV_STEPS
        if ur < 0:
            outer = [from_left(GROUP_ROWS + ur), from_right(GROUP_ROWS + ur)]
            edge = [
                shift(corner_of(0, 0), -width * r - slices),
                shift(corner_of(0, 1), -width * r + slices),
            ]
            outer = [jnp.where(group == 0, e, shift(o, width)) for e, o in zip(edge, outer)]
        elif ur >= GROUP_ROWS:
            i = ur - GROUP_ROWS
            outer = [from_left(i), from_right(i)]
            edge = [
                shift(corner_of(1, 0), width * (GROUPS - 1 - i) - slices),
                shift(corner_of(1, 1), width * (GROUPS - 1 - i) + slices),
            ]
            outer = [jnp.where(group == GROUPS - 1, e, shift(o, -width)) for e, o in zip(edge, outer)]
        else:
            outer = [from_left(ur), from_right(ur)]
        p_ref[r, 0:EXTRA, :] = jnp.where(
            first_tile, outer[0], shift(p_ref[r, TILE : TILE + EXTRA, :], slices)
        )
        p_ref[r, EXTRA + TILE :, :] = jnp.where(
            first_tile, shift(p_ref[r, EXTRA : 2 * EXTRA, :], -slices), outer[1]
        )

    one, nought = jnp.ones((8, TILE), jnp.float32), jnp.zeros((8, TILE), jnp.float32)

    def there(flag, outside):
        return jnp.where(outside, jnp.where(near_ref[flag] > 0, one, nought), one)

    keep_above = there(0, group == 0)[0:1]
    keep_below = there(1, group == GROUPS - 1)[0:1]
    keep_left = there(2, first_tile)
    keep_right = there(3, jnp.logical_not(first_tile))

    def flows(here, after):
        down = after - here
        across_ = pltpu.roll(here, SPAN - 1, 0) - here
        scale = lax.rsqrt(smoothing * smoothing + down * down + across_ * across_) * descent_step
        return down * scale, across_ * scale

    for step in range(TV_STEPS):
        low, high = step + 1, ROWS - 1 - step
        above_flow = flows(p_ref[step], p_ref[step + 1])[0]

        def one_row(r, above_flow, place):
            here = p_ref[r]
            flow_down, flow_right = flows(here, p_ref[r + 1])
            change = above_flow - flow_down + pltpu.roll(flow_right, 1, 0) - flow_right
            value = here - change
            if place == "out":
                turned = value[inner].T
                for g in range(GROUPS):
                    for t in range(across):
                        for s in range(0, slices, 8):
                            at = (g * across + t) * slices + s
                            start = s * TILE + g * GROUP_ROWS + r - TV_STEPS
                            z_ref[t, pl.ds(start, 8, stride=TILE), :] = turned[at : at + 8]
                return flow_down
            if place == "above":
                value = value * keep_above
            if place == "below":
                value = value * keep_below
            p_ref[r, inner, :] = value[inner]
            p_ref[r, 0:EXTRA, :] = value[0:EXTRA] * keep_left
            p_ref[r, EXTRA + TILE :, :] = value[EXTRA + TILE :] * keep_right
            return flow_down

        if step == TV_STEPS - 1:
            lax.fori_loop(low, high, lambda r, f: one_row(r, f, "out"), above_flow)
        else:
            for r in range(low, TV_STEPS):
                above_flow = one_row(r, above_flow, "above")
            above_flow = lax.fori_loop(
                TV_STEPS, TV_STEPS + GROUP_ROWS, lambda r, f: one_row(r, f, ""), above_flow
            )
            for r in range(TV_STEPS + GROUP_ROWS, high):
                above_flow = one_row(r, above_flow, "below")

    copies = [
        pltpu.make_async_copy(
            z_ref.at[t], out_ref.at[:, pl.ds(t * TILE, TILE)], sems.at[t]
        )
        for t in range(across)
    ]
    for copy in copies:
        copy.start()
    for copy in copies:
        copy.wait()


def smooth(y, row_halo, col_halo, corner, near, slices, across):
    shape = (slices * TILE, across * TILE)
    kernel = lambda *refs: smooth_kernel(*refs, slices=slices, across=across)
    return pl.pallas_call(
        kernel,
        out_shape=jax.ShapeDtypeStruct(shape, jnp.float32),
        in_specs=[SMEM] + [VMEM] * 4,
        out_specs=ANY,
        scratch_shapes=[
            pltpu.VMEM((ROWS, SPAN, TILE), jnp.float32),
            pltpu.VMEM((across, slices * TILE, TILE), jnp.float32),
            pltpu.SemaphoreType.DMA((across,)),
        ],
        compiler_params=pltpu.CompilerParams(vmem_limit_bytes=48 << 20),
        name="smooth",
    )(near, y, row_halo, col_halo, corner).reshape(slices, TILE, across * TILE)


def local(current_image, measured, ray_weight, angle_ids, shadow_start):
    row = lax.axis_index("row")
    col = lax.axis_index("col")
    rows = lax.axis_size("row")
    cols = lax.axis_size("col")
    slices = current_image.shape[0]
    across = current_image.shape[2] // TILE
    slopes, first, offset = geometry(angle_ids)
    own = lax.dynamic_slice(shadow_start, (row, col * across, 0), (1, across, ANGLES))[0]
    shift = (own % TILE).T
    sent, x = project(current_image, first, offset, slopes, shift)
    shadows = exchange(sent, measured, ray_weight, shadow_start, slices)
    y, row_edge, col_edge = back_project(shadows, x, first, offset, slopes, shift, slices)
    halos = exchange_edges(row_edge, col_edge)
    near = jnp.stack([row > 0, row < rows - 1, col > 0, col < cols - 1]).astype(jnp.int32)
    return smooth(y, *halos, near, slices, across)


def solution(mesh):
    return jax.shard_map(
        local,
        mesh=mesh,
        in_specs=(
            P(None, "row", "col"),
            P("col", "row", None, None),
            P("col", "row", None),
            P(),
            P(),
        ),
        out_specs=P(None, "row", "col"),
        check_vma=False,
    )
```

```python
import math

import jax
import jax.numpy as jnp
import numpy as np
from jax import lax
from jax.experimental import pallas as pl
from jax.experimental.pallas import tpu as pltpu
from jax.sharding import PartitionSpec as P

TILE = 128
ANGLES = 16
ALL_ANGLES = 256
TV_STEPS = 4
PACK = TILE // TV_STEPS

HIGH = 8
WIDE = 16
BINS = 16
MARGIN = 8
DEPTH = MARGIN + TILE + BINS
GROUPS = 4
GROUP_ROWS = TILE // GROUPS
DOWN = GROUP_ROWS // HIGH
RIGHT = TILE // WIDE
QUAD = 4

inverse_root = 0.7071067811865476
proj_scale = 0.03125
relaxation = 8.0
smoothing = 0.25
descent_step = 0.05

MESH = pl.DeviceIdType.MESH
SMEM = pl.BlockSpec(memory_space=pltpu.SMEM)
VMEM = pl.BlockSpec(memory_space=pltpu.VMEM)
HBM = pl.BlockSpec(memory_space=pltpu.HBM)


def lookup(table, index):
    return jnp.take_along_axis(table, index, axis=1, mode="promise_in_bounds")


def lane_iota():
    return lax.broadcasted_iota(jnp.int32, (8, TILE), 1)


def row_iota():
    return lax.broadcasted_iota(jnp.int32, (8, TILE), 0)


def geometry(angle_ids):
    radians = angle_ids.astype(jnp.float32) * (math.pi / ALL_ANGLES)
    down = jnp.cos(radians) * inverse_root
    right = jnp.sin(radians) * inverse_root
    centre = (TILE - 1) / 2.0
    row = jnp.arange(DOWN)[:, None] * HIGH + jnp.arange(GROUPS)[None, :] * GROUP_ROWS
    row = (row.astype(jnp.float32) - centre)[:, None, :, None]
    column = (jnp.arange(RIGHT) * WIDE).astype(jnp.float32)[None, :, None, None] - centre
    place = TILE / 2.0 + row * down + column * right
    lowest = place + jnp.minimum(0.0, (HIGH - 1) * down) + jnp.minimum(0.0, (WIDE - 1) * right)
    first = jnp.floor(lowest - 0.5)
    offset = place - first - 0.5
    shape = (DOWN * RIGHT, GROUPS * ANGLES)
    first = first.astype(jnp.int32) + MARGIN
    return jnp.stack([down, right]), first.reshape(shape), offset.reshape(shape)


def lane_orders(angles_here, slices_here, slices, across):
    rows = slices // slices_here
    to_owner = []
    for sub in range(QUAD // angles_here):
        for r in range(rows):
            for t in range(across):
                for a in range(angles_here):
                    for s in range(slices_here):
                        angle = sub * angles_here + a
                        to_owner.append((angle * across + t) * slices + r * slices_here + s)
    to_owner = np.array(to_owner, np.int32)
    back = np.argsort(to_owner).astype(np.int32)
    return to_owner, back


def row_shifts(shift_ref, quad, to_owner, slices, across, eight):
    rows = row_iota()
    keys = [int(to_owner[eight * 8 + r]) // slices for r in range(8)]
    result = jnp.full((8, TILE), shift_ref[quad * QUAD + keys[0] // across, keys[0] % across], jnp.int32)
    for r in range(1, 8):
        if keys[r] != keys[r - 1]:
            value = shift_ref[quad * QUAD + keys[r] // across, keys[r] % across]
            result = jnp.where(rows >= r, value, result)
    return result


def hat(distance):
    return jnp.maximum(1.0 - jnp.abs(distance), 0.0).astype(jnp.bfloat16)


def to_pixels(z_ref, ur, across, slices):
    parts = []
    for g in range(GROUPS):
        for t in range(across):
            for s in range(0, slices, 8):
                start = s * TILE + g * GROUP_ROWS + ur
                parts.append(z_ref[t, pl.ds(start, 8, stride=TILE), :])
    return jnp.concatenate(parts, axis=0).T


def forward_kernel(
    first_ref, offset_ref, slope_ref, shift_ref, order_ref, x_ref, out_ref,
    z_ref, xb_ref, acc_ref, q_ref, sems,
    *, slices, across, angles_here, slices_here, tile_rows,
):
    copies = [
        pltpu.make_async_copy(
            x_ref.at[:, pl.ds(t * TILE, TILE)], z_ref.at[t], sems.at[t]
        )
        for t in range(across)
    ]
    for copy in copies:
        copy.start()

    pixel = lax.broadcasted_iota(jnp.int32, (BINS, TILE), 1)
    bins = lax.broadcasted_iota(jnp.int32, (BINS, TILE), 0).astype(jnp.float32)
    pixel_row = (pixel // WIDE).astype(jnp.float32)
    pixel_column = (pixel % WIDE).astype(jnp.float32)
    for a in range(ANGLES):
        q_ref[a] = pixel_row * slope_ref[0, a] + pixel_column * slope_ref[1, a] - bins

    def clear(k, carry):
        acc_ref[k] = jnp.zeros((DEPTH, TILE), jnp.float32)
        return carry

    lax.fori_loop(0, GROUPS * ANGLES, clear, jnp.int32(0))
    for copy in copies:
        copy.wait()

    def turn(ur, carry):
        xb_ref[ur] = to_pixels(z_ref, ur, across, slices).astype(jnp.bfloat16)
        return carry

    lax.fori_loop(0, GROUP_ROWS, turn, jnp.int32(0), unroll=2)

    def block(i, carry):
        top = (i // RIGHT) * HIGH
        left = pl.multiple_of((i % RIGHT) * WIDE, WIDE)
        pixels = jnp.concatenate(
            [xb_ref[top + k, pl.ds(left, WIDE), :] for k in range(HIGH)], axis=0
        )
        for g in range(GROUPS):
            weights = jnp.concatenate(
                [hat(q_ref[a] + offset_ref[i, g * ANGLES + a]) for a in range(ANGLES)], axis=0
            )
            shadow = jnp.dot(weights, pixels, preferred_element_type=jnp.float32)
            for a in range(ANGLES):
                span = pl.ds(first_ref[i, g * ANGLES + a], BINS)
                k = g * ANGLES + a
                acc_ref[k, span, :] = acc_ref[k, span, :] + shadow[a * BINS : (a + 1) * BINS]
        return carry

    lax.fori_loop(0, DOWN * RIGHT, block, jnp.int32(0))

    width = TILE // GROUPS
    lanes = lane_iota()
    group = lanes // width
    to_owner, back = lane_orders(angles_here, slices_here, slices, across)
    order = order_ref[...]
    per_owner = across * angles_here * slices_here
    per_tile = angles_here * slices_here
    owners = slices // slices_here
    cols = ANGLES // angles_here
    for quad in range(ANGLES // QUAD):
        pieces = []
        for b in range(TILE // 8):
            span = slice(MARGIN + b * 8, MARGIN + b * 8 + 8)
            total = None
            for k in range(GROUPS):
                part = None
                for g in range(GROUPS):
                    angle = quad * QUAD + (g + k) % GROUPS
                    value = acc_ref[g * ANGLES + angle, span, :]
                    part = value if part is None else jnp.where(group == g, value, part)
                if k:
                    part = pltpu.roll(part, width * k, 1)
                total = part if total is None else total + part
            pieces.append(lookup(total, order))
        rows = jnp.concatenate(pieces, axis=0).T
        sent = []
        for e in range(TILE // 8):
            shift = row_shifts(shift_ref, quad, to_owner, slices, across, e)
            value = lookup(rows[e * 8 : e * 8 + 8], (lanes - shift) & (TILE - 1))
            sent.append(value * proj_scale)
        flat = jnp.concatenate(sent, axis=0)
        for sub in range(QUAD // angles_here):
            col = quad * (QUAD // angles_here) + sub
            for r in range(owners):
                at = (sub * owners + r) * per_owner
                parts = []
                for t in range(across):
                    parts.append(flat[at + t * per_tile : at + (t + 1) * per_tile])
                    if tile_rows > per_tile:
                        parts.append(jnp.zeros((tile_rows - per_tile, TILE), jnp.float32))
                message = jnp.concatenate(parts, axis=0)
                out_ref[r * cols + col] = message.astype(jnp.bfloat16)


def tile_rows_of(angles_here, slices_here):
    return pl.cdiv(angles_here * slices_here, 8) * 8


def project(image, first, offset, slopes, shift):
    row_count = lax.axis_size("row")
    col_count = lax.axis_size("col")
    slices, height, width = image.shape
    across = width // TILE
    angles_here = ANGLES // col_count
    slices_here = slices // row_count
    tile_rows = tile_rows_of(angles_here, slices_here)
    order = np.broadcast_to(lane_orders(angles_here, slices_here, slices, across)[0], (8, TILE))
    kernel = lambda *refs: forward_kernel(
        *refs, slices=slices, across=across, angles_here=angles_here,
        slices_here=slices_here, tile_rows=tile_rows,
    )
    return pl.pallas_call(
        kernel,
        out_shape=jax.ShapeDtypeStruct(
            (row_count * col_count, across * tile_rows, TILE), jnp.bfloat16
        ),
        in_specs=[SMEM] * 4 + [VMEM, HBM],
        out_specs=VMEM,
        scratch_shapes=[
            pltpu.VMEM((across, slices * height, TILE), jnp.float32),
            pltpu.VMEM((GROUP_ROWS, TILE, TILE), jnp.bfloat16),
            pltpu.VMEM((GROUPS * ANGLES, DEPTH, TILE), jnp.float32),
            pltpu.VMEM((ANGLES, BINS, TILE), jnp.float32),
            pltpu.SemaphoreType.DMA((across,)),
        ],
        compiler_params=pltpu.CompilerParams(vmem_limit_bytes=60 << 20),
        name="project",
    )(first, offset, slopes, shift, jnp.asarray(order), image.reshape(slices * height, width))


def ramp_table():
    bins = np.arange(TILE)
    tables = []
    for n in (-1, 0, 1):
        gap = bins[None, :] - bins[:, None] - n * TILE
        nonzero = np.where(gap == 0, 1, gap).astype(np.float64)
        value = np.where(gap % 2 != 0, -1.0 / (math.pi * math.pi * nonzero * nonzero), 0.0)
        value = np.where(gap == 0, 0.25, value)
        tables.append(np.where(np.abs(gap) < TILE, value, 0.0))
    return np.concatenate(tables, axis=0).astype(np.float32)


EXTRA = 8
SPAN = TILE + 2 * EXTRA
ROWS = GROUP_ROWS + 2 * TV_STEPS


def pack_edges(y_ref, row_edge_ref, col_edge_ref, slices):
    width = TILE // GROUPS
    lanes = lane_iota()
    group = lanes // width
    first_tile = lanes % width < slices
    for b in range(0, TILE, 16):
        for side in range(2):
            halves = []
            for half in range(2):
                span = slice(EXTRA + b + half * 8, EXTRA + b + half * 8 + 8)
                packed = None
                for i in range(TV_STEPS):
                    row = i if side == 0 else GROUP_ROWS - TV_STEPS + i
                    home = 0 if side == 0 else GROUPS - 1
                    value = pltpu.roll(y_ref[TV_STEPS + row, span, :], (width * (i - home)) % TILE, 1)
                    packed = value if packed is None else jnp.where(group == i, value, packed)
                halves.append(packed)
            row_edge_ref[side, b : b + 16, :] = jnp.concatenate(halves, axis=0).astype(jnp.bfloat16)
    half_rows = GROUP_ROWS // 2
    for j in range(0, half_rows, 2):
        for side in range(2):
            start = EXTRA if side == 0 else TILE
            span = slice(start, start + 8)
            parts = []
            for k in (j, j + 1):
                near = y_ref[TV_STEPS + k, span, :]
                far = y_ref[TV_STEPS + k + half_rows, span, :]
                if side == 0:
                    far = pltpu.roll(far, slices, 1)
                else:
                    near = pltpu.roll(near, TILE - slices, 1)
                parts.append(jnp.where(first_tile, near, far))
            col_edge_ref[side, j // 2] = jnp.concatenate(parts, axis=0).astype(jnp.bfloat16)


def update_kernel(
    starts_ref, first_ref, shift_ref, sent_ref, measured_ref, ramp_ref, slope_ref, order_ref,
    wide_ref, x_ref, out_ref,
    landed, scan, target_ref, outgoing, returned, store_ref, q_ref, p_ref, z_ref,
    row_edge, col_edge, row_halo, col_halo, corner,
    shadow_sems, scan_sems, window_sems, edge_sems, copy_sems,
    *, slices, angles_here, slices_here, across, tile_rows,
):
    rows = lax.axis_size("row")
    cols = lax.axis_size("col")
    row = lax.axis_index("row")
    col = lax.axis_index("col")
    count = rows * cols
    me = row * cols + col

    def send(src, dst, sems, k, to):
        return pltpu.make_async_remote_copy(
            src_ref=src, dst_ref=dst, send_sem=sems.at[0, k], recv_sem=sems.at[1, k],
            device_id=(to // cols, to % cols), device_id_type=MESH,
        )

    width = TILE // GROUPS
    lanes = lane_iota()
    group = lanes // width
    first_tile = lanes % width < slices
    to_owner, back = lane_orders(angles_here, slices_here, slices, across)
    order = order_ref[...]
    per_owner = across * angles_here * slices_here
    per_tile = angles_here * slices_here
    owners = slices // slices_here
    low, high = pl.ds(0, 16), pl.ds(TILE - 16, 16)
    routes = (
        (-1, 0, row_edge.at[0], row_halo.at[1]),
        (1, 0, row_edge.at[1], row_halo.at[0]),
        (0, -1, col_edge.at[0], col_halo.at[1]),
        (0, 1, col_edge.at[1], col_halo.at[0]),
        (-1, -1, row_edge.at[0, low], corner.at[1, 1]),
        (-1, 1, row_edge.at[0, high], corner.at[1, 0]),
        (1, -1, row_edge.at[1, low], corner.at[0, 1]),
        (1, 1, row_edge.at[1, high], corner.at[0, 0]),
    )

    def exists(down, right):
        to_row, to_col = row + down, col + right
        return (to_row >= 0) & (to_row < rows) & (to_col >= 0) & (to_col < cols)

    reads = [
        pltpu.make_async_copy(
            x_ref.at[:, pl.ds(t * TILE, TILE)], z_ref.at[t], copy_sems.at[t]
        )
        for t in range(across)
    ]
    for copy in reads:
        copy.start()
    row_halo[...] = jnp.zeros(row_halo.shape, row_halo.dtype)
    col_halo[...] = jnp.zeros(col_halo.shape, col_halo.dtype)
    corner[...] = jnp.zeros(corner.shape, corner.dtype)
    barrier = pltpu.get_barrier_semaphore()

    def greet(k, carry):
        to = lax.rem(me + k, count)
        pl.semaphore_signal(barrier, inc=1, device_id=(to // cols, to % cols), device_id_type=MESH)
        return carry

    lax.fori_loop(1, count, greet, jnp.int32(0))

    sublanes = row_iota()

    def aim(k, carry):
        peer = lax.rem(me + k, count)
        down, right = peer // cols, peer % cols
        for t in range(across):
            start = jnp.zeros((8, TILE), jnp.int32)
            for a in range(angles_here):
                value = starts_ref[down, (right * across + t) * ANGLES + col * angles_here + a]
                start = jnp.where(sublanes >= a * slices_here, value, start)
            block = (start >> 7) + jnp.where(lanes < (start & (TILE - 1)), 1, 0)
            target_ref[k, t] = block
        return carry

    lax.fori_loop(0, count, aim, jnp.int32(0), unroll=2)
    pl.semaphore_wait(barrier, count - 1)

    def shadow_copy(k):
        to = lax.rem(me + k, count)
        return send(sent_ref.at[to], landed.at[k], shadow_sems, k, to)

    def scan_copy(k):
        down = lax.rem(row + k, rows)
        return send(measured_ref.at[down], scan.at[k], scan_sems, k, down * cols + col)

    def start(copy):
        def body(k, carry):
            copy(k).start()
            return carry

        return body

    lax.fori_loop(1, count, start(shadow_copy), jnp.int32(0))
    lax.fori_loop(1, rows, start(scan_copy), jnp.int32(0))
    landed[0] = sent_ref[me]
    scan[0] = measured_ref[row]

    for k in range(GROUPS * ANGLES):
        store_ref[k, 0:MARGIN, :] = jnp.zeros((MARGIN, TILE), jnp.float32)
        store_ref[k, MARGIN + TILE :, :] = jnp.zeros((DEPTH - MARGIN - TILE, TILE), jnp.float32)
    pixel = lax.broadcasted_iota(jnp.int32, (TILE, 1), 0)
    pixel_row = (pixel // WIDE).astype(jnp.float32)
    pixel_column = (pixel % WIDE).astype(jnp.float32)
    full = ANGLES * BINS
    bins = (lax.broadcasted_iota(jnp.int32, (1, full), 1) % BINS).astype(jnp.float32)
    q_ref[...] = pixel_row * slope_ref[0:1, :] + pixel_column * slope_ref[1:2, :] - bins

    for copy in reads:
        copy.wait()

    def turn(ur, carry):
        p_ref[TV_STEPS + ur, EXTRA : EXTRA + TILE, :] = to_pixels(z_ref, ur, across, slices)
        return carry

    lax.fori_loop(0, GROUP_ROWS, turn, jnp.int32(0), unroll=2)

    def add(k, sums):
        other = lax.rem(count - k, count)
        message = landed[k].astype(jnp.float32)
        for t in range(across):
            value = message[t * tile_rows : (t + 1) * tile_rows]
            target = target_ref[other, t]
            sums = tuple(
                total + jnp.where(target == b, value, 0.0) for b, total in enumerate(sums)
            )
        return sums

    zero = jnp.zeros((tile_rows, TILE), jnp.float32)
    sums = add(0, (zero,) * rows)

    def add_next(k, sums):
        shadow_copy(k).wait_recv()
        return add(k, sums)

    sums = lax.fori_loop(1, count, add_next, sums)

    def wait_scan(k, carry):
        scan_copy(k).wait_recv()
        return carry

    lax.fori_loop(1, rows, wait_scan, jnp.int32(0))
    residual = []
    for b in range(rows):
        here = scan[lax.rem(row - b + rows, rows)]
        residual.append(here[tile_rows:] * (here[:tile_rows] - sums[b]))
    stacked = jnp.concatenate(
        [
            jnp.concatenate([zero] + residual[:-1], axis=0),
            jnp.concatenate(residual, axis=0),
            jnp.concatenate(residual[1:] + [zero], axis=0),
        ],
        axis=1,
    )
    filtered = jnp.dot(
        stacked, ramp_ref[...], precision=lax.Precision.HIGHEST,
        preferred_element_type=jnp.float32,
    )
    blocks = tuple(filtered[b * tile_rows : (b + 1) * tile_rows] for b in range(rows))

    def window(k):
        parts = []
        for t in range(across):
            target = target_ref[k, t]
            value = zero
            for b in range(rows):
                value = jnp.where(target == b, blocks[b], value)
            parts.append(value)
        return jnp.concatenate(parts, axis=0).astype(jnp.bfloat16)

    def window_copy(k):
        to = lax.rem(me + k, count)
        return send(outgoing.at[k], returned.at[me], window_sems, k, to)

    def reply(k, carry):
        outgoing[k] = window(k)
        window_copy(k).start()
        return carry

    lax.fori_loop(1, count, reply, jnp.int32(0))
    returned[me] = window(0)

    def finish(k, carry):
        window_copy(k).wait_recv()
        return carry

    lax.fori_loop(1, count, finish, jnp.int32(0))

    for quad in range(ANGLES // QUAD):
        parts = []
        for sub in range(QUAD // angles_here):
            at = quad * (QUAD // angles_here) + sub
            for r in range(owners):
                message = returned[r * cols + at].astype(jnp.float32)
                for t in range(across):
                    parts.append(message[t * tile_rows : t * tile_rows + per_tile])
        flat = jnp.concatenate(parts, axis=0)
        turned = []
        for e in range(TILE // 8):
            shift = row_shifts(shift_ref, quad, to_owner, slices, across, e)
            turned.append(lookup(flat[e * 8 : e * 8 + 8], (lanes + shift) & (TILE - 1)))
        bins_first = jnp.concatenate(turned, axis=0).T
        for b in range(TILE // 8):
            span = slice(MARGIN + b * 8, MARGIN + b * 8 + 8)
            value = lookup(bins_first[b * 8 : b * 8 + 8], order)
            for k in range(GROUPS):
                moved = pltpu.roll(value, width * k, 1) if k else value
                for a in range(QUAD):
                    g = (a + k) % GROUPS
                    store_ref[g * ANGLES + quad * QUAD + a, span, :] = jnp.where(
                        group == g, moved, 0.0
                    )

    def block(urb, vb):
        i = urb * RIGHT + vb
        top = urb * HIGH + TV_STEPS
        left = pl.multiple_of(vb * WIDE, WIDE) + EXTRA
        total = None
        for g in range(GROUPS):
            shadows = jnp.concatenate(
                [
                    store_ref[g * ANGLES + a, pl.ds(first_ref[i, g * ANGLES + a], BINS), :]
                    for a in range(ANGLES)
                ],
                axis=0,
            ).astype(jnp.bfloat16)
            weights = hat(q_ref[...] + wide_ref[pl.ds(i * GROUPS + g, 1), :])
            part = jnp.dot(weights, shadows, preferred_element_type=jnp.float32)
            total = part if total is None else total + part
        total = total * (relaxation * proj_scale)
        for k in range(HIGH):
            p_ref[top + k, pl.ds(left, WIDE), :] = (
                p_ref[top + k, pl.ds(left, WIDE), :] + total[k * WIDE : (k + 1) * WIDE]
            )

    def outer_rows(i, carry):
        block((i // RIGHT) * (DOWN - 1), i % RIGHT)
        return carry

    def outer_columns(i, carry):
        block(1 + i // 2, (i % 2) * (RIGHT - 1))
        return carry

    def inner_blocks(i, carry):
        block(1 + i // (RIGHT - 2), 1 + i % (RIGHT - 2))
        return carry

    lax.fori_loop(0, 2 * RIGHT, outer_rows, jnp.int32(0))
    lax.fori_loop(0, 2 * (DOWN - 2), outer_columns, jnp.int32(0))
    pack_edges(p_ref, row_edge, col_edge, slices)

    copies = []
    for k, (down, right, src, dst) in enumerate(routes):
        copy = pltpu.make_async_remote_copy(
            src_ref=src,
            dst_ref=dst,
            send_sem=edge_sems.at[0, k],
            recv_sem=edge_sems.at[1, k],
            device_id=(row + down, col + right),
            device_id_type=MESH,
        )
        copies.append((down, right, copy))
        pl.when(exists(down, right))(copy.start)
    lax.fori_loop(0, (DOWN - 2) * (RIGHT - 2), inner_blocks, jnp.int32(0))
    for down, right, copy in copies:
        pl.when(exists(-down, -right))(copy.wait_recv)

    inner = slice(EXTRA, EXTRA + TILE)
    half_rows = GROUP_ROWS // 2

    def shift(value, by):
        by = by % TILE
        return pltpu.roll(value, by, 1) if by else value

    for i in range(TV_STEPS):
        for b in range(0, TILE, 16):
            above = row_halo[0, b : b + 16, :].astype(jnp.float32)
            below = row_halo[1, b : b + 16, :].astype(jnp.float32)
            for half in range(2):
                to = slice(EXTRA + b + half * 8, EXTRA + b + half * 8 + 8)
                piece = slice(half * 8, half * 8 + 8)
                p_ref[i, to, :] = jnp.where(
                    group == 0,
                    shift(above[piece], -width * i),
                    shift(p_ref[GROUP_ROWS + i, to, :], width),
                )
                p_ref[TV_STEPS + GROUP_ROWS + i, to, :] = jnp.where(
                    group == GROUPS - 1,
                    shift(below[piece], width * (GROUPS - 1 - i)),
                    shift(p_ref[TV_STEPS + i, to, :], -width),
                )

    left, right = [], []
    for j in range(half_rows):
        piece = slice((j % 2) * 8, (j % 2) * 8 + 8)
        left.append(col_halo[0, j // 2].astype(jnp.float32)[piece])
        right.append(col_halo[1, j // 2].astype(jnp.float32)[piece])

    def from_left(ur):
        return left[ur] if ur < half_rows else shift(left[ur - half_rows], -slices)

    def from_right(ur):
        return shift(right[ur], slices) if ur < half_rows else right[ur - half_rows]

    def corner_of(down, side):
        value = corner[down, side].astype(jnp.float32)
        return value[8:16] if side == 0 else value[0:8]

    for r in range(ROWS):
        ur = r - TV_STEPS
        if ur < 0:
            outer = [from_left(GROUP_ROWS + ur), from_right(GROUP_ROWS + ur)]
            edge = [
                shift(corner_of(0, 0), -width * r - slices),
                shift(corner_of(0, 1), -width * r + slices),
            ]
            outer = [jnp.where(group == 0, e, shift(o, width)) for e, o in zip(edge, outer)]
        elif ur >= GROUP_ROWS:
            i = ur - GROUP_ROWS
            outer = [from_left(i), from_right(i)]
            edge = [
                shift(corner_of(1, 0), width * (GROUPS - 1 - i) - slices),
                shift(corner_of(1, 1), width * (GROUPS - 1 - i) + slices),
            ]
            outer = [jnp.where(group == GROUPS - 1, e, shift(o, -width)) for e, o in zip(edge, outer)]
        else:
            outer = [from_left(ur), from_right(ur)]
        p_ref[r, 0:EXTRA, :] = jnp.where(
            first_tile, outer[0], shift(p_ref[r, TILE : TILE + EXTRA, :], slices)
        )
        p_ref[r, EXTRA + TILE :, :] = jnp.where(
            first_tile, shift(p_ref[r, EXTRA : 2 * EXTRA, :], -slices), outer[1]
        )

    one, nought = jnp.ones((8, TILE), jnp.float32), jnp.zeros((8, TILE), jnp.float32)

    def there(near, outside):
        return jnp.where(outside, jnp.where(near, one, nought), one)

    keep_above = there(row > 0, group == 0)[0:1]
    keep_below = there(row < rows - 1, group == GROUPS - 1)[0:1]
    keep_left = there(col > 0, first_tile)
    keep_right = there(col < cols - 1, jnp.logical_not(first_tile))

    def flows(here, after):
        down = after - here
        across_ = pltpu.roll(here, SPAN - 1, 0) - here
        scale = lax.rsqrt(smoothing * smoothing + down * down + across_ * across_) * descent_step
        return down * scale, across_ * scale

    for step in range(TV_STEPS):
        low, high = step + 1, ROWS - 1 - step
        above_flow = flows(p_ref[step], p_ref[step + 1])[0]

        def one_row(r, above_flow, place):
            here = p_ref[r]
            flow_down, flow_right = flows(here, p_ref[r + 1])
            change = above_flow - flow_down + pltpu.roll(flow_right, 1, 0) - flow_right
            value = here - change
            if place == "out":
                turned = value[inner].T
                for g in range(GROUPS):
                    for t in range(across):
                        for s in range(0, slices, 8):
                            at = (g * across + t) * slices + s
                            start = s * TILE + g * GROUP_ROWS + r - TV_STEPS
                            z_ref[t, pl.ds(start, 8, stride=TILE), :] = turned[at : at + 8]
                return flow_down
            if place == "above":
                value = value * keep_above
            if place == "below":
                value = value * keep_below
            p_ref[r, inner, :] = value[inner]
            p_ref[r, 0:EXTRA, :] = value[0:EXTRA] * keep_left
            p_ref[r, EXTRA + TILE :, :] = value[EXTRA + TILE :] * keep_right
            return flow_down

        if step == TV_STEPS - 1:
            lax.fori_loop(low, high, lambda r, f: one_row(r, f, "out"), above_flow)
        else:
            for r in range(low, TV_STEPS):
                above_flow = one_row(r, above_flow, "above")
            above_flow = lax.fori_loop(
                TV_STEPS, TV_STEPS + GROUP_ROWS, lambda r, f: one_row(r, f, ""), above_flow
            )
            for r in range(TV_STEPS + GROUP_ROWS, high):
                above_flow = one_row(r, above_flow, "below")

    writes = [
        pltpu.make_async_copy(
            z_ref.at[t], out_ref.at[:, pl.ds(t * TILE, TILE)], copy_sems.at[t]
        )
        for t in range(across)
    ]
    for copy in writes:
        copy.start()
    for down, right, copy in copies:
        pl.when(exists(down, right))(copy.wait_send)
    def settle(k, carry):
        shadow_copy(k).wait_send()
        window_copy(k).wait_send()
        return carry

    lax.fori_loop(1, count, settle, jnp.int32(0))

    def settle_scan(k, carry):
        scan_copy(k).wait_send()
        return carry

    lax.fori_loop(1, rows, settle_scan, jnp.int32(0))
    for copy in writes:
        copy.wait()


def update(image, sent, measured, ray_weight, shadow_start, first, offset, slopes, shift):
    rows = lax.axis_size("row")
    cols = lax.axis_size("col")
    slices, height, width = image.shape
    angles_here = ANGLES // cols
    slices_here = slices // rows
    tile_rows = tile_rows_of(angles_here, slices_here)
    count, depth, unused = sent.shape
    across = depth // tile_rows
    per_tile = angles_here * slices_here
    natural = measured.reshape(angles_here, rows, slices_here, TILE).transpose(1, 0, 2, 3)
    weight = jnp.broadcast_to(ray_weight.reshape(1, angles_here, 1, TILE), natural.shape)
    scan = jnp.stack([natural, weight], axis=1).reshape(rows, 2, per_tile, TILE)
    scan = jnp.pad(scan, ((0, 0), (0, 0), (0, tile_rows - per_tile), (0, 0)))
    scan = scan.reshape(rows, 2 * tile_rows, TILE)
    order = np.broadcast_to(lane_orders(angles_here, slices_here, slices, across)[1], (8, TILE))
    wide = jnp.repeat(offset.reshape(DOWN * RIGHT * GROUPS, ANGLES), BINS, axis=1)
    kernel = lambda *refs: update_kernel(
        *refs, slices=slices, angles_here=angles_here, slices_here=slices_here,
        across=across, tile_rows=tile_rows,
    )
    dma = pltpu.SemaphoreType.DMA
    row_edge = pltpu.VMEM((2, TILE, TILE), jnp.bfloat16)
    col_edge = pltpu.VMEM((2, GROUP_ROWS // 4, 16, TILE), jnp.bfloat16)
    return pl.pallas_call(
        kernel,
        out_shape=jax.ShapeDtypeStruct((slices * height, width), jnp.float32),
        in_specs=[SMEM] * 3 + [VMEM] * 6 + [HBM],
        out_specs=HBM,
        scratch_shapes=[
            pltpu.VMEM(sent.shape, jnp.bfloat16),
            pltpu.VMEM(scan.shape, jnp.float32),
            pltpu.VMEM((count, across, tile_rows, TILE), jnp.int32),
            pltpu.VMEM(sent.shape, jnp.bfloat16),
            pltpu.VMEM(sent.shape, jnp.bfloat16),
            pltpu.VMEM((GROUPS * ANGLES, DEPTH, TILE), jnp.float32),
            pltpu.VMEM((TILE, ANGLES * BINS), jnp.float32),
            pltpu.VMEM((ROWS, SPAN, TILE), jnp.float32),
            pltpu.VMEM((across, slices * height, TILE), jnp.float32),
            row_edge, col_edge, row_edge, col_edge,
            pltpu.VMEM((2, 2, 16, TILE), jnp.bfloat16),
            dma((2, count)),
            dma((2, rows)),
            dma((2, count)),
            dma((2, 8)),
            dma((across,)),
        ],
        compiler_params=pltpu.CompilerParams(
            collective_id=0, has_side_effects=True, vmem_limit_bytes=60 << 20
        ),
        name="update",
    )(
        shadow_start.reshape(rows, -1), first, shift, sent, scan, jnp.asarray(ramp_table()),
        jnp.repeat(slopes, BINS, axis=1), jnp.asarray(order), wide,
        image.reshape(slices * height, width),
    ).reshape(image.shape)


def local(current_image, measured, ray_weight, angle_ids, shadow_start):
    row = lax.axis_index("row")
    col = lax.axis_index("col")
    across = current_image.shape[2] // TILE
    slopes, first, offset = geometry(angle_ids)
    own = lax.dynamic_slice(shadow_start, (row, col * across, 0), (1, across, ANGLES))[0]
    shift = (own % TILE).T
    sent = project(current_image, first, offset, slopes, shift)
    return update(
        current_image, sent, measured, ray_weight, shadow_start, first, offset, slopes, shift
    )


def solution(mesh):
    return jax.shard_map(
        local,
        mesh=mesh,
        in_specs=(
            P(None, "row", "col"),
            P("col", "row", None, None),
            P("col", "row", None),
            P(),
            P(),
        ),
        out_specs=P(None, "row", "col"),
        check_vma=False,
    )
```

```python
import math

import jax
import jax.numpy as jnp
from jax import lax
from jax.experimental import pallas as pl
from jax.experimental.pallas import tpu as pltpu
from jax.sharding import PartitionSpec as P

TILE = 128
ANGLES = 16
ALL_ANGLES = 256
TV_STEPS = 4
PACK = TILE // TV_STEPS

HIGH = 8
WIDE = 16
BINS = 16
MARGIN = 8
DEPTH = MARGIN + TILE + BINS
GROUPS = 4
GROUP_ROWS = TILE // GROUPS
DOWN = GROUP_ROWS // HIGH
RIGHT = TILE // WIDE
QUAD = 4

inverse_root = 0.7071067811865476
proj_scale = 0.03125
relaxation = 8.0
smoothing = 0.25
descent_step = 0.05

MESH = pl.DeviceIdType.MESH
SMEM = pl.BlockSpec(memory_space=pltpu.SMEM)
VMEM = pl.BlockSpec(memory_space=pltpu.VMEM)
HBM = pl.BlockSpec(memory_space=pltpu.HBM)


def lookup(table, index):
    return jnp.take_along_axis(table, index, axis=1, mode="promise_in_bounds")


def lane_iota():
    return lax.broadcasted_iota(jnp.int32, (8, TILE), 1)


def row_iota():
    return lax.broadcasted_iota(jnp.int32, (8, TILE), 0)


BLOCKS = DOWN * RIGHT
PAIR = 2


def geometry(angle_ref):
    lanes = lane_iota()
    ids = jnp.zeros((8, TILE), jnp.int32)
    for a in range(ANGLES):
        ids = jnp.where(lanes % ANGLES == a, angle_ref[a], ids)
    radians = ids.astype(jnp.float32) * (math.pi / ALL_ANGLES)
    down = jnp.cos(radians) * inverse_root
    right = jnp.sin(radians) * inverse_root
    centre = (TILE - 1) / 2.0
    firsts, offsets = [], []
    for b in range(0, BLOCKS, 8):
        block = row_iota() + b
        row = (block // RIGHT) * HIGH + (lanes // ANGLES % GROUPS) * GROUP_ROWS
        column = (block % RIGHT) * WIDE
        row = row.astype(jnp.float32) - centre
        column = column.astype(jnp.float32) - centre
        place = TILE / 2.0 + (row * down + column * right)
        lowest = place + jnp.minimum(0.0, (HIGH - 1) * down) + jnp.minimum(0.0, (WIDE - 1) * right)
        first = jnp.floor(lowest - 0.5)
        firsts.append(first.astype(jnp.int32) + MARGIN)
        offsets.append(place - first - 0.5)
    return down, right, jnp.concatenate(firsts, axis=0), jnp.concatenate(offsets, axis=0)


def pair_source(slices_here, slices, across):
    lanes = lane_iota()
    owners = slices // slices_here
    s = lanes % slices_here
    a = lanes // slices_here % PAIR
    t = lanes // (slices_here * PAIR) % across
    r = lanes // (slices_here * PAIR * across) % owners
    kind = lanes // (slices_here * PAIR * across * owners)
    return ((kind * PAIR + a) * across + t) * slices + r * slices_here + s


def quad_source(angles_here, slices_here, slices, across):
    lanes = lane_iota()
    slice_ = lanes % slices
    t = lanes // slices % across
    angle = lanes // (slices * across)
    sub, a = angle // angles_here, angle % angles_here
    r, s = slice_ // slices_here, slice_ % slices_here
    owner = sub * (slices // slices_here) + r
    return ((owner * across + t) * angles_here + a) * slices_here + s


def select_rows(values):
    rows = row_iota()
    result = jnp.full((8, TILE), values[0][1], jnp.int32)
    for r in range(1, 8):
        if values[r][0] != values[r - 1][0]:
            result = jnp.where(rows >= r, values[r][1], result)
    return result


def hat(distance):
    return jnp.maximum(1.0 - jnp.abs(distance), 0.0).astype(jnp.bfloat16)


def to_pixels(z_ref, ur, across, slices, mirrored=GROUPS):
    parts = []
    mirror = TILE - 1 - lane_iota()
    for g in range(GROUPS):
        row = ur if g < mirrored else GROUP_ROWS - 1 - ur
        for t in range(across):
            for s in range(0, slices, 8):
                start = s * TILE + g * GROUP_ROWS + row
                part = z_ref[t, pl.ds(start, 8, stride=TILE), :]
                parts.append(part if g < mirrored else lookup(part, mirror))
    return jnp.concatenate(parts, axis=0).T


def forward_kernel(
    angle_ref, starts_ref, x_ref, out_ref, first_out, table_out,
    z_ref, xb_ref, acc_ref, q_ref, first_ref, offset_ref, sems,
    *, slices, across, angles_here, slices_here, tile_rows,
):
    row_index = lax.axis_index("row")
    col_index = lax.axis_index("col")
    copies = [
        pltpu.make_async_copy(
            x_ref.at[:, pl.ds(t * TILE, TILE)], z_ref.at[t], sems.at[t]
        )
        for t in range(across)
    ]
    for copy in copies:
        copy.start()

    down, right, first, offset = geometry(angle_ref)
    first_out[...] = first
    table_out[0:BLOCKS] = offset
    table_out[BLOCKS : BLOCKS + 8] = down
    table_out[BLOCKS + 8 :] = right
    scalars = [
        pltpu.make_async_copy(first_out, first_ref, sems.at[across]),
        pltpu.make_async_copy(table_out.at[0:BLOCKS], offset_ref, sems.at[across + 1]),
    ]
    for copy in scalars:
        copy.start()
    pixel = lane_iota()
    pixel_row = (pixel // WIDE).astype(jnp.float32)
    pixel_column = (pixel % WIDE).astype(jnp.float32)
    bins = row_iota().astype(jnp.float32)
    for a in range(ANGLES):
        at = jnp.full((8, TILE), a, jnp.int32)
        place = pixel_row * lookup(down, at) + pixel_column * lookup(right, at)
        for b in range(0, BINS, 8):
            q_ref[a, b : b + 8, :] = place - (bins + b)

    half = GROUPS // 2

    def clear(k, carry):
        acc_ref[k] = jnp.zeros((DEPTH, TILE), jnp.float32)
        return carry

    lax.fori_loop(0, half * ANGLES, clear, jnp.int32(0))
    for copy in copies:
        copy.wait()

    def turn(ur, carry):
        xb_ref[ur] = to_pixels(z_ref, ur, across, slices, half).astype(jnp.bfloat16)
        return carry

    lax.fori_loop(0, GROUP_ROWS, turn, jnp.int32(0), unroll=2)
    for copy in scalars:
        copy.wait()

    def block(i, carry):
        top = (i // RIGHT) * HIGH
        left = pl.multiple_of((i % RIGHT) * WIDE, WIDE)
        pixels = jnp.concatenate(
            [xb_ref[top + k, pl.ds(left, WIDE), :] for k in range(HIGH)], axis=0
        )
        for g in range(half):
            weights = jnp.concatenate(
                [hat(q_ref[a] + offset_ref[i, g * ANGLES + a]) for a in range(ANGLES)], axis=0
            )
            shadow = jnp.dot(weights, pixels, preferred_element_type=jnp.float32)
            spans = [pl.ds(first_ref[i, g * ANGLES + a], BINS) for a in range(ANGLES)]
            olds = [acc_ref[g * ANGLES + a, spans[a], :] for a in range(ANGLES)]
            for a in range(ANGLES):
                acc_ref[g * ANGLES + a, spans[a], :] = (
                    olds[a] + shadow[a * BINS : (a + 1) * BINS]
                )
        return carry

    lax.fori_loop(0, BLOCKS, block, jnp.int32(0))

    width = TILE // GROUPS
    lanes = lane_iota()
    group = lanes // width
    near = pair_source(slices_here, slices, across)
    far = near ^ width
    cols = ANGLES // angles_here
    owners = slices // slices_here
    piece = PAIR * slices_here
    per_tile = angles_here * slices_here
    kind_rows = TILE // 2

    def pick(span, values):
        result = acc_ref[values[0], span, :]
        for g in range(1, GROUPS):
            result = jnp.where(group == g, acc_ref[values[g], span, :], result)
        return result

    def pair_shadows(pair):
        here, there = pair * PAIR, pair * PAIR + 1
        pieces = []
        for b in range(TILE // 8):
            span = slice(MARGIN + b * 8, MARGIN + b * 8 + 8)
            own = pick(span, (here, ANGLES + there, ANGLES + here, there))
            other = pick(span, (there, ANGLES + here, ANGLES + there, here))
            pieces.append(lookup(own, near) + lookup(other, far))
        rows = jnp.concatenate(pieces, axis=0).T
        sent = []
        for e in range(kind_rows // 8):
            keys = []
            for r in range(e * 8, e * 8 + 8):
                a = r // slices_here % PAIR
                t = r // (slices_here * PAIR) % across
                start = starts_ref[row_index, col_index * across + t, pair * PAIR + a]
                keys.append(((a, t), start))
            index = (lanes - select_rows(keys)) & (TILE - 1)
            value = lookup(rows[e * 8 : e * 8 + 8], index) + lookup(
                rows[kind_rows + e * 8 : kind_rows + e * 8 + 8], TILE - 1 - index
            )
            sent.append(value * proj_scale)
        return jnp.concatenate(sent, axis=0)

    for col in range(cols):
        count = angles_here // PAIR
        shadows = [pair_shadows(col * count + p) for p in range(count)]
        for r in range(owners):
            parts = []
            for t in range(across):
                at = (r * across + t) * piece
                parts += [shadow[at : at + piece] for shadow in shadows]
                if tile_rows > per_tile:
                    parts.append(jnp.zeros((tile_rows - per_tile, TILE), jnp.float32))
            message = jnp.concatenate(parts, axis=0)
            out_ref[r * cols + col] = message.astype(jnp.bfloat16)


def tile_rows_of(angles_here, slices_here):
    return pl.cdiv(angles_here * slices_here, 8) * 8


def project(image, angle_ids, shadow_start):
    row_count = lax.axis_size("row")
    col_count = lax.axis_size("col")
    slices, height, width = image.shape
    across = width // TILE
    angles_here = ANGLES // col_count
    slices_here = slices // row_count
    tile_rows = tile_rows_of(angles_here, slices_here)
    kernel = lambda *refs: forward_kernel(
        *refs, slices=slices, across=across, angles_here=angles_here,
        slices_here=slices_here, tile_rows=tile_rows,
    )
    return pl.pallas_call(
        kernel,
        out_shape=[
            jax.ShapeDtypeStruct((row_count * col_count, across * tile_rows, TILE), jnp.bfloat16),
            jax.ShapeDtypeStruct((BLOCKS, TILE), jnp.int32),
            jax.ShapeDtypeStruct((BLOCKS + 16, TILE), jnp.float32),
        ],
        in_specs=[SMEM, SMEM, HBM],
        out_specs=[VMEM] * 3,
        scratch_shapes=[
            pltpu.VMEM((across, slices * height, TILE), jnp.float32),
            pltpu.VMEM((GROUP_ROWS, TILE, TILE), jnp.bfloat16),
            pltpu.VMEM((GROUPS // 2 * ANGLES, DEPTH, TILE), jnp.float32),
            pltpu.VMEM((ANGLES, BINS, TILE), jnp.float32),
            pltpu.SMEM((BLOCKS, TILE), jnp.int32),
            pltpu.SMEM((BLOCKS, TILE), jnp.float32),
            pltpu.SemaphoreType.DMA((across + 2,)),
        ],
        compiler_params=pltpu.CompilerParams(vmem_limit_bytes=60 << 20),
        name="project",
    )(angle_ids, shadow_start, image.reshape(slices * height, width))


def ramp_table(n):
    gap = lax.broadcasted_iota(jnp.int32, (TILE, TILE), 1) - n * TILE
    gap = gap - lax.broadcasted_iota(jnp.int32, (TILE, TILE), 0)
    nonzero = jnp.where(gap == 0, 1, gap).astype(jnp.float32)
    value = -1.0 / (math.pi * math.pi * nonzero * nonzero)
    value = jnp.where((gap & 1) == 1, value, 0.0)
    value = jnp.where(gap == 0, 0.25, value)
    return jnp.where(jnp.abs(gap) < TILE, value, 0.0)


EXTRA = 8
SPAN = TILE + 2 * EXTRA
ROWS = GROUP_ROWS + 2 * TV_STEPS


def pack_edges(y_ref, row_edge_ref, col_edge_ref, slices):
    width = TILE // GROUPS
    lanes = lane_iota()
    group = lanes // width
    first_tile = lanes % width < slices
    for b in range(0, TILE, 16):
        for side in range(2):
            halves = []
            for half in range(2):
                span = slice(EXTRA + b + half * 8, EXTRA + b + half * 8 + 8)
                packed = None
                for i in range(TV_STEPS):
                    row = i if side == 0 else GROUP_ROWS - TV_STEPS + i
                    home = 0 if side == 0 else GROUPS - 1
                    value = pltpu.roll(y_ref[TV_STEPS + row, span, :], (width * (i - home)) % TILE, 1)
                    packed = value if packed is None else jnp.where(group == i, value, packed)
                halves.append(packed)
            row_edge_ref[side, b : b + 16, :] = jnp.concatenate(halves, axis=0).astype(jnp.bfloat16)
    half_rows = GROUP_ROWS // 2
    for j in range(0, half_rows, 2):
        for side in range(2):
            start = EXTRA if side == 0 else TILE
            span = slice(start, start + 8)
            parts = []
            for k in (j, j + 1):
                near = y_ref[TV_STEPS + k, span, :]
                far = y_ref[TV_STEPS + k + half_rows, span, :]
                if side == 0:
                    far = pltpu.roll(far, slices, 1)
                else:
                    near = pltpu.roll(near, TILE - slices, 1)
                parts.append(jnp.where(first_tile, near, far))
            col_edge_ref[side, j // 2] = jnp.concatenate(parts, axis=0).astype(jnp.bfloat16)


def update_kernel(
    starts_ref, first_ref, sent_ref, measured_ref, weight_ref, table_ref, x_ref, out_ref,
    scan_out, wide_ref, ramp_ref, landed, scan, target_ref, outgoing, returned, store_ref, q_ref, p_ref, z_ref,
    row_edge, col_edge, row_halo, col_halo, corner,
    shadow_sems, scan_sems, window_sems, edge_sems, copy_sems,
    *, slices, angles_here, slices_here, across, tile_rows,
):
    rows = lax.axis_size("row")
    cols = lax.axis_size("col")
    row = lax.axis_index("row")
    col = lax.axis_index("col")
    count = rows * cols
    me = row * cols + col

    def send(src, dst, sems, k, to):
        return pltpu.make_async_remote_copy(
            src_ref=src, dst_ref=dst, send_sem=sems.at[0, k], recv_sem=sems.at[1, k],
            device_id=(to // cols, to % cols), device_id_type=MESH,
        )

    width = TILE // GROUPS
    lanes = lane_iota()
    group = lanes // width
    first_tile = lanes % width < slices
    order = quad_source(angles_here, slices_here, slices, across)
    per_tile = angles_here * slices_here
    owners = slices // slices_here
    low, high = pl.ds(0, 16), pl.ds(TILE - 16, 16)
    routes = (
        (-1, 0, row_edge.at[0], row_halo.at[1]),
        (1, 0, row_edge.at[1], row_halo.at[0]),
        (0, -1, col_edge.at[0], col_halo.at[1]),
        (0, 1, col_edge.at[1], col_halo.at[0]),
        (-1, -1, row_edge.at[0, low], corner.at[1, 1]),
        (-1, 1, row_edge.at[0, high], corner.at[1, 0]),
        (1, -1, row_edge.at[1, low], corner.at[0, 1]),
        (1, 1, row_edge.at[1, high], corner.at[0, 0]),
    )

    def exists(down, right):
        to_row, to_col = row + down, col + right
        return (to_row >= 0) & (to_row < rows) & (to_col >= 0) & (to_col < cols)

    reads = [
        pltpu.make_async_copy(
            x_ref.at[:, pl.ds(t * TILE, TILE)], z_ref.at[t], copy_sems.at[t]
        )
        for t in range(across)
    ]
    for copy in reads:
        copy.start()
    for r in range(rows):
        for a in range(angles_here):
            to = a * slices_here
            scan_out[r, to : to + slices_here] = measured_ref[
                a * slices + r * slices_here : a * slices + (r + 1) * slices_here
            ]
            scan_out[r, tile_rows + to : tile_rows + to + slices_here] = jnp.broadcast_to(
                weight_ref[a : a + 1], (slices_here, TILE)
            )
        if tile_rows > per_tile:
            spare = jnp.zeros((tile_rows - per_tile, TILE), jnp.float32)
            scan_out[r, per_tile:tile_rows] = spare
            scan_out[r, tile_rows + per_tile :] = spare
    row_halo[...] = jnp.zeros(row_halo.shape, row_halo.dtype)
    col_halo[...] = jnp.zeros(col_halo.shape, col_halo.dtype)
    corner[...] = jnp.zeros(corner.shape, corner.dtype)
    barrier = pltpu.get_barrier_semaphore()

    def greet(k, carry):
        to = lax.rem(me + k, count)
        pl.semaphore_signal(barrier, inc=1, device_id=(to // cols, to % cols), device_id_type=MESH)
        return carry

    lax.fori_loop(1, count, greet, jnp.int32(0))

    sublanes = row_iota()

    def aim(k, carry):
        peer = lax.rem(me + k, count)
        down, right = peer // cols, peer % cols
        for t in range(across):
            start = jnp.zeros((8, TILE), jnp.int32)
            for a in range(angles_here):
                value = starts_ref[down, right * across + t, col * angles_here + a]
                start = jnp.where(sublanes >= a * slices_here, value, start)
            block = (start >> 7) + jnp.where(lanes < (start & (TILE - 1)), 1, 0)
            target_ref[k, t] = block
        return carry

    lax.fori_loop(0, count, aim, jnp.int32(0), unroll=2)
    pl.semaphore_wait(barrier, count - 1)

    def shadow_copy(k):
        to = lax.rem(me + k, count)
        return send(sent_ref.at[to], landed.at[k], shadow_sems, k, to)

    def scan_copy(k):
        down = lax.rem(row + k, rows)
        return send(scan_out.at[down], scan.at[k], scan_sems, k, down * cols + col)

    def start(copy):
        def body(k, carry):
            copy(k).start()
            return carry

        return body

    lax.fori_loop(1, count, start(shadow_copy), jnp.int32(0))
    lax.fori_loop(1, rows, start(scan_copy), jnp.int32(0))
    landed[0] = sent_ref[me]
    scan[0] = scan_out[row]

    for k in range(GROUPS * ANGLES):
        store_ref[k, 0:MARGIN, :] = jnp.zeros((MARGIN, TILE), jnp.float32)
        store_ref[k, MARGIN + TILE :, :] = jnp.zeros((DEPTH - MARGIN - TILE, TILE), jnp.float32)
    pixel = row_iota()
    bins = (lanes % BINS).astype(jnp.float32)
    down = table_ref[BLOCKS : BLOCKS + 8]
    right = table_ref[BLOCKS + 8 :]
    for h in range(ANGLES * BINS // TILE):
        at = lanes // BINS + h * (TILE // BINS)
        down_here, right_here = lookup(down, at), lookup(right, at)
        span = slice(h * TILE, (h + 1) * TILE)
        for b in range(0, TILE, 8):
            pixel_row = ((pixel + b) // WIDE).astype(jnp.float32)
            pixel_column = ((pixel + b) % WIDE).astype(jnp.float32)
            q_ref[b : b + 8, span] = pixel_row * down_here + pixel_column * right_here - bins
        for g in range(GROUPS):
            for b in range(0, BLOCKS, 8):
                wide_ref[g, b : b + 8, span] = lookup(table_ref[b : b + 8], at + g * ANGLES)
    for n in (-1, 0, 1):
        ramp_ref[(n + 1) * TILE : (n + 2) * TILE] = ramp_table(n)

    for copy in reads:
        copy.wait()

    def turn(ur, carry):
        p_ref[TV_STEPS + ur, EXTRA : EXTRA + TILE, :] = to_pixels(z_ref, ur, across, slices)
        return carry

    lax.fori_loop(0, GROUP_ROWS, turn, jnp.int32(0), unroll=2)

    def add(k, sums):
        other = lax.rem(count - k, count)
        message = landed[k].astype(jnp.float32)
        for t in range(across):
            value = message[t * tile_rows : (t + 1) * tile_rows]
            target = target_ref[other, t]
            sums = tuple(
                total + jnp.where(target == b, value, 0.0) for b, total in enumerate(sums)
            )
        return sums

    zero = jnp.zeros((tile_rows, TILE), jnp.float32)
    sums = add(0, (zero,) * rows)

    def add_next(k, sums):
        shadow_copy(k).wait_recv()
        return add(k, sums)

    sums = lax.fori_loop(1, count, add_next, sums)

    def wait_scan(k, carry):
        scan_copy(k).wait_recv()
        return carry

    lax.fori_loop(1, rows, wait_scan, jnp.int32(0))
    residual = []
    for b in range(rows):
        here = scan[lax.rem(row - b + rows, rows)]
        residual.append(here[tile_rows:] * (here[:tile_rows] - sums[b]))
    stacked = jnp.concatenate(
        [
            jnp.concatenate([zero] + residual[:-1], axis=0),
            jnp.concatenate(residual, axis=0),
            jnp.concatenate(residual[1:] + [zero], axis=0),
        ],
        axis=1,
    )
    filtered = jnp.dot(
        stacked, ramp_ref[...], precision=lax.Precision.HIGHEST,
        preferred_element_type=jnp.float32,
    )
    blocks = tuple(filtered[b * tile_rows : (b + 1) * tile_rows] for b in range(rows))

    def window(k):
        parts = []
        for t in range(across):
            target = target_ref[k, t]
            value = zero
            for b in range(rows):
                value = jnp.where(target == b, blocks[b], value)
            parts.append(value)
        return jnp.concatenate(parts, axis=0).astype(jnp.bfloat16)

    def window_copy(k):
        to = lax.rem(me + k, count)
        return send(outgoing.at[k], returned.at[me], window_sems, k, to)

    def reply(k, carry):
        outgoing[k] = window(k)
        window_copy(k).start()
        return carry

    lax.fori_loop(1, count, reply, jnp.int32(0))
    returned[me] = window(0)

    def finish(k, carry):
        window_copy(k).wait_recv()
        return carry

    lax.fori_loop(1, count, finish, jnp.int32(0))

    for quad in range(ANGLES // QUAD):
        parts = []
        for sub in range(QUAD // angles_here):
            at = quad * (QUAD // angles_here) + sub
            for r in range(owners):
                message = returned[r * cols + at].astype(jnp.float32)
                for t in range(across):
                    parts.append(message[t * tile_rows : t * tile_rows + per_tile])
        flat = jnp.concatenate(parts, axis=0)
        turned = []
        for e in range(TILE // 8):
            keys = []
            for r in range(e * 8, e * 8 + 8):
                a = r // slices_here % angles_here
                t = r // (slices_here * angles_here) % across
                a = a + r // (slices_here * angles_here * across * owners) * angles_here
                start = starts_ref[row, col * across + t, quad * QUAD + a]
                keys.append(((a, t), start))
            shift = select_rows(keys)
            turned.append(lookup(flat[e * 8 : e * 8 + 8], (lanes + shift) & (TILE - 1)))
        bins_first = jnp.concatenate(turned, axis=0).T
        for b in range(TILE // 8):
            span = slice(MARGIN + b * 8, MARGIN + b * 8 + 8)
            value = lookup(bins_first[b * 8 : b * 8 + 8], order)
            for k in range(GROUPS):
                moved = pltpu.roll(value, width * k, 1) if k else value
                for a in range(QUAD):
                    g = (a + k) % GROUPS
                    store_ref[g * ANGLES + quad * QUAD + a, span, :] = jnp.where(
                        group == g, moved, 0.0
                    )

    def block(urb, vb):
        i = urb * RIGHT + vb
        top = urb * HIGH + TV_STEPS
        left = pl.multiple_of(vb * WIDE, WIDE) + EXTRA
        total = None
        for g in range(GROUPS):
            shadows = jnp.concatenate(
                [
                    store_ref[g * ANGLES + a, pl.ds(first_ref[i, g * ANGLES + a], BINS), :]
                    for a in range(ANGLES)
                ],
                axis=0,
            ).astype(jnp.bfloat16)
            weights = hat(q_ref[...] + wide_ref[g, pl.ds(i, 1), :])
            part = jnp.dot(weights, shadows, preferred_element_type=jnp.float32)
            total = part if total is None else total + part
        total = total * (relaxation * proj_scale)
        for k in range(HIGH):
            p_ref[top + k, pl.ds(left, WIDE), :] = (
                p_ref[top + k, pl.ds(left, WIDE), :] + total[k * WIDE : (k + 1) * WIDE]
            )

    def outer_rows(i, carry):
        block((i // RIGHT) * (DOWN - 1), i % RIGHT)
        return carry

    def outer_columns(i, carry):
        block(1 + i // 2, (i % 2) * (RIGHT - 1))
        return carry

    def inner_blocks(i, carry):
        block(1 + i // (RIGHT - 2), 1 + i % (RIGHT - 2))
        return carry

    lax.fori_loop(0, 2 * RIGHT, outer_rows, jnp.int32(0))
    lax.fori_loop(0, 2 * (DOWN - 2), outer_columns, jnp.int32(0))
    pack_edges(p_ref, row_edge, col_edge, slices)

    copies = []
    for k, (down, right, src, dst) in enumerate(routes):
        copy = pltpu.make_async_remote_copy(
            src_ref=src,
            dst_ref=dst,
            send_sem=edge_sems.at[0, k],
            recv_sem=edge_sems.at[1, k],
            device_id=(row + down, col + right),
            device_id_type=MESH,
        )
        copies.append((down, right, copy))
        pl.when(exists(down, right))(copy.start)
    lax.fori_loop(0, (DOWN - 2) * (RIGHT - 2), inner_blocks, jnp.int32(0))
    for down, right, copy in copies:
        pl.when(exists(-down, -right))(copy.wait_recv)

    inner = slice(EXTRA, EXTRA + TILE)
    half_rows = GROUP_ROWS // 2

    def shift(value, by):
        by = by % TILE
        return pltpu.roll(value, by, 1) if by else value

    for i in range(TV_STEPS):
        for b in range(0, TILE, 16):
            above = row_halo[0, b : b + 16, :].astype(jnp.float32)
            below = row_halo[1, b : b + 16, :].astype(jnp.float32)
            for half in range(2):
                to = slice(EXTRA + b + half * 8, EXTRA + b + half * 8 + 8)
                piece = slice(half * 8, half * 8 + 8)
                p_ref[i, to, :] = jnp.where(
                    group == 0,
                    shift(above[piece], -width * i),
                    shift(p_ref[GROUP_ROWS + i, to, :], width),
                )
                p_ref[TV_STEPS + GROUP_ROWS + i, to, :] = jnp.where(
                    group == GROUPS - 1,
                    shift(below[piece], width * (GROUPS - 1 - i)),
                    shift(p_ref[TV_STEPS + i, to, :], -width),
                )

    left, right = [], []
    for j in range(half_rows):
        piece = slice((j % 2) * 8, (j % 2) * 8 + 8)
        left.append(col_halo[0, j // 2].astype(jnp.float32)[piece])
        right.append(col_halo[1, j // 2].astype(jnp.float32)[piece])

    def from_left(ur):
        return left[ur] if ur < half_rows else shift(left[ur - half_rows], -slices)

    def from_right(ur):
        return shift(right[ur], slices) if ur < half_rows else right[ur - half_rows]

    def corner_of(down, side):
        value = corner[down, side].astype(jnp.float32)
        return value[8:16] if side == 0 else value[0:8]

    for r in range(ROWS):
        ur = r - TV_STEPS
        if ur < 0:
            outer = [from_left(GROUP_ROWS + ur), from_right(GROUP_ROWS + ur)]
            edge = [
                shift(corner_of(0, 0), -width * r - slices),
                shift(corner_of(0, 1), -width * r + slices),
            ]
            outer = [jnp.where(group == 0, e, shift(o, width)) for e, o in zip(edge, outer)]
        elif ur >= GROUP_ROWS:
            i = ur - GROUP_ROWS
            outer = [from_left(i), from_right(i)]
            edge = [
                shift(corner_of(1, 0), width * (GROUPS - 1 - i) - slices),
                shift(corner_of(1, 1), width * (GROUPS - 1 - i) + slices),
            ]
            outer = [jnp.where(group == GROUPS - 1, e, shift(o, -width)) for e, o in zip(edge, outer)]
        else:
            outer = [from_left(ur), from_right(ur)]
        p_ref[r, 0:EXTRA, :] = jnp.where(
            first_tile, outer[0], shift(p_ref[r, TILE : TILE + EXTRA, :], slices)
        )
        p_ref[r, EXTRA + TILE :, :] = jnp.where(
            first_tile, shift(p_ref[r, EXTRA : 2 * EXTRA, :], -slices), outer[1]
        )

    one, nought = jnp.ones((8, TILE), jnp.float32), jnp.zeros((8, TILE), jnp.float32)

    def there(near, outside):
        return jnp.where(outside, jnp.where(near, one, nought), one)

    keep_above = there(row > 0, group == 0)[0:1]
    keep_below = there(row < rows - 1, group == GROUPS - 1)[0:1]
    keep_left = there(col > 0, first_tile)
    keep_right = there(col < cols - 1, jnp.logical_not(first_tile))

    def flows(here, after):
        down = after - here
        across_ = pltpu.roll(here, SPAN - 1, 0) - here
        scale = lax.rsqrt(smoothing * smoothing + down * down + across_ * across_) * descent_step
        return down * scale, across_ * scale

    for step in range(TV_STEPS):
        low, high = step + 1, ROWS - 1 - step
        above_flow = flows(p_ref[step], p_ref[step + 1])[0]

        def one_row(r, above_flow, place):
            here = p_ref[r]
            flow_down, flow_right = flows(here, p_ref[r + 1])
            change = above_flow - flow_down + pltpu.roll(flow_right, 1, 0) - flow_right
            value = here - change
            if place == "out":
                turned = value[inner].T
                for g in range(GROUPS):
                    for t in range(across):
                        for s in range(0, slices, 8):
                            at = (g * across + t) * slices + s
                            start = s * TILE + g * GROUP_ROWS + r - TV_STEPS
                            z_ref[t, pl.ds(start, 8, stride=TILE), :] = turned[at : at + 8]
                return flow_down
            if place == "above":
                value = value * keep_above
            if place == "below":
                value = value * keep_below
            p_ref[r, inner, :] = value[inner]
            p_ref[r, 0:EXTRA, :] = value[0:EXTRA] * keep_left
            p_ref[r, EXTRA + TILE :, :] = value[EXTRA + TILE :] * keep_right
            return flow_down

        if step == TV_STEPS - 1:
            lax.fori_loop(low, high, lambda r, f: one_row(r, f, "out"), above_flow)
        else:
            for r in range(low, TV_STEPS):
                above_flow = one_row(r, above_flow, "above")
            above_flow = lax.fori_loop(
                TV_STEPS, TV_STEPS + GROUP_ROWS, lambda r, f: one_row(r, f, ""), above_flow
            )
            for r in range(TV_STEPS + GROUP_ROWS, high):
                above_flow = one_row(r, above_flow, "below")

    writes = [
        pltpu.make_async_copy(
            z_ref.at[t], out_ref.at[:, pl.ds(t * TILE, TILE)], copy_sems.at[t]
        )
        for t in range(across)
    ]
    for copy in writes:
        copy.start()
    for down, right, copy in copies:
        pl.when(exists(down, right))(copy.wait_send)
    def settle(k, carry):
        shadow_copy(k).wait_send()
        window_copy(k).wait_send()
        return carry

    lax.fori_loop(1, count, settle, jnp.int32(0))

    def settle_scan(k, carry):
        scan_copy(k).wait_send()
        return carry

    lax.fori_loop(1, rows, settle_scan, jnp.int32(0))
    for copy in writes:
        copy.wait()


def update(image, sent, measured, ray_weight, shadow_start, first, table):
    rows = lax.axis_size("row")
    cols = lax.axis_size("col")
    slices, height, width = image.shape
    angles_here = ANGLES // cols
    slices_here = slices // rows
    tile_rows = tile_rows_of(angles_here, slices_here)
    count, depth, unused = sent.shape
    across = depth // tile_rows
    kernel = lambda *refs: update_kernel(
        *refs, slices=slices, angles_here=angles_here, slices_here=slices_here,
        across=across, tile_rows=tile_rows,
    )
    dma = pltpu.SemaphoreType.DMA
    row_edge = pltpu.VMEM((2, TILE, TILE), jnp.bfloat16)
    col_edge = pltpu.VMEM((2, GROUP_ROWS // 4, 16, TILE), jnp.bfloat16)
    return pl.pallas_call(
        kernel,
        out_shape=jax.ShapeDtypeStruct((slices * height, width), jnp.float32),
        in_specs=[SMEM] * 2 + [VMEM] * 4 + [HBM],
        out_specs=HBM,
        scratch_shapes=[
            pltpu.VMEM((rows, 2 * tile_rows, TILE), jnp.float32),
            pltpu.VMEM((GROUPS, BLOCKS, ANGLES * BINS), jnp.float32),
            pltpu.VMEM((3 * TILE, TILE), jnp.float32),
            pltpu.VMEM(sent.shape, jnp.bfloat16),
            pltpu.VMEM((rows, 2 * tile_rows, TILE), jnp.float32),
            pltpu.VMEM((count, across, tile_rows, TILE), jnp.int32),
            pltpu.VMEM(sent.shape, jnp.bfloat16),
            pltpu.VMEM(sent.shape, jnp.bfloat16),
            pltpu.VMEM((GROUPS * ANGLES, DEPTH, TILE), jnp.float32),
            pltpu.VMEM((TILE, ANGLES * BINS), jnp.float32),
            pltpu.VMEM((ROWS, SPAN, TILE), jnp.float32),
            pltpu.VMEM((across, slices * height, TILE), jnp.float32),
            row_edge, col_edge, row_edge, col_edge,
            pltpu.VMEM((2, 2, 16, TILE), jnp.bfloat16),
            dma((2, count)),
            dma((2, rows)),
            dma((2, count)),
            dma((2, 8)),
            dma((across,)),
        ],
        compiler_params=pltpu.CompilerParams(
            collective_id=0, has_side_effects=True, vmem_limit_bytes=60 << 20
        ),
        name="update",
    )(
        shadow_start, first, sent, measured.reshape(-1, TILE), ray_weight.reshape(-1, TILE),
        table, image.reshape(slices * height, width),
    ).reshape(image.shape)


def local(current_image, measured, ray_weight, angle_ids, shadow_start):
    sent, first, table = project(current_image, angle_ids, shadow_start)
    return update(current_image, sent, measured, ray_weight, shadow_start, first, table)


def solution(mesh):
    return jax.shard_map(
        local,
        mesh=mesh,
        in_specs=(
            P(None, "row", "col"),
            P("col", "row", None, None),
            P("col", "row", None),
            P(),
            P(),
        ),
        out_specs=P(None, "row", "col"),
        check_vma=False,
    )
```

```python
import math

import jax
import jax.numpy as jnp
from jax import lax
from jax.experimental import pallas as pl
from jax.experimental.pallas import tpu as pltpu
from jax.sharding import PartitionSpec as P

TILE = 128
ANGLES = 16
ALL_ANGLES = 256
TV_STEPS = 4
PACK = TILE // TV_STEPS

HIGH = 8
WIDE = 16
BINS = 16
MARGIN = 8
DEPTH = MARGIN + TILE + BINS
GROUPS = 4
GROUP_ROWS = TILE // GROUPS
DOWN = GROUP_ROWS // HIGH
RIGHT = TILE // WIDE
QUAD = 4

inverse_root = 0.7071067811865476
proj_scale = 0.03125
relaxation = 8.0
smoothing = 0.25
descent_step = 0.05

MESH = pl.DeviceIdType.MESH
SMEM = pl.BlockSpec(memory_space=pltpu.SMEM)
VMEM = pl.BlockSpec(memory_space=pltpu.VMEM)
HBM = pl.BlockSpec(memory_space=pltpu.HBM)


def lookup(table, index):
    return jnp.take_along_axis(table, index, axis=1, mode="promise_in_bounds")


def lane_iota():
    return lax.broadcasted_iota(jnp.int32, (8, TILE), 1)


def row_iota():
    return lax.broadcasted_iota(jnp.int32, (8, TILE), 0)


BLOCKS = DOWN * RIGHT
PAIR = 2


def geometry(angle_ref):
    lanes = lane_iota()
    ids = jnp.zeros((8, TILE), jnp.int32)
    for a in range(ANGLES):
        ids = jnp.where(lanes % ANGLES == a, angle_ref[a], ids)
    radians = ids.astype(jnp.float32) * (math.pi / ALL_ANGLES)
    down = jnp.cos(radians) * inverse_root
    right = jnp.sin(radians) * inverse_root
    centre = (TILE - 1) / 2.0
    firsts, offsets = [], []
    for b in range(0, BLOCKS, 8):
        block = row_iota() + b
        row = (block // RIGHT) * HIGH + (lanes // ANGLES % GROUPS) * GROUP_ROWS
        column = (block % RIGHT) * WIDE
        row = row.astype(jnp.float32) - centre
        column = column.astype(jnp.float32) - centre
        place = TILE / 2.0 + (row * down + column * right)
        lowest = place + jnp.minimum(0.0, (HIGH - 1) * down) + jnp.minimum(0.0, (WIDE - 1) * right)
        first = jnp.floor(lowest - 0.5)
        firsts.append(first.astype(jnp.int32) + MARGIN)
        offsets.append(place - first - 0.5)
    return down, right, jnp.concatenate(firsts, axis=0), jnp.concatenate(offsets, axis=0)


def pair_source(slices_here, slices, across):
    lanes = lane_iota()
    owners = slices // slices_here
    s = lanes % slices_here
    a = lanes // slices_here % PAIR
    t = lanes // (slices_here * PAIR) % across
    r = lanes // (slices_here * PAIR * across) % owners
    kind = lanes // (slices_here * PAIR * across * owners)
    return ((kind * PAIR + a) * across + t) * slices + r * slices_here + s


def quad_source(angles_here, slices_here, slices, across):
    lanes = lane_iota()
    slice_ = lanes % slices
    t = lanes // slices % across
    angle = lanes // (slices * across)
    sub, a = angle // angles_here, angle % angles_here
    r, s = slice_ // slices_here, slice_ % slices_here
    owner = sub * (slices // slices_here) + r
    return ((owner * across + t) * angles_here + a) * slices_here + s


def select_rows(values):
    rows = row_iota()
    result = jnp.full((8, TILE), values[0][1], jnp.int32)
    for r in range(1, 8):
        if values[r][0] != values[r - 1][0]:
            result = jnp.where(rows >= r, values[r][1], result)
    return result


def hat(distance):
    return jnp.maximum(1.0 - jnp.abs(distance), 0.0).astype(jnp.bfloat16)


def to_pixels(z_ref, ur, across, slices, mirrored=GROUPS):
    parts = []
    mirror = TILE - 1 - lane_iota()
    for g in range(GROUPS):
        row = ur if g < mirrored else GROUP_ROWS - 1 - ur
        for t in range(across):
            for s in range(0, slices, 8):
                start = s * TILE + g * GROUP_ROWS + row
                part = z_ref[t, pl.ds(start, 8, stride=TILE), :]
                parts.append(part if g < mirrored else lookup(part, mirror))
    pixels = jnp.concatenate(parts, axis=0)
    return pixels.T if mirrored == GROUPS else pixels.astype(jnp.bfloat16).T


def forward_kernel(
    angle_ref, x_ref, starts_ref, measured_ref, weight_ref,
    acc_ref, first_out, table_out, starts_out, measured_out, weight_out,
    z_ref, xb_ref, q_ref, first_ref, offset_ref, sems,
    *, slices, across,
):
    copies = [
        pltpu.make_async_copy(
            x_ref.at[:, pl.ds(t * TILE, TILE)], z_ref.at[t], sems.at[t]
        )
        for t in range(across)
    ]
    for copy in copies:
        copy.start()

    passed = [
        pltpu.make_async_copy(starts_ref, starts_out, sems.at[across + 2]),
        pltpu.make_async_copy(measured_ref, measured_out, sems.at[across + 3]),
        pltpu.make_async_copy(weight_ref, weight_out, sems.at[across + 4]),
    ]
    for copy in passed:
        copy.start()
    down, right, first, offset = geometry(angle_ref)
    first_out[...] = first
    table_out[0:BLOCKS] = offset
    table_out[BLOCKS : BLOCKS + 8] = down
    table_out[BLOCKS + 8 :] = right
    scalars = [
        pltpu.make_async_copy(first_out, first_ref, sems.at[across]),
        pltpu.make_async_copy(table_out.at[0:BLOCKS], offset_ref, sems.at[across + 1]),
    ]
    for copy in scalars:
        copy.start()
    pixel = lane_iota()
    pixel_row = (pixel // WIDE).astype(jnp.float32)
    pixel_column = (pixel % WIDE).astype(jnp.float32)
    bins = row_iota().astype(jnp.float32)
    for a in range(ANGLES):
        at = jnp.full((8, TILE), a, jnp.int32)
        place = pixel_row * lookup(down, at) + pixel_column * lookup(right, at)
        for b in range(0, BINS, 8):
            q_ref[a, b : b + 8, :] = place - (bins + b)

    half = GROUPS // 2

    def clear(k, carry):
        acc_ref[k] = jnp.zeros((DEPTH, TILE), jnp.float32)
        return carry

    lax.fori_loop(0, half * ANGLES, clear, jnp.int32(0))
    for copy in copies:
        copy.wait()

    def turn(ur, carry):
        xb_ref[ur] = to_pixels(z_ref, ur, across, slices, half)
        return carry

    lax.fori_loop(0, GROUP_ROWS, turn, jnp.int32(0), unroll=4)
    for copy in scalars:
        copy.wait()

    def block(i, carry):
        top = (i // RIGHT) * HIGH
        left = pl.multiple_of((i % RIGHT) * WIDE, WIDE)
        pixels = jnp.concatenate(
            [xb_ref[top + k, pl.ds(left, WIDE), :] for k in range(HIGH)], axis=0
        )
        for g in range(half):
            weights = jnp.concatenate(
                [hat(q_ref[a] + offset_ref[i, g * ANGLES + a]) for a in range(ANGLES)], axis=0
            )
            shadow = jnp.dot(weights, pixels, preferred_element_type=jnp.float32)
            spans = [pl.ds(first_ref[i, g * ANGLES + a], BINS) for a in range(ANGLES)]
            olds = [acc_ref[g * ANGLES + a, spans[a], :] for a in range(ANGLES)]
            for a in range(ANGLES):
                acc_ref[g * ANGLES + a, spans[a], :] = (
                    olds[a] + shadow[a * BINS : (a + 1) * BINS]
                )
        return carry

    lax.fori_loop(0, BLOCKS, block, jnp.int32(0), unroll=4)
    for copy in passed:
        copy.wait()


def tile_rows_of(angles_here, slices_here):
    return pl.cdiv(angles_here * slices_here, 8) * 8


def project(image, angle_ids, starts, measured, weight):
    slices, height, width = image.shape
    across = width // TILE
    kernel = lambda *refs: forward_kernel(*refs, slices=slices, across=across)
    return pl.pallas_call(
        kernel,
        out_shape=[
            pltpu.VMEM((GROUPS // 2 * ANGLES, DEPTH, TILE), jnp.float32),
            pltpu.VMEM((BLOCKS, TILE), jnp.int32),
            pltpu.VMEM((BLOCKS + 16, TILE), jnp.float32),
            pltpu.VMEM(starts.shape, starts.dtype),
            pltpu.VMEM(measured.shape, measured.dtype),
            pltpu.VMEM(weight.shape, weight.dtype),
        ],
        in_specs=[SMEM] + [HBM] * 4,
        out_specs=[VMEM] * 6,
        scratch_shapes=[
            pltpu.VMEM((across, slices * height, TILE), jnp.float32),
            pltpu.VMEM((GROUP_ROWS, TILE, TILE), jnp.bfloat16),
            pltpu.VMEM((ANGLES, BINS, TILE), jnp.float32),
            pltpu.SMEM((BLOCKS, TILE), jnp.int32),
            pltpu.SMEM((BLOCKS, TILE), jnp.float32),
            pltpu.SemaphoreType.DMA((across + 5,)),
        ],
        compiler_params=pltpu.CompilerParams(vmem_limit_bytes=58 << 20),
        name="project",
    )(angle_ids, image.reshape(slices * height, width), starts, measured, weight)


def ramp_table(n):
    gap = lax.broadcasted_iota(jnp.int32, (TILE, TILE), 1) - n * TILE
    gap = gap - lax.broadcasted_iota(jnp.int32, (TILE, TILE), 0)
    nonzero = jnp.where(gap == 0, 1, gap).astype(jnp.float32)
    value = -1.0 / (math.pi * math.pi * nonzero * nonzero)
    value = jnp.where((gap & 1) == 1, value, 0.0)
    value = jnp.where(gap == 0, 0.25, value)
    return jnp.where(jnp.abs(gap) < TILE, value, 0.0)


EXTRA = 8
SPAN = TILE + 2 * EXTRA
ROWS = GROUP_ROWS + 2 * TV_STEPS


def pack_edges(y_ref, row_edge_ref, col_edge_ref, slices):
    width = TILE // GROUPS
    lanes = lane_iota()
    group = lanes // width
    first_tile = lanes % width < slices
    for b in range(0, TILE, 16):
        for side in range(2):
            halves = []
            for half in range(2):
                span = slice(EXTRA + b + half * 8, EXTRA + b + half * 8 + 8)
                packed = None
                for i in range(TV_STEPS):
                    row = i if side == 0 else GROUP_ROWS - TV_STEPS + i
                    home = 0 if side == 0 else GROUPS - 1
                    value = pltpu.roll(y_ref[TV_STEPS + row, span, :], (width * (i - home)) % TILE, 1)
                    packed = value if packed is None else jnp.where(group == i, value, packed)
                halves.append(packed)
            row_edge_ref[side, b : b + 16, :] = jnp.concatenate(halves, axis=0).astype(jnp.bfloat16)
    half_rows = GROUP_ROWS // 2
    for j in range(0, half_rows, 2):
        for side in range(2):
            start = EXTRA if side == 0 else TILE
            span = slice(start, start + 8)
            parts = []
            for k in (j, j + 1):
                near = y_ref[TV_STEPS + k, span, :]
                far = y_ref[TV_STEPS + k + half_rows, span, :]
                if side == 0:
                    far = pltpu.roll(far, slices, 1)
                else:
                    near = pltpu.roll(near, TILE - slices, 1)
                parts.append(jnp.where(first_tile, near, far))
            col_edge_ref[side, j // 2] = jnp.concatenate(parts, axis=0).astype(jnp.bfloat16)


def update_kernel(
    starts_ref, first_ref, acc_ref, measured_ref, weight_ref, table_ref, x_ref, z_ref,
    sent_ref, scan_out, wide_ref, ramp_ref, landed, scan, target_ref, outgoing, returned, store_ref, q_ref, p_ref,
    row_edge, col_edge, row_halo, col_halo, corner,
    shadow_sems, scan_sems, window_sems, edge_sems, copy_sems,
    *, slices, angles_here, slices_here, across, tile_rows,
):
    rows = lax.axis_size("row")
    cols = lax.axis_size("col")
    row = lax.axis_index("row")
    col = lax.axis_index("col")
    count = rows * cols
    me = row * cols + col

    def send(src, dst, sems, k, to_row, to_col):
        return pltpu.make_async_remote_copy(
            src_ref=src, dst_ref=dst, send_sem=sems.at[0, k], recv_sem=sems.at[1, k],
            device_id=(to_row, to_col), device_id_type=MESH,
        )

    width = TILE // GROUPS
    lanes = lane_iota()
    group = lanes // width
    first_tile = lanes % width < slices
    order = quad_source(angles_here, slices_here, slices, across)
    per_tile = angles_here * slices_here
    owners = slices // slices_here
    low, high = pl.ds(0, 16), pl.ds(TILE - 16, 16)
    routes = (
        (-1, 0, row_edge.at[0], row_halo.at[1]),
        (1, 0, row_edge.at[1], row_halo.at[0]),
        (0, -1, col_edge.at[0], col_halo.at[1]),
        (0, 1, col_edge.at[1], col_halo.at[0]),
        (-1, -1, row_edge.at[0, low], corner.at[1, 1]),
        (-1, 1, row_edge.at[0, high], corner.at[1, 0]),
        (1, -1, row_edge.at[1, low], corner.at[0, 1]),
        (1, 1, row_edge.at[1, high], corner.at[0, 0]),
    )

    def exists(down, right):
        to_row, to_col = row + down, col + right
        return (to_row >= 0) & (to_row < rows) & (to_col >= 0) & (to_col < cols)

    reads = [
        pltpu.make_async_copy(
            x_ref.at[:, pl.ds(t * TILE, TILE)], z_ref.at[t], copy_sems.at[t]
        )
        for t in range(across)
    ]
    for copy in reads:
        copy.start()
    for r in range(rows):
        for a in range(angles_here):
            to = a * slices_here
            scan_out[r, to : to + slices_here] = measured_ref[
                a * slices + r * slices_here : a * slices + (r + 1) * slices_here
            ]
            scan_out[r, tile_rows + to : tile_rows + to + slices_here] = jnp.broadcast_to(
                weight_ref[a : a + 1], (slices_here, TILE)
            )
        if tile_rows > per_tile:
            spare = jnp.zeros((tile_rows - per_tile, TILE), jnp.float32)
            scan_out[r, per_tile:tile_rows] = spare
            scan_out[r, tile_rows + per_tile :] = spare
    row_halo[...] = jnp.zeros(row_halo.shape, row_halo.dtype)
    col_halo[...] = jnp.zeros(col_halo.shape, col_halo.dtype)
    corner[...] = jnp.zeros(corner.shape, corner.dtype)
    barrier = pltpu.get_barrier_semaphore()

    def peer(down, right):
        to_row, to_col = row + down, col + right
        to_row = jnp.where(to_row >= rows, to_row - rows, to_row)
        return to_row, jnp.where(to_col >= cols, to_col - cols, to_col)

    def all_peers(body, first=0):
        def some(j, carry):
            down = lax.rem(j + first, rows)

            @pl.when(down > 0)
            def _():
                body(down, 0)

            for right in range(1, cols):
                body(down, right)
            return carry

        lax.fori_loop(0, rows, some, jnp.int32(0))

    def greet(down, right):
        pl.semaphore_signal(barrier, inc=1, device_id=peer(down, right), device_id_type=MESH)

    all_peers(greet, rows // 2)

    near = pair_source(slices_here, slices, across)
    far = near ^ width
    piece = PAIR * slices_here
    kind_rows = TILE // 2

    def pick(span, values):
        result = acc_ref[values[0], span, :]
        for g in range(1, GROUPS):
            result = jnp.where(group == g, acc_ref[values[g], span, :], result)
        return result

    def pair_shadows(pair):
        here, there = pair * PAIR, pair * PAIR + 1
        pieces = []
        for b in range(TILE // 8):
            span = slice(MARGIN + b * 8, MARGIN + b * 8 + 8)
            own = pick(span, (here, ANGLES + there, ANGLES + here, there))
            other = pick(span, (there, ANGLES + here, ANGLES + there, here))
            pieces.append(lookup(own, near) + lookup(other, far))
        rows = jnp.concatenate(pieces, axis=0).T
        sent = []
        for e in range(kind_rows // 8):
            keys = []
            for r in range(e * 8, e * 8 + 8):
                a = r // slices_here % PAIR
                t = r // (slices_here * PAIR) % across
                start = starts_ref[row, col * across + t, pair * PAIR + a]
                keys.append(((a, t), start))
            index = (lanes - select_rows(keys)) & (TILE - 1)
            value = lookup(rows[e * 8 : e * 8 + 8], index) + lookup(
                rows[kind_rows + e * 8 : kind_rows + e * 8 + 8], TILE - 1 - index
            )
            sent.append(value * proj_scale)
        return jnp.concatenate(sent, axis=0)

    for owner in range(cols):
        pairs = angles_here // PAIR
        shadows = [pair_shadows(owner * pairs + p) for p in range(pairs)]
        for r in range(owners):
            parts = []
            for t in range(across):
                at = (r * across + t) * piece
                parts += [shadow[at : at + piece] for shadow in shadows]
                if tile_rows > per_tile:
                    parts.append(jnp.zeros((tile_rows - per_tile, TILE), jnp.float32))
            message = jnp.concatenate(parts, axis=0)
            sent_ref[r * cols + owner] = message.astype(jnp.bfloat16)

    pl.semaphore_wait(barrier, count - 1)

    def shadow_copy(down, right):
        k = down * cols + right
        to_row, to_col = peer(down, right)
        src = sent_ref.at[to_row * cols + to_col]
        return send(src, landed.at[k], shadow_sems, k, to_row, to_col)

    def scan_copy(down):
        to_row, to_col = peer(down, 0)
        return send(scan_out.at[to_row], scan.at[down], scan_sems, down, to_row, to_col)

    all_peers(lambda down, right: shadow_copy(down, right).start(), rows // 2)
    for down in range(1, rows):
        scan_copy(down).start()
    landed[0] = sent_ref[me]
    scan[0] = scan_out[row]

    sublanes = row_iota()

    def aim(down, carry):
        for right in range(cols):
            to_row, to_col = peer(down, right)
            for t in range(across):
                start = jnp.full(
                    (8, TILE), starts_ref[to_row, to_col * across + t, col * angles_here], jnp.int32
                )
                for a in range(1, angles_here):
                    value = starts_ref[to_row, to_col * across + t, col * angles_here + a]
                    start = jnp.where(sublanes >= a * slices_here, value, start)
                block = (start >> 7) + jnp.where(lanes < (start & (TILE - 1)), 1, 0)
                target_ref[down, right, t] = block
        return carry

    lax.fori_loop(0, rows, aim, jnp.int32(0))

    for k in range(GROUPS * ANGLES):
        store_ref[k, 0:MARGIN, :] = jnp.zeros((MARGIN, TILE), jnp.float32)
        store_ref[k, MARGIN + TILE :, :] = jnp.zeros((DEPTH - MARGIN - TILE, TILE), jnp.float32)
    for n in (-1, 0, 1):
        ramp_ref[(n + 1) * TILE : (n + 2) * TILE] = ramp_table(n)

    def add(down, right, sums):
        message = landed[down * cols + right].astype(jnp.float32)
        back = lax.rem(rows - down, rows)
        for t in range(across):
            value = message[t * tile_rows : (t + 1) * tile_rows]
            target = target_ref[back, (cols - right) % cols, t]
            sums = tuple(
                total + jnp.where(target == b, value, 0.0) for b, total in enumerate(sums)
            )
        return sums

    zero = jnp.zeros((tile_rows, TILE), jnp.float32)
    sums = add(0, 0, (zero,) * rows)
    for right in range(1, cols):
        shadow_copy(0, right).wait_recv()
        sums = add(0, right, sums)

    def add_row(down, sums):
        for right in range(cols):
            shadow_copy(down, right).wait_recv()
        for right in range(cols):
            sums = add(down, right, sums)
        return sums

    sums = lax.fori_loop(1, rows, add_row, sums)
    for down in range(1, rows):
        scan_copy(down).wait_recv()
    residual = []
    for b in range(rows):
        here = scan[lax.rem(row - b + rows, rows)]
        residual.append(here[tile_rows:] * (here[:tile_rows] - sums[b]))
    stacked = jnp.concatenate(
        [
            jnp.concatenate([zero] + residual[:-1], axis=0),
            jnp.concatenate(residual, axis=0),
            jnp.concatenate(residual[1:] + [zero], axis=0),
        ],
        axis=1,
    )
    filtered = jnp.dot(
        stacked, ramp_ref[...], precision=lax.Precision.HIGHEST,
        preferred_element_type=jnp.float32,
    )
    blocks = tuple(filtered[b * tile_rows : (b + 1) * tile_rows] for b in range(rows))

    def window(down, right):
        parts = []
        for t in range(across):
            target = target_ref[down, right, t]
            value = zero
            for b in range(rows):
                value = jnp.where(target == b, blocks[b], value)
            parts.append(value)
        return jnp.concatenate(parts, axis=0).astype(jnp.bfloat16)

    def window_copy(down, right):
        k = down * cols + right
        return send(outgoing.at[k], returned.at[me], window_sems, k, *peer(down, right))

    def reply(j, carry):
        down = lax.rem(j + rows // 2, rows)
        for right in range(cols):
            outgoing[down * cols + right] = window(down, right)
        pl.when(down > 0)(window_copy(down, 0).start)
        for right in range(1, cols):
            window_copy(down, right).start()
        return carry

    lax.fori_loop(0, rows, reply, jnp.int32(0))
    returned[me] = outgoing[0]

    pixel = row_iota()
    bins = (lanes % BINS).astype(jnp.float32)
    down = table_ref[BLOCKS : BLOCKS + 8]
    right = table_ref[BLOCKS + 8 :]
    for h in range(ANGLES * BINS // TILE):
        at = lanes // BINS + h * (TILE // BINS)
        down_here, right_here = lookup(down, at), lookup(right, at)
        span = slice(h * TILE, (h + 1) * TILE)
        for b in range(0, TILE, 8):
            pixel_row = ((pixel + b) // WIDE).astype(jnp.float32)
            pixel_column = ((pixel + b) % WIDE).astype(jnp.float32)
            q_ref[b : b + 8, span] = pixel_row * down_here + pixel_column * right_here - bins
        for g in range(GROUPS):
            for b in range(0, BLOCKS, 8):
                wide_ref[g, b : b + 8, span] = lookup(table_ref[b : b + 8], at + g * ANGLES)

    for copy in reads:
        copy.wait()

    def turn(ur, carry):
        p_ref[TV_STEPS + ur, EXTRA : EXTRA + TILE, :] = to_pixels(z_ref, ur, across, slices) * (
            1.0 / descent_step
        )
        return carry

    lax.fori_loop(0, GROUP_ROWS, turn, jnp.int32(0), unroll=2)

    all_peers(lambda down, right: window_copy(down, right).wait_recv())

    for quad in range(ANGLES // QUAD):
        parts = []
        for sub in range(QUAD // angles_here):
            at = quad * (QUAD // angles_here) + sub
            for r in range(owners):
                message = returned[r * cols + at].astype(jnp.float32)
                for t in range(across):
                    parts.append(message[t * tile_rows : t * tile_rows + per_tile])
        flat = jnp.concatenate(parts, axis=0)
        turned = []
        for e in range(TILE // 8):
            keys = []
            for r in range(e * 8, e * 8 + 8):
                a = r // slices_here % angles_here
                t = r // (slices_here * angles_here) % across
                a = a + r // (slices_here * angles_here * across * owners) * angles_here
                start = starts_ref[row, col * across + t, quad * QUAD + a]
                keys.append(((a, t), start))
            shift = select_rows(keys)
            turned.append(lookup(flat[e * 8 : e * 8 + 8], (lanes + shift) & (TILE - 1)))
        bins_first = jnp.concatenate(turned, axis=0).T
        for b in range(TILE // 8):
            span = slice(MARGIN + b * 8, MARGIN + b * 8 + 8)
            value = lookup(bins_first[b * 8 : b * 8 + 8], order)
            for k in range(GROUPS):
                moved = pltpu.roll(value, width * k, 1) if k else value
                for a in range(QUAD):
                    g = (a + k) % GROUPS
                    store_ref[g * ANGLES + quad * QUAD + a, span, :] = jnp.where(
                        group == g, moved, 0.0
                    )

    def block(urb, vb):
        i = urb * RIGHT + vb
        top = urb * HIGH + TV_STEPS
        left = pl.multiple_of(vb * WIDE, WIDE) + EXTRA
        total = None
        for g in range(GROUPS):
            shadows = jnp.concatenate(
                [
                    store_ref[g * ANGLES + a, pl.ds(first_ref[i, g * ANGLES + a], BINS), :]
                    for a in range(ANGLES)
                ],
                axis=0,
            ).astype(jnp.bfloat16)
            weights = hat(q_ref[...] + wide_ref[g, pl.ds(i, 1), :])
            part = jnp.dot(weights, shadows, preferred_element_type=jnp.float32)
            total = part if total is None else total + part
        total = total * (relaxation * proj_scale / descent_step)
        for k in range(HIGH):
            p_ref[top + k, pl.ds(left, WIDE), :] = (
                p_ref[top + k, pl.ds(left, WIDE), :] + total[k * WIDE : (k + 1) * WIDE]
            )

    def outer_rows(i, carry):
        block((i // RIGHT) * (DOWN - 1), i % RIGHT)
        return carry

    def outer_columns(i, carry):
        block(1 + i // 2, (i % 2) * (RIGHT - 1))
        return carry

    def inner_blocks(i, carry):
        block(1 + i // (RIGHT - 2), 1 + i % (RIGHT - 2))
        return carry

    lax.fori_loop(0, 2 * RIGHT, outer_rows, jnp.int32(0), unroll=4)
    lax.fori_loop(0, 2 * (DOWN - 2), outer_columns, jnp.int32(0), unroll=4)
    pack_edges(p_ref, row_edge, col_edge, slices)

    copies = []
    for k, (down, right, src, dst) in enumerate(routes):
        copy = pltpu.make_async_remote_copy(
            src_ref=src,
            dst_ref=dst,
            send_sem=edge_sems.at[0, k],
            recv_sem=edge_sems.at[1, k],
            device_id=(row + down, col + right),
            device_id_type=MESH,
        )
        copies.append((down, right, copy))
        pl.when(exists(down, right))(copy.start)
    lax.fori_loop(0, (DOWN - 2) * (RIGHT - 2), inner_blocks, jnp.int32(0), unroll=4)
    for down, right, copy in copies:
        pl.when(exists(-down, -right))(copy.wait_recv)

    inner = slice(EXTRA, EXTRA + TILE)
    half_rows = GROUP_ROWS // 2

    def shift(value, by):
        by = by % TILE
        return pltpu.roll(value, by, 1) if by else value

    for i in range(TV_STEPS):
        for b in range(0, TILE, 16):
            above = row_halo[0, b : b + 16, :].astype(jnp.float32)
            below = row_halo[1, b : b + 16, :].astype(jnp.float32)
            for half in range(2):
                to = slice(EXTRA + b + half * 8, EXTRA + b + half * 8 + 8)
                piece = slice(half * 8, half * 8 + 8)
                p_ref[i, to, :] = jnp.where(
                    group == 0,
                    shift(above[piece], -width * i),
                    shift(p_ref[GROUP_ROWS + i, to, :], width),
                )
                p_ref[TV_STEPS + GROUP_ROWS + i, to, :] = jnp.where(
                    group == GROUPS - 1,
                    shift(below[piece], width * (GROUPS - 1 - i)),
                    shift(p_ref[TV_STEPS + i, to, :], -width),
                )

    left, right = [], []
    for j in range(half_rows):
        piece = slice((j % 2) * 8, (j % 2) * 8 + 8)
        left.append(col_halo[0, j // 2].astype(jnp.float32)[piece])
        right.append(col_halo[1, j // 2].astype(jnp.float32)[piece])

    def from_left(ur):
        return left[ur] if ur < half_rows else shift(left[ur - half_rows], -slices)

    def from_right(ur):
        return shift(right[ur], slices) if ur < half_rows else right[ur - half_rows]

    def corner_of(down, side):
        value = corner[down, side].astype(jnp.float32)
        return value[8:16] if side == 0 else value[0:8]

    for r in range(ROWS):
        ur = r - TV_STEPS
        if ur < 0:
            outer = [from_left(GROUP_ROWS + ur), from_right(GROUP_ROWS + ur)]
            edge = [
                shift(corner_of(0, 0), -width * r - slices),
                shift(corner_of(0, 1), -width * r + slices),
            ]
            outer = [jnp.where(group == 0, e, shift(o, width)) for e, o in zip(edge, outer)]
        elif ur >= GROUP_ROWS:
            i = ur - GROUP_ROWS
            outer = [from_left(i), from_right(i)]
            edge = [
                shift(corner_of(1, 0), width * (GROUPS - 1 - i) - slices),
                shift(corner_of(1, 1), width * (GROUPS - 1 - i) + slices),
            ]
            outer = [jnp.where(group == GROUPS - 1, e, shift(o, -width)) for e, o in zip(edge, outer)]
        else:
            outer = [from_left(ur), from_right(ur)]
        p_ref[r, 0:EXTRA, :] = jnp.where(
            first_tile, outer[0], shift(p_ref[r, TILE : TILE + EXTRA, :], slices)
        )
        p_ref[r, EXTRA + TILE :, :] = jnp.where(
            first_tile, shift(p_ref[r, EXTRA : 2 * EXTRA, :], -slices), outer[1]
        )

    one, nought = jnp.ones((8, TILE), jnp.float32), jnp.zeros((8, TILE), jnp.float32)

    def there(near, outside):
        return jnp.where(outside, jnp.where(near, one, nought), one)

    keep_above = there(row > 0, group == 0)[0:1]
    keep_below = there(row < rows - 1, group == GROUPS - 1)[0:1]
    keep_left = there(col > 0, first_tile)
    keep_right = there(col < cols - 1, jnp.logical_not(first_tile))

    limit = (smoothing / descent_step) ** 2
    columns = SPAN // 8
    sublanes = row_iota()
    last, head = sublanes == 7, sublanes == 0

    def flow_rows(r, wanted):
        here = [p_ref[r, j * 8 : j * 8 + 8, :] for j in range(columns)]
        turned = [pltpu.roll(value, 7, 0) for value in here]
        result = []
        for j in range(columns):
            following = jnp.where(last, turned[min(j + 1, columns - 1)], turned[j])
            down = p_ref[r + 1, j * 8 : j * 8 + 8, :] - here[j]
            right = following - here[j]
            scale = lax.rsqrt(limit + down * down + right * right)
            result.append((here[j], down * scale, right * scale if wanted else None))
        return result

    for step in range(TV_STEPS):
        low, high = step + 1, ROWS - 1 - step
        above_flow = tuple(flow for here, flow, unused in flow_rows(step, False))

        def one_row(r, above_flow, place):
            found = flow_rows(r, True)
            turned = [pltpu.roll(right, 1, 0) for here, down, right in found]
            values = []
            for j, (here, down, right) in enumerate(found):
                before = jnp.where(head, turned[max(j - 1, 0)], turned[j])
                values.append(here - (above_flow[j] - down + (before - right)))
            below_flow = tuple(down for here, down, right in found)
            if place == "out":
                kept = jnp.concatenate(values[EXTRA // 8 : -(EXTRA // 8)], axis=0) * descent_step
                flipped = kept.T
                for g in range(GROUPS):
                    for t in range(across):
                        for s in range(0, slices, 8):
                            at = (g * across + t) * slices + s
                            start = s * TILE + g * GROUP_ROWS + r - TV_STEPS
                            z_ref[t, pl.ds(start, 8, stride=TILE), :] = flipped[at : at + 8]
                return below_flow
            values[0] = values[0] * keep_left
            values[-1] = values[-1] * keep_right
            for j, value in enumerate(values):
                if place == "above":
                    value = value * keep_above
                if place == "below":
                    value = value * keep_below
                p_ref[r, j * 8 : j * 8 + 8, :] = value
            return below_flow

        if step == TV_STEPS - 1:
            lax.fori_loop(low, high, lambda r, f: one_row(r, f, "out"), above_flow, unroll=4)
        else:
            for r in range(low, TV_STEPS):
                above_flow = one_row(r, above_flow, "above")
            above_flow = lax.fori_loop(
                TV_STEPS, TV_STEPS + GROUP_ROWS, lambda r, f: one_row(r, f, ""), above_flow, unroll=4
            )
            for r in range(TV_STEPS + GROUP_ROWS, high):
                above_flow = one_row(r, above_flow, "below")

    for down, right, copy in copies:
        pl.when(exists(down, right))(copy.wait_send)
    def settle(down, right):
        shadow_copy(down, right).wait_send()
        window_copy(down, right).wait_send()

    all_peers(settle)
    for down in range(1, rows):
        scan_copy(down).wait_send()


def update(image, shadows, first, table, starts, measured, weight):
    rows = lax.axis_size("row")
    cols = lax.axis_size("col")
    slices, height, width = image.shape
    angles_here = ANGLES // cols
    slices_here = slices // rows
    tile_rows = tile_rows_of(angles_here, slices_here)
    count = rows * cols
    across = width // TILE
    message = pltpu.VMEM((count, across * tile_rows, TILE), jnp.bfloat16)
    kernel = lambda *refs: update_kernel(
        *refs, slices=slices, angles_here=angles_here, slices_here=slices_here,
        across=across, tile_rows=tile_rows,
    )
    dma = pltpu.SemaphoreType.DMA
    row_edge = pltpu.VMEM((2, TILE, TILE), jnp.bfloat16)
    col_edge = pltpu.VMEM((2, GROUP_ROWS // 4, 16, TILE), jnp.bfloat16)
    parts = pl.pallas_call(
        kernel,
        out_shape=pltpu.VMEM((across, slices * height, TILE), jnp.float32),
        in_specs=[SMEM] * 2 + [VMEM] * 4 + [HBM],
        out_specs=VMEM,
        scratch_shapes=[
            message,
            pltpu.VMEM((rows, 2 * tile_rows, TILE), jnp.float32),
            pltpu.VMEM((GROUPS, BLOCKS, ANGLES * BINS), jnp.float32),
            pltpu.VMEM((3 * TILE, TILE), jnp.float32),
            message,
            pltpu.VMEM((rows, 2 * tile_rows, TILE), jnp.float32),
            pltpu.VMEM((rows, cols, across, tile_rows, TILE), jnp.int32),
            message,
            message,
            pltpu.VMEM((GROUPS * ANGLES, DEPTH, TILE), jnp.float32),
            pltpu.VMEM((TILE, ANGLES * BINS), jnp.float32),
            pltpu.VMEM((ROWS, SPAN, TILE), jnp.float32),
            row_edge, col_edge, row_edge, col_edge,
            pltpu.VMEM((2, 2, 16, TILE), jnp.bfloat16),
            dma((2, count)),
            dma((2, rows)),
            dma((2, count)),
            dma((2, 8)),
            dma((across,)),
        ],
        compiler_params=pltpu.CompilerParams(
            collective_id=0, has_side_effects=True, vmem_limit_bytes=40 << 20
        ),
        name="update",
    )(
        starts, first, shadows, measured, weight, table, image.reshape(slices * height, width),
    )
    parts = parts.reshape(across, slices, height, TILE)
    return parts.transpose(1, 2, 0, 3).reshape(image.shape)


def local(current_image, measured, ray_weight, angle_ids, shadow_start):
    measured, weight = measured.reshape(-1, TILE), ray_weight.reshape(-1, TILE)
    made = project(current_image, angle_ids, shadow_start, measured, weight)
    return update(current_image, *made)


def solution(mesh):
    return jax.shard_map(
        local,
        mesh=mesh,
        in_specs=(
            P(None, "row", "col"),
            P("col", "row", None, None),
            P("col", "row", None),
            P(),
            P(),
        ),
        out_specs=P(None, "row", "col"),
        check_vma=False,
    )
```

```python
import math

import jax
import jax.numpy as jnp
from jax import lax
from jax.experimental import pallas as pl
from jax.experimental.pallas import tpu as pltpu
from jax.sharding import PartitionSpec as P

TILE = 128
ANGLES = 16
ALL_ANGLES = 256
TV_STEPS = 4
PACK = TILE // TV_STEPS

HIGH = 8
WIDE = 16
BINS = 16
MARGIN = 8
DEPTH = MARGIN + TILE + BINS
GROUPS = 4
GROUP_ROWS = TILE // GROUPS
DOWN = GROUP_ROWS // HIGH
RIGHT = TILE // WIDE
QUAD = 4

inverse_root = 0.7071067811865476
proj_scale = 0.03125
relaxation = 8.0
smoothing = 0.25
descent_step = 0.05

MESH = pl.DeviceIdType.MESH
SMEM = pl.BlockSpec(memory_space=pltpu.SMEM)
VMEM = pl.BlockSpec(memory_space=pltpu.VMEM)
HBM = pl.BlockSpec(memory_space=pltpu.HBM)


def lookup(table, index):
    return jnp.take_along_axis(table, index, axis=1, mode="promise_in_bounds")


def lane_iota():
    return lax.broadcasted_iota(jnp.int32, (8, TILE), 1)


def row_iota():
    return lax.broadcasted_iota(jnp.int32, (8, TILE), 0)


BLOCKS = DOWN * RIGHT
PAIR = 2


def geometry(angle_ref):
    lanes = lane_iota()
    ids = jnp.zeros((8, TILE), jnp.int32)
    for a in range(ANGLES):
        ids = jnp.where(lanes % ANGLES == a, angle_ref[a], ids)
    radians = ids.astype(jnp.float32) * (math.pi / ALL_ANGLES)
    down = jnp.cos(radians) * inverse_root
    right = jnp.sin(radians) * inverse_root
    centre = (TILE - 1) / 2.0
    firsts, offsets = [], []
    for b in range(0, BLOCKS, 8):
        block = row_iota() + b
        row = (block // RIGHT) * HIGH + (lanes // ANGLES % GROUPS) * GROUP_ROWS
        column = (block % RIGHT) * WIDE
        row = row.astype(jnp.float32) - centre
        column = column.astype(jnp.float32) - centre
        place = TILE / 2.0 + (row * down + column * right)
        lowest = place + jnp.minimum(0.0, (HIGH - 1) * down) + jnp.minimum(0.0, (WIDE - 1) * right)
        first = jnp.floor(lowest - 0.5)
        firsts.append(first.astype(jnp.int32) + MARGIN)
        offsets.append(place - first - 0.5)
    return down, right, jnp.concatenate(firsts, axis=0), jnp.concatenate(offsets, axis=0)


def pair_source(slices_here, slices, across):
    lanes = lane_iota()
    owners = slices // slices_here
    s = lanes % slices_here
    a = lanes // slices_here % PAIR
    t = lanes // (slices_here * PAIR) % across
    r = lanes // (slices_here * PAIR * across) % owners
    kind = lanes // (slices_here * PAIR * across * owners)
    return ((kind * PAIR + a) * across + t) * slices + r * slices_here + s


def quad_source(angles_here, slices_here, slices, across):
    lanes = lane_iota()
    slice_ = lanes % slices
    t = lanes // slices % across
    angle = lanes // (slices * across)
    sub, a = angle // angles_here, angle % angles_here
    r, s = slice_ // slices_here, slice_ % slices_here
    owner = sub * (slices // slices_here) + r
    return ((owner * across + t) * angles_here + a) * slices_here + s


def select_rows(values):
    rows = row_iota()
    result = jnp.full((8, TILE), values[0][1], jnp.int32)
    for r in range(1, 8):
        if values[r][0] != values[r - 1][0]:
            result = jnp.where(rows >= r, values[r][1], result)
    return result


def hat(distance):
    return jnp.maximum(1.0 - jnp.abs(distance), 0.0).astype(jnp.bfloat16)


def to_pixels(z_ref, ur, across, slices, mirrored=GROUPS):
    parts = []
    mirror = TILE - 1 - lane_iota()
    for g in range(GROUPS):
        row = ur if g < mirrored else GROUP_ROWS - 1 - ur
        for t in range(across):
            for s in range(0, slices, 8):
                start = s * TILE + g * GROUP_ROWS + row
                part = z_ref[t, pl.ds(start, 8, stride=TILE), :]
                parts.append(part if g < mirrored else lookup(part, mirror))
    pixels = jnp.concatenate(parts, axis=0)
    return pixels.T if mirrored == GROUPS else pixels.astype(jnp.bfloat16).T


def forward_kernel(
    angle_ref, x_ref, starts_ref, measured_ref, weight_ref,
    acc_ref, first_out, table_out, starts_out, measured_out, weight_out, z_ref,
    xb_ref, q_ref, first_ref, offset_ref, sems,
    *, slices, across,
):
    copies = [
        pltpu.make_async_copy(
            x_ref.at[:, pl.ds(t * TILE, TILE)], z_ref.at[t], sems.at[t]
        )
        for t in range(across)
    ]
    for copy in copies:
        copy.start()

    passed = [
        pltpu.make_async_copy(starts_ref, starts_out, sems.at[across + 2]),
        pltpu.make_async_copy(measured_ref, measured_out, sems.at[across + 3]),
        pltpu.make_async_copy(weight_ref, weight_out, sems.at[across + 4]),
    ]
    for copy in passed:
        copy.start()
    down, right, first, offset = geometry(angle_ref)
    first_out[...] = first
    table_out[0:BLOCKS] = offset
    table_out[BLOCKS : BLOCKS + 8] = down
    table_out[BLOCKS + 8 :] = right
    scalars = [
        pltpu.make_async_copy(first_out, first_ref, sems.at[across]),
        pltpu.make_async_copy(table_out.at[0:BLOCKS], offset_ref, sems.at[across + 1]),
    ]
    for copy in scalars:
        copy.start()
    pixel = lane_iota()
    pixel_row = (pixel // WIDE).astype(jnp.float32)
    pixel_column = (pixel % WIDE).astype(jnp.float32)
    bins = row_iota().astype(jnp.float32)
    for a in range(ANGLES):
        at = jnp.full((8, TILE), a, jnp.int32)
        place = pixel_row * lookup(down, at) + pixel_column * lookup(right, at)
        for b in range(0, BINS, 8):
            q_ref[a, b : b + 8, :] = place - (bins + b)

    half = GROUPS // 2

    def clear(k, carry):
        acc_ref[k] = jnp.zeros((DEPTH, TILE), jnp.float32)
        return carry

    lax.fori_loop(0, half * ANGLES, clear, jnp.int32(0))
    for copy in copies:
        copy.wait()

    def turn(ur, carry):
        xb_ref[ur] = to_pixels(z_ref, ur, across, slices, half)
        return carry

    lax.fori_loop(0, GROUP_ROWS, turn, jnp.int32(0), unroll=8)
    for copy in scalars:
        copy.wait()

    def block(i, carry):
        top = (i // RIGHT) * HIGH
        left = pl.multiple_of((i % RIGHT) * WIDE, WIDE)
        pixels = jnp.concatenate(
            [xb_ref[top + k, pl.ds(left, WIDE), :] for k in range(HIGH)], axis=0
        )
        for g in range(half):
            weights = jnp.concatenate(
                [hat(q_ref[a] + offset_ref[i, g * ANGLES + a]) for a in range(ANGLES)], axis=0
            )
            shadow = jnp.dot(weights, pixels, preferred_element_type=jnp.float32)
            spans = [pl.ds(first_ref[i, g * ANGLES + a], BINS) for a in range(ANGLES)]
            olds = [acc_ref[g * ANGLES + a, spans[a], :] for a in range(ANGLES)]
            for a in range(ANGLES):
                acc_ref[g * ANGLES + a, spans[a], :] = (
                    olds[a] + shadow[a * BINS : (a + 1) * BINS]
                )
        return carry

    lax.fori_loop(0, BLOCKS, block, jnp.int32(0), unroll=8)
    for copy in passed:
        copy.wait()


def tile_rows_of(angles_here, slices_here):
    return pl.cdiv(angles_here * slices_here, 8) * 8


def project(image, angle_ids, starts, measured, weight):
    slices, height, width = image.shape
    across = width // TILE
    kernel = lambda *refs: forward_kernel(*refs, slices=slices, across=across)
    return pl.pallas_call(
        kernel,
        out_shape=[
            pltpu.VMEM((GROUPS // 2 * ANGLES, DEPTH, TILE), jnp.float32),
            pltpu.VMEM((BLOCKS, TILE), jnp.int32),
            pltpu.VMEM((BLOCKS + 16, TILE), jnp.float32),
            pltpu.VMEM(starts.shape, starts.dtype),
            pltpu.VMEM(measured.shape, measured.dtype),
            pltpu.VMEM(weight.shape, weight.dtype),
            pltpu.VMEM((across, slices * height, TILE), jnp.float32),
        ],
        in_specs=[SMEM] + [HBM] * 4,
        out_specs=[VMEM] * 7,
        scratch_shapes=[
            pltpu.VMEM((GROUP_ROWS, TILE, TILE), jnp.bfloat16),
            pltpu.VMEM((ANGLES, BINS, TILE), jnp.float32),
            pltpu.SMEM((BLOCKS, TILE), jnp.int32),
            pltpu.SMEM((BLOCKS, TILE), jnp.float32),
            pltpu.SemaphoreType.DMA((across + 5,)),
        ],
        compiler_params=pltpu.CompilerParams(vmem_limit_bytes=58 << 20),
        name="project",
    )(angle_ids, image.reshape(slices * height, width), starts, measured, weight)


def ramp_table(n):
    gap = lax.broadcasted_iota(jnp.int32, (TILE, TILE), 1) - n * TILE
    gap = gap - lax.broadcasted_iota(jnp.int32, (TILE, TILE), 0)
    nonzero = jnp.where(gap == 0, 1, gap).astype(jnp.float32)
    value = -1.0 / (math.pi * math.pi * nonzero * nonzero)
    value = jnp.where((gap & 1) == 1, value, 0.0)
    value = jnp.where(gap == 0, 0.25, value)
    return jnp.where(jnp.abs(gap) < TILE, value, 0.0)


EXTRA = 8
SPAN = TILE + 2 * EXTRA
ROWS = GROUP_ROWS + 2 * TV_STEPS


def pack_rows(y_ref, row_edge_ref):
    width = TILE // GROUPS
    group = lane_iota() // width
    for b in range(0, TILE, 16):
        for side in range(2):
            halves = []
            for half in range(2):
                span = slice(EXTRA + b + half * 8, EXTRA + b + half * 8 + 8)
                packed = None
                for i in range(TV_STEPS):
                    row = i if side == 0 else GROUP_ROWS - TV_STEPS + i
                    home = 0 if side == 0 else GROUPS - 1
                    value = pltpu.roll(y_ref[TV_STEPS + row, span, :], (width * (i - home)) % TILE, 1)
                    packed = value if packed is None else jnp.where(group == i, value, packed)
                halves.append(packed)
            row_edge_ref[side, b : b + 16, :] = jnp.concatenate(halves, axis=0).astype(jnp.bfloat16)


def pack_columns(y_ref, col_edge_ref, slices):
    first_tile = lane_iota() % (TILE // GROUPS) < slices
    half_rows = GROUP_ROWS // 2
    for j in range(0, half_rows, 2):
        for side in range(2):
            start = EXTRA if side == 0 else TILE
            span = slice(start, start + 8)
            parts = []
            for k in (j, j + 1):
                near = y_ref[TV_STEPS + k, span, :]
                far = y_ref[TV_STEPS + k + half_rows, span, :]
                if side == 0:
                    far = pltpu.roll(far, slices, 1)
                else:
                    near = pltpu.roll(near, TILE - slices, 1)
                parts.append(jnp.where(first_tile, near, far))
            col_edge_ref[side, j // 2] = jnp.concatenate(parts, axis=0).astype(jnp.bfloat16)


def update_kernel(
    starts_ref, first_ref, acc_ref, measured_ref, weight_ref, table_ref, x_ref, p_ref,
    sent_ref, scan_out, wide_ref, ramp_ref, landed, scan, target_ref, outgoing, returned, store_ref, q_ref,
    row_edge, col_edge, row_halo, col_halo, corner,
    shadow_sems, scan_sems, window_sems, edge_sems,
    *, slices, angles_here, slices_here, across, tile_rows,
):
    rows = lax.axis_size("row")
    cols = lax.axis_size("col")
    row = lax.axis_index("row")
    col = lax.axis_index("col")
    count = rows * cols
    me = row * cols + col

    def send(src, dst, sems, k, to_row, to_col):
        return pltpu.make_async_remote_copy(
            src_ref=src, dst_ref=dst, send_sem=sems.at[0, k], recv_sem=sems.at[1, k],
            device_id=(to_row, to_col), device_id_type=MESH,
        )

    width = TILE // GROUPS
    lanes = lane_iota()
    group = lanes // width
    first_tile = lanes % width < slices
    order = quad_source(angles_here, slices_here, slices, across)
    per_tile = angles_here * slices_here
    owners = slices // slices_here
    low, high = pl.ds(0, 16), pl.ds(TILE - 16, 16)
    routes = (
        (-1, 0, row_edge.at[0], row_halo.at[1]),
        (1, 0, row_edge.at[1], row_halo.at[0]),
        (0, -1, col_edge.at[0], col_halo.at[1]),
        (0, 1, col_edge.at[1], col_halo.at[0]),
        (-1, -1, row_edge.at[0, low], corner.at[1, 1]),
        (-1, 1, row_edge.at[0, high], corner.at[1, 0]),
        (1, -1, row_edge.at[1, low], corner.at[0, 1]),
        (1, 1, row_edge.at[1, high], corner.at[0, 0]),
    )

    def exists(down, right):
        to_row, to_col = row + down, col + right
        return (to_row >= 0) & (to_row < rows) & (to_col >= 0) & (to_col < cols)

    for r in range(rows):
        for a in range(angles_here):
            to = a * slices_here
            scan_out[r, to : to + slices_here] = measured_ref[
                a * slices + r * slices_here : a * slices + (r + 1) * slices_here
            ]
            scan_out[r, tile_rows + to : tile_rows + to + slices_here] = jnp.broadcast_to(
                weight_ref[a : a + 1], (slices_here, TILE)
            )
        if tile_rows > per_tile:
            spare = jnp.zeros((tile_rows - per_tile, TILE), jnp.float32)
            scan_out[r, per_tile:tile_rows] = spare
            scan_out[r, tile_rows + per_tile :] = spare
    row_halo[...] = jnp.zeros(row_halo.shape, row_halo.dtype)
    col_halo[...] = jnp.zeros(col_halo.shape, col_halo.dtype)
    corner[...] = jnp.zeros(corner.shape, corner.dtype)
    barrier = pltpu.get_barrier_semaphore()

    def peer(down, right):
        to_row, to_col = row + down, col + right
        to_row = jnp.where(to_row >= rows, to_row - rows, to_row)
        return to_row, jnp.where(to_col >= cols, to_col - cols, to_col)

    def all_peers(body, first=0):
        def some(j, carry):
            down = lax.rem(j + first, rows)

            @pl.when(down > 0)
            def _():
                body(down, 0)

            for right in range(1, cols):
                body(down, right)
            return carry

        lax.fori_loop(0, rows, some, jnp.int32(0))

    def greet(down, right):
        pl.semaphore_signal(barrier, inc=1, device_id=peer(down, right), device_id_type=MESH)

    all_peers(greet, rows // 2)

    near = pair_source(slices_here, slices, across)
    far = near ^ width
    piece = PAIR * slices_here
    kind_rows = TILE // 2

    def pick(span, values):
        result = acc_ref[values[0], span, :]
        for g in range(1, GROUPS):
            result = jnp.where(group == g, acc_ref[values[g], span, :], result)
        return result

    def pair_shadows(pair):
        here, there = pair * PAIR, pair * PAIR + 1
        pieces = []
        for b in range(TILE // 8):
            span = slice(MARGIN + b * 8, MARGIN + b * 8 + 8)
            own = pick(span, (here, ANGLES + there, ANGLES + here, there))
            other = pick(span, (there, ANGLES + here, ANGLES + there, here))
            pieces.append(lookup(own, near) + lookup(other, far))
        rows = jnp.concatenate(pieces, axis=0).T
        sent = []
        for e in range(kind_rows // 8):
            keys = []
            for r in range(e * 8, e * 8 + 8):
                a = r // slices_here % PAIR
                t = r // (slices_here * PAIR) % across
                start = starts_ref[row, col * across + t, pair * PAIR + a]
                keys.append(((a, t), start))
            index = (lanes - select_rows(keys)) & (TILE - 1)
            value = lookup(rows[e * 8 : e * 8 + 8], index) + lookup(
                rows[kind_rows + e * 8 : kind_rows + e * 8 + 8], TILE - 1 - index
            )
            sent.append(value * proj_scale)
        return jnp.concatenate(sent, axis=0)

    for owner in range(cols):
        pairs = angles_here // PAIR
        shadows = [pair_shadows(owner * pairs + p) for p in range(pairs)]
        for r in range(owners):
            parts = []
            for t in range(across):
                at = (r * across + t) * piece
                parts += [shadow[at : at + piece] for shadow in shadows]
                if tile_rows > per_tile:
                    parts.append(jnp.zeros((tile_rows - per_tile, TILE), jnp.float32))
            message = jnp.concatenate(parts, axis=0)
            sent_ref[r * cols + owner] = message.astype(jnp.bfloat16)

    pl.semaphore_wait(barrier, count - 1)

    def shadow_copy(down, right):
        k = down * cols + right
        to_row, to_col = peer(down, right)
        src = sent_ref.at[to_row * cols + to_col]
        return send(src, landed.at[k], shadow_sems, k, to_row, to_col)

    def scan_copy(down):
        to_row, to_col = peer(down, 0)
        return send(scan_out.at[to_row], scan.at[down], scan_sems, down, to_row, to_col)

    all_peers(lambda down, right: shadow_copy(down, right).start(), rows // 2)
    for down in range(1, rows):
        scan_copy(down).start()
    landed[0] = sent_ref[me]
    scan[0] = scan_out[row]

    sublanes = row_iota()

    def aim(down, carry):
        for right in range(cols):
            to_row, to_col = peer(down, right)
            for t in range(across):
                start = jnp.full(
                    (8, TILE), starts_ref[to_row, to_col * across + t, col * angles_here], jnp.int32
                )
                for a in range(1, angles_here):
                    value = starts_ref[to_row, to_col * across + t, col * angles_here + a]
                    start = jnp.where(sublanes >= a * slices_here, value, start)
                block = (start >> 7) + jnp.where(lanes < (start & (TILE - 1)), 1, 0)
                target_ref[down, right, t] = block
        return carry

    lax.fori_loop(0, rows, aim, jnp.int32(0))

    for k in range(GROUPS * ANGLES):
        store_ref[k, 0:MARGIN, :] = jnp.zeros((MARGIN, TILE), jnp.float32)
        store_ref[k, MARGIN + TILE :, :] = jnp.zeros((DEPTH - MARGIN - TILE, TILE), jnp.float32)
    for n in (-1, 0, 1):
        taps = ramp_table(n)
        coarse = taps.astype(jnp.bfloat16)
        ramp_ref[0, (n + 1) * TILE : (n + 2) * TILE] = coarse
        ramp_ref[1, (n + 1) * TILE : (n + 2) * TILE] = (
            taps - coarse.astype(jnp.float32)
        ).astype(jnp.bfloat16)

    def add(down, right, sums):
        message = landed[down * cols + right].astype(jnp.float32)
        back = lax.rem(rows - down, rows)
        for t in range(across):
            value = message[t * tile_rows : (t + 1) * tile_rows]
            target = target_ref[back, (cols - right) % cols, t]
            sums = tuple(
                total + jnp.where(target == b, value, 0.0) for b, total in enumerate(sums)
            )
        return sums

    zero = jnp.zeros((tile_rows, TILE), jnp.float32)
    sums = add(0, 0, (zero,) * rows)
    for right in range(1, cols):
        shadow_copy(0, right).wait_recv()
        sums = add(0, right, sums)

    def add_row(down, sums):
        for right in range(cols):
            shadow_copy(down, right).wait_recv()
        for right in range(cols):
            sums = add(down, right, sums)
        return sums

    sums = lax.fori_loop(1, rows, add_row, sums)
    for down in range(1, rows):
        scan_copy(down).wait_recv()
    residual = []
    for b in range(rows):
        here = scan[lax.rem(row - b + rows, rows)]
        residual.append(here[tile_rows:] * (here[:tile_rows] - sums[b]))
    stacked = jnp.concatenate(
        [
            jnp.concatenate([zero] + residual[:-1], axis=0),
            jnp.concatenate(residual, axis=0),
            jnp.concatenate(residual[1:] + [zero], axis=0),
        ],
        axis=1,
    )
    coarse = stacked.astype(jnp.bfloat16)
    fine = (stacked - coarse.astype(jnp.float32)).astype(jnp.bfloat16)
    both = jnp.dot(
        jnp.concatenate([coarse, fine], axis=0), ramp_ref[0], preferred_element_type=jnp.float32
    )
    filtered = both[: rows * tile_rows] + (
        both[rows * tile_rows :]
        + jnp.dot(coarse, ramp_ref[1], preferred_element_type=jnp.float32)
    )
    blocks = tuple(filtered[b * tile_rows : (b + 1) * tile_rows] for b in range(rows))

    def window(down, right):
        parts = []
        for t in range(across):
            target = target_ref[down, right, t]
            value = zero
            for b in range(rows):
                value = jnp.where(target == b, blocks[b], value)
            parts.append(value)
        return jnp.concatenate(parts, axis=0).astype(jnp.bfloat16)

    def window_copy(down, right):
        k = down * cols + right
        return send(outgoing.at[k], returned.at[me], window_sems, k, *peer(down, right))

    def reply(j, carry):
        down = lax.rem(j + rows // 2, rows)
        for right in range(cols):
            outgoing[down * cols + right] = window(down, right)
        pl.when(down > 0)(window_copy(down, 0).start)
        for right in range(1, cols):
            window_copy(down, right).start()
        return carry

    lax.fori_loop(0, rows, reply, jnp.int32(0), unroll=2)
    returned[me] = outgoing[0]

    pixel = row_iota()
    bins = (lanes % BINS).astype(jnp.float32)
    down = table_ref[BLOCKS : BLOCKS + 8]
    right = table_ref[BLOCKS + 8 :]
    for h in range(ANGLES * BINS // TILE):
        at = lanes // BINS + h * (TILE // BINS)
        down_here, right_here = lookup(down, at), lookup(right, at)
        span = slice(h * TILE, (h + 1) * TILE)
        for b in range(0, TILE, 8):
            pixel_row = ((pixel + b) // WIDE).astype(jnp.float32)
            pixel_column = ((pixel + b) % WIDE).astype(jnp.float32)
            q_ref[b : b + 8, span] = pixel_row * down_here + pixel_column * right_here - bins
        for g in range(GROUPS):
            for b in range(0, BLOCKS, 8):
                wide_ref[g, b : b + 8, span] = lookup(table_ref[b : b + 8], at + g * ANGLES)

    def turn(ur, carry):
        p_ref[TV_STEPS + ur, EXTRA : EXTRA + TILE, :] = to_pixels(x_ref, ur, across, slices) * (
            1.0 / descent_step
        )
        return carry

    lax.fori_loop(0, GROUP_ROWS, turn, jnp.int32(0), unroll=2)

    for quad in range(ANGLES // QUAD):
        parts = []
        for sub in range(QUAD // angles_here):
            at = quad * (QUAD // angles_here) + sub
            right = lax.rem(col - at + cols, cols)

            def arrived(down, carry, right=right):
                pl.when((down > 0) | (right > 0))(window_copy(down, right).wait_recv)
                return carry

            lax.fori_loop(0, rows, arrived, jnp.int32(0))
            for r in range(owners):
                message = returned[r * cols + at].astype(jnp.float32)
                for t in range(across):
                    parts.append(message[t * tile_rows : t * tile_rows + per_tile])
        flat = jnp.concatenate(parts, axis=0)
        turned = []
        for e in range(TILE // 8):
            keys = []
            for r in range(e * 8, e * 8 + 8):
                a = r // slices_here % angles_here
                t = r // (slices_here * angles_here) % across
                a = a + r // (slices_here * angles_here * across * owners) * angles_here
                start = starts_ref[row, col * across + t, quad * QUAD + a]
                keys.append(((a, t), start))
            shift = select_rows(keys)
            turned.append(lookup(flat[e * 8 : e * 8 + 8], (lanes + shift) & (TILE - 1)))
        bins_first = jnp.concatenate(turned, axis=0).T
        for b in range(TILE // 8):
            span = slice(MARGIN + b * 8, MARGIN + b * 8 + 8)
            value = lookup(bins_first[b * 8 : b * 8 + 8], order)
            for k in range(GROUPS):
                moved = pltpu.roll(value, width * k, 1) if k else value
                for a in range(QUAD):
                    g = (a + k) % GROUPS
                    store_ref[g * ANGLES + quad * QUAD + a, span, :] = jnp.where(
                        group == g, moved, 0.0
                    )

    def block(urb, vb):
        i = urb * RIGHT + vb
        top = urb * HIGH + TV_STEPS
        left = pl.multiple_of(vb * WIDE, WIDE) + EXTRA
        total = None
        for g in range(GROUPS):
            shadows = jnp.concatenate(
                [
                    store_ref[g * ANGLES + a, pl.ds(first_ref[i, g * ANGLES + a], BINS), :]
                    for a in range(ANGLES)
                ],
                axis=0,
            ).astype(jnp.bfloat16)
            weights = hat(q_ref[...] + wide_ref[g, pl.ds(i, 1), :])
            part = jnp.dot(weights, shadows, preferred_element_type=jnp.float32)
            total = part if total is None else total + part
        total = total * (relaxation * proj_scale / descent_step)
        for k in range(HIGH):
            p_ref[top + k, pl.ds(left, WIDE), :] = (
                p_ref[top + k, pl.ds(left, WIDE), :] + total[k * WIDE : (k + 1) * WIDE]
            )

    def outer_rows(i, carry):
        block((i // RIGHT) * (DOWN - 1), i % RIGHT)
        return carry

    def outer_columns(i, carry):
        block(1 + i // 2, (i % 2) * (RIGHT - 1))
        return carry

    def inner_blocks(i, carry):
        block(1 + i // (RIGHT - 2), 1 + i % (RIGHT - 2))
        return carry

    copies = []
    for k, (down, right, src, dst) in enumerate(routes):
        copy = pltpu.make_async_remote_copy(
            src_ref=src,
            dst_ref=dst,
            send_sem=edge_sems.at[0, k],
            recv_sem=edge_sems.at[1, k],
            device_id=(row + down, col + right),
            device_id_type=MESH,
        )
        copies.append((down, right, copy))
    lax.fori_loop(0, 2 * RIGHT, outer_rows, jnp.int32(0), unroll=8)
    pack_rows(p_ref, row_edge)
    for down, right, copy in copies:
        if down:
            pl.when(exists(down, right))(copy.start)
    lax.fori_loop(0, 2 * (DOWN - 2), outer_columns, jnp.int32(0), unroll=4)
    pack_columns(p_ref, col_edge, slices)
    for down, right, copy in copies:
        if not down:
            pl.when(exists(down, right))(copy.start)
    lax.fori_loop(0, (DOWN - 2) * (RIGHT - 2), inner_blocks, jnp.int32(0), unroll=6)
    for down, right, copy in copies:
        pl.when(exists(-down, -right))(copy.wait_recv)

    inner = slice(EXTRA, EXTRA + TILE)
    half_rows = GROUP_ROWS // 2

    def shift(value, by):
        by = by % TILE
        return pltpu.roll(value, by, 1) if by else value

    for i in range(TV_STEPS):
        for b in range(0, TILE, 16):
            above = row_halo[0, b : b + 16, :].astype(jnp.float32)
            below = row_halo[1, b : b + 16, :].astype(jnp.float32)
            for half in range(2):
                to = slice(EXTRA + b + half * 8, EXTRA + b + half * 8 + 8)
                piece = slice(half * 8, half * 8 + 8)
                p_ref[i, to, :] = jnp.where(
                    group == 0,
                    shift(above[piece], -width * i),
                    shift(p_ref[GROUP_ROWS + i, to, :], width),
                )
                p_ref[TV_STEPS + GROUP_ROWS + i, to, :] = jnp.where(
                    group == GROUPS - 1,
                    shift(below[piece], width * (GROUPS - 1 - i)),
                    shift(p_ref[TV_STEPS + i, to, :], -width),
                )

    left, right = [], []
    for j in range(half_rows):
        piece = slice((j % 2) * 8, (j % 2) * 8 + 8)
        left.append(col_halo[0, j // 2].astype(jnp.float32)[piece])
        right.append(col_halo[1, j // 2].astype(jnp.float32)[piece])

    def from_left(ur):
        return left[ur] if ur < half_rows else shift(left[ur - half_rows], -slices)

    def from_right(ur):
        return shift(right[ur], slices) if ur < half_rows else right[ur - half_rows]

    def corner_of(down, side):
        value = corner[down, side].astype(jnp.float32)
        return value[8:16] if side == 0 else value[0:8]

    for r in range(ROWS):
        ur = r - TV_STEPS
        if ur < 0:
            outer = [from_left(GROUP_ROWS + ur), from_right(GROUP_ROWS + ur)]
            edge = [
                shift(corner_of(0, 0), -width * r - slices),
                shift(corner_of(0, 1), -width * r + slices),
            ]
            outer = [jnp.where(group == 0, e, shift(o, width)) for e, o in zip(edge, outer)]
        elif ur >= GROUP_ROWS:
            i = ur - GROUP_ROWS
            outer = [from_left(i), from_right(i)]
            edge = [
                shift(corner_of(1, 0), width * (GROUPS - 1 - i) - slices),
                shift(corner_of(1, 1), width * (GROUPS - 1 - i) + slices),
            ]
            outer = [jnp.where(group == GROUPS - 1, e, shift(o, -width)) for e, o in zip(edge, outer)]
        else:
            outer = [from_left(ur), from_right(ur)]
        p_ref[r, 0:EXTRA, :] = jnp.where(
            first_tile, outer[0], shift(p_ref[r, TILE : TILE + EXTRA, :], slices)
        )
        p_ref[r, EXTRA + TILE :, :] = jnp.where(
            first_tile, shift(p_ref[r, EXTRA : 2 * EXTRA, :], -slices), outer[1]
        )

    for down, right, copy in copies:
        pl.when(exists(down, right))(copy.wait_send)
    def settle(down, right):
        shadow_copy(down, right).wait_send()
        window_copy(down, right).wait_send()

    all_peers(settle)
    for down in range(1, rows):
        scan_copy(down).wait_send()


def update(image, shadows, first, table, starts, measured, weight, x):
    rows = lax.axis_size("row")
    cols = lax.axis_size("col")
    slices, height, width = image.shape
    angles_here = ANGLES // cols
    slices_here = slices // rows
    tile_rows = tile_rows_of(angles_here, slices_here)
    count = rows * cols
    across = width // TILE
    message = pltpu.VMEM((count, across * tile_rows, TILE), jnp.bfloat16)
    kernel = lambda *refs: update_kernel(
        *refs, slices=slices, angles_here=angles_here, slices_here=slices_here,
        across=across, tile_rows=tile_rows,
    )
    dma = pltpu.SemaphoreType.DMA
    row_edge = pltpu.VMEM((2, TILE, TILE), jnp.bfloat16)
    col_edge = pltpu.VMEM((2, GROUP_ROWS // 4, 16, TILE), jnp.bfloat16)
    return pl.pallas_call(
        kernel,
        out_shape=pltpu.VMEM((ROWS, SPAN, TILE), jnp.float32),
        in_specs=[SMEM] * 2 + [VMEM] * 5,
        out_specs=VMEM,
        scratch_shapes=[
            message,
            pltpu.VMEM((rows, 2 * tile_rows, TILE), jnp.float32),
            pltpu.VMEM((GROUPS, BLOCKS, ANGLES * BINS), jnp.float32),
            pltpu.VMEM((2, 3 * TILE, TILE), jnp.bfloat16),
            message,
            pltpu.VMEM((rows, 2 * tile_rows, TILE), jnp.float32),
            pltpu.VMEM((rows, cols, across, tile_rows, TILE), jnp.int32),
            message,
            message,
            pltpu.VMEM((GROUPS * ANGLES, DEPTH, TILE), jnp.float32),
            pltpu.VMEM((TILE, ANGLES * BINS), jnp.float32),
            row_edge, col_edge, row_edge, col_edge,
            pltpu.VMEM((2, 2, 16, TILE), jnp.bfloat16),
            dma((2, count)),
            dma((2, rows)),
            dma((2, count)),
            dma((2, 8)),
        ],
        compiler_params=pltpu.CompilerParams(
            collective_id=0, has_side_effects=True, vmem_limit_bytes=40 << 20
        ),
        name="update",
    )(
        starts, first, shadows, measured, weight, table, x,
    )


CHUNK = 8


def smooth_kernel(p_ref, out_ref, held_ref, z_ref, sems, *, slices, across):
    row = lax.axis_index("row")
    col = lax.axis_index("col")
    rows = lax.axis_size("row")
    cols = lax.axis_size("col")
    group = lane_iota() // (TILE // GROUPS)
    first_tile = lane_iota() % (TILE // GROUPS) < slices
    whole = z_ref.reshape(across, slices, GROUPS, GROUP_ROWS, TILE)
    writes = []
    one, nought = jnp.ones((8, TILE), jnp.float32), jnp.zeros((8, TILE), jnp.float32)

    def there(near, outside):
        return jnp.where(outside, jnp.where(near, one, nought), one)

    keep_above = there(row > 0, group == 0)[0:1]
    keep_below = there(row < rows - 1, group == GROUPS - 1)[0:1]
    keep_left = there(col > 0, first_tile)
    keep_right = there(col < cols - 1, jnp.logical_not(first_tile))

    limit = (smoothing / descent_step) ** 2
    columns = SPAN // 8
    sublanes = row_iota()
    last, head = sublanes == 7, sublanes == 0

    def sweep(source, r, above, emit):
        def at(r, j):
            return source[r, j * 8 : j * 8 + 8, :]

        below = []
        here, turned, left = at(r, 0), pltpu.roll(at(r, 0), 7, 0), None
        for j in range(columns):
            k = min(j + 1, columns - 1)
            ahead = at(r, k)
            ahead_turned = pltpu.roll(ahead, 7, 0)
            down = at(r + 1, j) - here
            right = jnp.where(last, ahead_turned, turned) - here
            scale = lax.rsqrt(limit + (down * down + right * right))
            down, right = down * scale, right * scale
            if emit is not None:
                moved = pltpu.roll(right, 1, 0)
                before = moved if left is None else jnp.where(head, left, moved)
                emit(j, (here - above[j]) + (down - before) + right)
                left = moved
            below.append(down)
            here, turned = ahead, ahead_turned
        return tuple(below)

    for step in range(TV_STEPS):
        low, high = step + 1, ROWS - 1 - step
        source = p_ref if step == 0 else held_ref
        above_flow = sweep(source, step, None, None)

        def one_row(r, above_flow, place, source=source):
            values = []

            def emit(j, value):
                if place == "out":
                    values.append(value)
                    return
                if j == 0:
                    value = value * keep_left
                if j == columns - 1:
                    value = value * keep_right
                if place == "above":
                    value = value * keep_above
                if place == "below":
                    value = value * keep_below
                held_ref[r, j * 8 : j * 8 + 8, :] = value

            below_flow = sweep(source, r, above_flow, emit)
            if place == "out":
                kept = jnp.concatenate(values[EXTRA // 8 : -(EXTRA // 8)], axis=0) * descent_step
                flipped = kept.T
                for g in range(GROUPS):
                    for t in range(across):
                        for s in range(0, slices, 8):
                            lane = (g * across + t) * slices + s
                            start = s * TILE + g * GROUP_ROWS + r - TV_STEPS
                            z_ref[t, pl.ds(start, 8, stride=TILE), :] = flipped[lane : lane + 8]
            return below_flow

        if step == TV_STEPS - 1:
            for c in range(GROUP_ROWS // CHUNK):
                span = range(low + c * CHUNK, low + (c + 1) * CHUNK)
                above_flow = lax.fori_loop(
                    span.start, span.stop, lambda r, f: one_row(r, f, "out"), above_flow, unroll=CHUNK
                )
                here = pl.ds(c * CHUNK, CHUNK)
                for t in range(across):
                    copy = pltpu.make_async_copy(
                        whole.at[t, :, :, here],
                        out_ref.at[:, :, here, pl.ds(t * TILE, TILE)],
                        sems.at[t, c],
                    )
                    copy.start()
                    writes.append(copy)
        else:
            for r in range(low, TV_STEPS):
                above_flow = one_row(r, above_flow, "above")
            above_flow = lax.fori_loop(
                TV_STEPS, TV_STEPS + GROUP_ROWS, lambda r, f: one_row(r, f, ""), above_flow, unroll=8
            )
            for r in range(TV_STEPS + GROUP_ROWS, high):
                above_flow = one_row(r, above_flow, "below")
    for copy in writes:
        copy.wait()


def smooth(p, image):
    slices, height, width = image.shape
    across = width // TILE
    kernel = lambda *refs: smooth_kernel(*refs, slices=slices, across=across)
    return pl.pallas_call(
        kernel,
        out_shape=jax.ShapeDtypeStruct((slices, GROUPS, GROUP_ROWS, width), jnp.float32),
        in_specs=[VMEM],
        out_specs=HBM,
        scratch_shapes=[
            pltpu.VMEM(p.shape, jnp.float32),
            pltpu.VMEM((across, slices * height, TILE), jnp.float32),
            pltpu.SemaphoreType.DMA((across, GROUP_ROWS // CHUNK)),
        ],
        compiler_params=pltpu.CompilerParams(vmem_limit_bytes=40 << 20),
        name="smooth",
    )(p).reshape(image.shape)


def local(current_image, measured, ray_weight, angle_ids, shadow_start):
    measured, weight = measured.reshape(-1, TILE), ray_weight.reshape(-1, TILE)
    made = project(current_image, angle_ids, shadow_start, measured, weight)
    return smooth(update(current_image, *made), current_image)


def solution(mesh):
    return jax.shard_map(
        local,
        mesh=mesh,
        in_specs=(
            P(None, "row", "col"),
            P("col", "row", None, None),
            P("col", "row", None),
            P(),
            P(),
        ),
        out_specs=P(None, "row", "col"),
        check_vma=False,
    )
```

```python
import math

import jax
import jax.numpy as jnp
from jax import lax
from jax.experimental import pallas as pl
from jax.experimental.pallas import tpu as pltpu
from jax.sharding import PartitionSpec as P

TILE = 128
ANGLES = 16
ALL_ANGLES = 256
TV_STEPS = 4
PACK = TILE // TV_STEPS

HIGH = 8
WIDE = 16
BINS = 16
MARGIN = 8
DEPTH = MARGIN + TILE + BINS
GROUPS = 4
GROUP_ROWS = TILE // GROUPS
DOWN = GROUP_ROWS // HIGH
RIGHT = TILE // WIDE
QUAD = 4
CHUNK = 8

inverse_root = 0.7071067811865476
proj_scale = 0.03125
relaxation = 8.0
smoothing = 0.25
descent_step = 0.05

MESH = pl.DeviceIdType.MESH
SMEM = pl.BlockSpec(memory_space=pltpu.SMEM)
VMEM = pl.BlockSpec(memory_space=pltpu.VMEM)
HBM = pl.BlockSpec(memory_space=pltpu.HBM)


def lookup(table, index):
    return jnp.take_along_axis(table, index, axis=1, mode="promise_in_bounds")


def lane_iota():
    return lax.broadcasted_iota(jnp.int32, (8, TILE), 1)


def row_iota():
    return lax.broadcasted_iota(jnp.int32, (8, TILE), 0)


BLOCKS = DOWN * RIGHT
PAIR = 2


def geometry(angle_ref):
    lanes = lane_iota()
    ids = jnp.zeros((8, TILE), jnp.int32)
    for a in range(ANGLES):
        ids = jnp.where(lanes % ANGLES == a, angle_ref[a], ids)
    radians = ids.astype(jnp.float32) * (math.pi / ALL_ANGLES)
    down = jnp.cos(radians) * inverse_root
    right = jnp.sin(radians) * inverse_root
    centre = (TILE - 1) / 2.0
    firsts, offsets = [], []
    for b in range(0, BLOCKS, 8):
        block = row_iota() + b
        row = (block // RIGHT) * HIGH + (lanes // ANGLES % GROUPS) * GROUP_ROWS
        column = (block % RIGHT) * WIDE
        row = row.astype(jnp.float32) - centre
        column = column.astype(jnp.float32) - centre
        place = TILE / 2.0 + (row * down + column * right)
        lowest = place + jnp.minimum(0.0, (HIGH - 1) * down) + jnp.minimum(0.0, (WIDE - 1) * right)
        first = jnp.floor(lowest - 0.5)
        firsts.append(first.astype(jnp.int32) + MARGIN)
        offsets.append(place - first - 0.5)
    return down, right, jnp.concatenate(firsts, axis=0), jnp.concatenate(offsets, axis=0)


def pair_source(slices_here, slices, across):
    lanes = lane_iota()
    owners = slices // slices_here
    s = lanes % slices_here
    a = lanes // slices_here % PAIR
    t = lanes // (slices_here * PAIR) % across
    r = lanes // (slices_here * PAIR * across) % owners
    kind = lanes // (slices_here * PAIR * across * owners)
    return ((kind * PAIR + a) * across + t) * slices + r * slices_here + s


def quad_source(angles_here, slices_here, slices, across):
    lanes = lane_iota()
    slice_ = lanes % slices
    t = lanes // slices % across
    angle = lanes // (slices * across)
    sub, a = angle // angles_here, angle % angles_here
    r, s = slice_ // slices_here, slice_ % slices_here
    owner = sub * (slices // slices_here) + r
    return ((owner * across + t) * angles_here + a) * slices_here + s


def select_rows(values):
    rows = row_iota()
    result = jnp.full((8, TILE), values[0][1], jnp.int32)
    for r in range(1, 8):
        if values[r][0] != values[r - 1][0]:
            result = jnp.where(rows >= r, values[r][1], result)
    return result


def hat(distance):
    return jnp.maximum(1.0 - jnp.abs(distance), 0.0).astype(jnp.bfloat16)


def to_pixels(z_ref, ur, across, slices, mirrored=GROUPS):
    parts = []
    mirror = TILE - 1 - lane_iota()
    for g in range(GROUPS):
        row = ur if g < mirrored else GROUP_ROWS - 1 - ur
        for t in range(across):
            for s in range(0, slices, 8):
                start = s * TILE + g * GROUP_ROWS + row
                part = z_ref[t, pl.ds(start, 8, stride=TILE), :]
                parts.append(part if g < mirrored else lookup(part, mirror))
    pixels = jnp.concatenate(parts, axis=0)
    return pixels.T if mirrored == GROUPS else pixels.astype(jnp.bfloat16).T


def forward_kernel(
    angle_ref, x_ref, starts_ref, measured_ref, weight_ref,
    acc_ref, first_out, table_out, starts_out, measured_out, weight_out, z_ref,
    xb_ref, q_ref, first_ref, offset_ref, sems, read_sems,
    *, slices, across,
):
    half = GROUPS // 2
    slices = x_ref.shape[0]
    whole = z_ref.reshape(across, slices, GROUPS, GROUP_ROWS, TILE)
    chunks = GROUP_ROWS // CHUNK
    copies = []
    for c in range(chunks):
        for t in range(across):
            for h, k in ((0, c), (half, chunks - 1 - c)):
                groups, here = pl.ds(h, half), pl.ds(k * CHUNK, CHUNK)
                copies.append(
                    pltpu.make_async_copy(
                        x_ref.at[:, groups, here, pl.ds(t * TILE, TILE)],
                        whole.at[t, :, groups, here],
                        read_sems.at[c, t, h // half],
                    )
                )
                copies[-1].start()

    passed = [
        pltpu.make_async_copy(starts_ref, starts_out, sems.at[2]),
        pltpu.make_async_copy(measured_ref, measured_out, sems.at[3]),
        pltpu.make_async_copy(weight_ref, weight_out, sems.at[4]),
    ]
    for copy in passed:
        copy.start()
    down, right, first, offset = geometry(angle_ref)
    first_out[...] = first
    table_out[0:BLOCKS] = offset
    table_out[BLOCKS : BLOCKS + 8] = down
    table_out[BLOCKS + 8 :] = right
    scalars = [
        pltpu.make_async_copy(first_out, first_ref, sems.at[5]),
        pltpu.make_async_copy(table_out.at[0:BLOCKS], offset_ref, sems.at[1]),
    ]
    for copy in scalars:
        copy.start()
    pixel = lane_iota()
    pixel_row = (pixel // WIDE).astype(jnp.float32)
    pixel_column = (pixel % WIDE).astype(jnp.float32)
    bins = row_iota().astype(jnp.float32)
    for a in range(ANGLES):
        at = jnp.full((8, TILE), a, jnp.int32)
        place = pixel_row * lookup(down, at) + pixel_column * lookup(right, at)
        for b in range(0, BINS, 8):
            q_ref[a, b : b + 8, :] = place - (bins + b)

    def clear(k, carry):
        acc_ref[k] = jnp.zeros((DEPTH, TILE), jnp.float32)
        return carry

    lax.fori_loop(0, half * ANGLES, clear, jnp.int32(0))

    def turn(ur, carry):
        xb_ref[ur] = to_pixels(z_ref, ur, across, slices, half)
        return carry

    for c in range(chunks):
        for copy in copies[c * 2 * across : (c + 1) * 2 * across]:
            copy.wait()
        lax.fori_loop(c * CHUNK, (c + 1) * CHUNK, turn, jnp.int32(0), unroll=CHUNK)
    for copy in scalars:
        copy.wait()

    def block(i, carry):
        top = (i // RIGHT) * HIGH
        left = pl.multiple_of((i % RIGHT) * WIDE, WIDE)
        pixels = jnp.concatenate(
            [xb_ref[top + k, pl.ds(left, WIDE), :] for k in range(HIGH)], axis=0
        )
        for g in range(half):
            weights = jnp.concatenate(
                [hat(q_ref[a] + offset_ref[i, g * ANGLES + a]) for a in range(ANGLES)], axis=0
            )
            shadow = jnp.dot(weights, pixels, preferred_element_type=jnp.float32)
            spans = [pl.ds(first_ref[i, g * ANGLES + a], BINS) for a in range(ANGLES)]
            olds = [acc_ref[g * ANGLES + a, spans[a], :] for a in range(ANGLES)]
            for a in range(ANGLES):
                acc_ref[g * ANGLES + a, spans[a], :] = (
                    olds[a] + shadow[a * BINS : (a + 1) * BINS]
                )
        return carry

    lax.fori_loop(0, BLOCKS, block, jnp.int32(0), unroll=8)
    for copy in passed:
        copy.wait()


def tile_rows_of(angles_here, slices_here):
    return pl.cdiv(angles_here * slices_here, 8) * 8


def project(image, angle_ids, starts, measured, weight):
    slices, height, width = image.shape
    across = width // TILE
    kernel = lambda *refs: forward_kernel(*refs, slices=slices, across=across)
    return pl.pallas_call(
        kernel,
        out_shape=[
            pltpu.VMEM((GROUPS // 2 * ANGLES, DEPTH, TILE), jnp.float32),
            pltpu.VMEM((BLOCKS, TILE), jnp.int32),
            pltpu.VMEM((BLOCKS + 16, TILE), jnp.float32),
            pltpu.VMEM(starts.shape, starts.dtype),
            pltpu.VMEM(measured.shape, measured.dtype),
            pltpu.VMEM(weight.shape, weight.dtype),
            pltpu.VMEM((across, slices * height, TILE), jnp.float32),
        ],
        in_specs=[SMEM] + [HBM] * 4,
        out_specs=[VMEM] * 7,
        scratch_shapes=[
            pltpu.VMEM((GROUP_ROWS, TILE, TILE), jnp.bfloat16),
            pltpu.VMEM((ANGLES, BINS, TILE), jnp.float32),
            pltpu.SMEM((BLOCKS, TILE), jnp.int32),
            pltpu.SMEM((BLOCKS, TILE), jnp.float32),
            pltpu.SemaphoreType.DMA((6,)),
            pltpu.SemaphoreType.DMA((GROUP_ROWS // CHUNK, across, 2)),
        ],
        compiler_params=pltpu.CompilerParams(vmem_limit_bytes=58 << 20),
        name="project",
    )(
        angle_ids, image.reshape(slices, GROUPS, GROUP_ROWS, width), starts, measured, weight
    )


def ramp_table(n):
    gap = lax.broadcasted_iota(jnp.int32, (TILE, TILE), 1) - n * TILE
    gap = gap - lax.broadcasted_iota(jnp.int32, (TILE, TILE), 0)
    nonzero = jnp.where(gap == 0, 1, gap).astype(jnp.float32)
    value = -1.0 / (math.pi * math.pi * nonzero * nonzero)
    value = jnp.where((gap & 1) == 1, value, 0.0)
    value = jnp.where(gap == 0, 0.25, value)
    return jnp.where(jnp.abs(gap) < TILE, value, 0.0)


EXTRA = 8
SPAN = TILE + 2 * EXTRA
ROWS = GROUP_ROWS + 2 * TV_STEPS


def pack_rows(y_ref, row_edge_ref):
    width = TILE // GROUPS
    group = lane_iota() // width
    for b in range(0, TILE, 16):
        for side in range(2):
            halves = []
            for half in range(2):
                span = slice(EXTRA + b + half * 8, EXTRA + b + half * 8 + 8)
                packed = None
                for i in range(TV_STEPS):
                    row = i if side == 0 else GROUP_ROWS - TV_STEPS + i
                    home = 0 if side == 0 else GROUPS - 1
                    value = pltpu.roll(y_ref[TV_STEPS + row, span, :], (width * (i - home)) % TILE, 1)
                    packed = value if packed is None else jnp.where(group == i, value, packed)
                halves.append(packed)
            row_edge_ref[side, b : b + 16, :] = jnp.concatenate(halves, axis=0).astype(jnp.bfloat16)


def pack_columns(y_ref, col_edge_ref, slices):
    first_tile = lane_iota() % (TILE // GROUPS) < slices
    half_rows = GROUP_ROWS // 2
    for j in range(0, half_rows, 2):
        for side in range(2):
            start = EXTRA if side == 0 else TILE
            span = slice(start, start + 8)
            parts = []
            for k in (j, j + 1):
                near = y_ref[TV_STEPS + k, span, :]
                far = y_ref[TV_STEPS + k + half_rows, span, :]
                if side == 0:
                    far = pltpu.roll(far, slices, 1)
                else:
                    near = pltpu.roll(near, TILE - slices, 1)
                parts.append(jnp.where(first_tile, near, far))
            col_edge_ref[side, j // 2] = jnp.concatenate(parts, axis=0).astype(jnp.bfloat16)


def update_kernel(
    starts_ref, first_ref, acc_ref, measured_ref, weight_ref, table_ref, x_ref, p_ref,
    sent_ref, scan_out, wide_ref, ramp_ref, landed, scan, target_ref, outgoing, returned, store_ref, q_ref,
    row_edge, col_edge, row_halo, col_halo, corner,
    shadow_sems, scan_sems, window_sems, edge_sems,
    *, slices, angles_here, slices_here, across, tile_rows,
):
    rows = lax.axis_size("row")
    cols = lax.axis_size("col")
    row = lax.axis_index("row")
    col = lax.axis_index("col")
    count = rows * cols
    me = row * cols + col

    def send(src, dst, sems, k, to_row, to_col):
        return pltpu.make_async_remote_copy(
            src_ref=src, dst_ref=dst, send_sem=sems.at[0, k], recv_sem=sems.at[1, k],
            device_id=(to_row, to_col), device_id_type=MESH,
        )

    width = TILE // GROUPS
    lanes = lane_iota()
    group = lanes // width
    first_tile = lanes % width < slices
    order = quad_source(angles_here, slices_here, slices, across)
    per_tile = angles_here * slices_here
    owners = slices // slices_here
    low, high = pl.ds(0, 16), pl.ds(TILE - 16, 16)
    routes = (
        (-1, 0, row_edge.at[0], row_halo.at[1]),
        (1, 0, row_edge.at[1], row_halo.at[0]),
        (0, -1, col_edge.at[0], col_halo.at[1]),
        (0, 1, col_edge.at[1], col_halo.at[0]),
        (-1, -1, row_edge.at[0, low], corner.at[1, 1]),
        (-1, 1, row_edge.at[0, high], corner.at[1, 0]),
        (1, -1, row_edge.at[1, low], corner.at[0, 1]),
        (1, 1, row_edge.at[1, high], corner.at[0, 0]),
    )

    def exists(down, right):
        to_row, to_col = row + down, col + right
        return (to_row >= 0) & (to_row < rows) & (to_col >= 0) & (to_col < cols)

    for r in range(rows):
        for a in range(angles_here):
            to = a * slices_here
            scan_out[r, to : to + slices_here] = measured_ref[
                a * slices + r * slices_here : a * slices + (r + 1) * slices_here
            ]
            scan_out[r, tile_rows + to : tile_rows + to + slices_here] = jnp.broadcast_to(
                weight_ref[a : a + 1], (slices_here, TILE)
            )
        if tile_rows > per_tile:
            spare = jnp.zeros((tile_rows - per_tile, TILE), jnp.float32)
            scan_out[r, per_tile:tile_rows] = spare
            scan_out[r, tile_rows + per_tile :] = spare
    row_halo[...] = jnp.zeros(row_halo.shape, row_halo.dtype)
    col_halo[...] = jnp.zeros(col_halo.shape, col_halo.dtype)
    corner[...] = jnp.zeros(corner.shape, corner.dtype)
    barrier = pltpu.get_barrier_semaphore()

    def peer(down, right):
        to_row, to_col = row + down, col + right
        to_row = jnp.where(to_row >= rows, to_row - rows, to_row)
        return to_row, jnp.where(to_col >= cols, to_col - cols, to_col)

    def all_peers(body, first=0):
        def some(j, carry):
            down = lax.rem(j + first, rows)

            @pl.when(down > 0)
            def _():
                body(down, 0)

            for right in range(1, cols):
                body(down, right)
            return carry

        lax.fori_loop(0, rows, some, jnp.int32(0))

    def greet(down, right):
        pl.semaphore_signal(barrier, inc=1, device_id=peer(down, right), device_id_type=MESH)

    all_peers(greet, rows // 2)

    near = pair_source(slices_here, slices, across)
    far = near ^ width
    piece = PAIR * slices_here
    kind_rows = TILE // 2

    def pick(span, values):
        result = acc_ref[values[0], span, :]
        for g in range(1, GROUPS):
            result = jnp.where(group == g, acc_ref[values[g], span, :], result)
        return result

    def pair_shadows(pair):
        here, there = pair * PAIR, pair * PAIR + 1
        pieces = []
        for b in range(TILE // 8):
            span = slice(MARGIN + b * 8, MARGIN + b * 8 + 8)
            own = pick(span, (here, ANGLES + there, ANGLES + here, there))
            other = pick(span, (there, ANGLES + here, ANGLES + there, here))
            pieces.append(lookup(own, near) + lookup(other, far))
        rows = jnp.concatenate(pieces, axis=0).T
        sent = []
        for e in range(kind_rows // 8):
            keys = []
            for r in range(e * 8, e * 8 + 8):
                a = r // slices_here % PAIR
                t = r // (slices_here * PAIR) % across
                start = starts_ref[row, col * across + t, pair * PAIR + a]
                keys.append(((a, t), start))
            index = (lanes - select_rows(keys)) & (TILE - 1)
            value = lookup(rows[e * 8 : e * 8 + 8], index) + lookup(
                rows[kind_rows + e * 8 : kind_rows + e * 8 + 8], TILE - 1 - index
            )
            sent.append(value * proj_scale)
        return jnp.concatenate(sent, axis=0)

    for owner in range(cols):
        pairs = angles_here // PAIR
        shadows = [pair_shadows(owner * pairs + p) for p in range(pairs)]
        for r in range(owners):
            parts = []
            for t in range(across):
                at = (r * across + t) * piece
                parts += [shadow[at : at + piece] for shadow in shadows]
                if tile_rows > per_tile:
                    parts.append(jnp.zeros((tile_rows - per_tile, TILE), jnp.float32))
            message = jnp.concatenate(parts, axis=0)
            sent_ref[r * cols + owner] = message.astype(jnp.bfloat16)

    pl.semaphore_wait(barrier, count - 1)

    def shadow_copy(down, right):
        k = down * cols + right
        to_row, to_col = peer(down, right)
        src = sent_ref.at[to_row * cols + to_col]
        return send(src, landed.at[k], shadow_sems, k, to_row, to_col)

    def scan_copy(down):
        to_row, to_col = peer(down, 0)
        return send(scan_out.at[to_row], scan.at[down], scan_sems, down, to_row, to_col)

    all_peers(lambda down, right: shadow_copy(down, right).start(), rows // 2)
    for down in range(1, rows):
        scan_copy(down).start()
    landed[0] = sent_ref[me]
    scan[0] = scan_out[row]

    sublanes = row_iota()

    def aim(down, carry):
        for right in range(cols):
            to_row, to_col = peer(down, right)
            for t in range(across):
                start = jnp.full(
                    (8, TILE), starts_ref[to_row, to_col * across + t, col * angles_here], jnp.int32
                )
                for a in range(1, angles_here):
                    value = starts_ref[to_row, to_col * across + t, col * angles_here + a]
                    start = jnp.where(sublanes >= a * slices_here, value, start)
                block = (start >> 7) + jnp.where(lanes < (start & (TILE - 1)), 1, 0)
                target_ref[down, right, t] = block
        return carry

    lax.fori_loop(0, rows, aim, jnp.int32(0))

    for k in range(GROUPS * ANGLES):
        store_ref[k, 0:MARGIN, :] = jnp.zeros((MARGIN, TILE), jnp.float32)
        store_ref[k, MARGIN + TILE :, :] = jnp.zeros((DEPTH - MARGIN - TILE, TILE), jnp.float32)
    for n in (-1, 0, 1):
        taps = ramp_table(n)
        coarse = taps.astype(jnp.bfloat16)
        ramp_ref[0, (n + 1) * TILE : (n + 2) * TILE] = coarse
        ramp_ref[1, (n + 1) * TILE : (n + 2) * TILE] = (
            taps - coarse.astype(jnp.float32)
        ).astype(jnp.bfloat16)

    def add(down, right, sums):
        message = landed[down * cols + right].astype(jnp.float32)
        back = lax.rem(rows - down, rows)
        for t in range(across):
            value = message[t * tile_rows : (t + 1) * tile_rows]
            target = target_ref[back, (cols - right) % cols, t]
            sums = tuple(
                total + jnp.where(target == b, value, 0.0) for b, total in enumerate(sums)
            )
        return sums

    zero = jnp.zeros((tile_rows, TILE), jnp.float32)
    sums = add(0, 0, (zero,) * rows)
    for right in range(1, cols):
        shadow_copy(0, right).wait_recv()
        sums = add(0, right, sums)

    def add_row(down, sums):
        for right in range(cols):
            shadow_copy(down, right).wait_recv()
        for right in range(cols):
            sums = add(down, right, sums)
        return sums

    sums = lax.fori_loop(1, rows, add_row, sums)
    for down in range(1, rows):
        scan_copy(down).wait_recv()
    residual = []
    for b in range(rows):
        here = scan[lax.rem(row - b + rows, rows)]
        residual.append(here[tile_rows:] * (here[:tile_rows] - sums[b]))
    stacked = jnp.concatenate(
        [
            jnp.concatenate([zero] + residual[:-1], axis=0),
            jnp.concatenate(residual, axis=0),
            jnp.concatenate(residual[1:] + [zero], axis=0),
        ],
        axis=1,
    )
    coarse = stacked.astype(jnp.bfloat16)
    fine = (stacked - coarse.astype(jnp.float32)).astype(jnp.bfloat16)
    both = jnp.dot(
        jnp.concatenate([coarse, fine], axis=0), ramp_ref[0], preferred_element_type=jnp.float32
    )
    filtered = both[: rows * tile_rows] + (
        both[rows * tile_rows :]
        + jnp.dot(coarse, ramp_ref[1], preferred_element_type=jnp.float32)
    )
    blocks = tuple(filtered[b * tile_rows : (b + 1) * tile_rows] for b in range(rows))

    def window(down, right):
        parts = []
        for t in range(across):
            target = target_ref[down, right, t]
            value = zero
            for b in range(rows):
                value = jnp.where(target == b, blocks[b], value)
            parts.append(value)
        return jnp.concatenate(parts, axis=0).astype(jnp.bfloat16)

    def window_copy(down, right):
        k = down * cols + right
        return send(outgoing.at[k], returned.at[me], window_sems, k, *peer(down, right))

    def reply(j, carry):
        down = lax.rem(j + rows // 2, rows)
        for right in range(cols):
            outgoing[down * cols + right] = window(down, right)
        pl.when(down > 0)(window_copy(down, 0).start)
        for right in range(1, cols):
            window_copy(down, right).start()
        return carry

    lax.fori_loop(0, rows, reply, jnp.int32(0), unroll=2)
    returned[me] = outgoing[0]

    pixel = row_iota()
    bins = (lanes % BINS).astype(jnp.float32)
    down = table_ref[BLOCKS : BLOCKS + 8]
    right = table_ref[BLOCKS + 8 :]
    for h in range(ANGLES * BINS // TILE):
        at = lanes // BINS + h * (TILE // BINS)
        down_here, right_here = lookup(down, at), lookup(right, at)
        span = slice(h * TILE, (h + 1) * TILE)
        for b in range(0, TILE, 8):
            pixel_row = ((pixel + b) // WIDE).astype(jnp.float32)
            pixel_column = ((pixel + b) % WIDE).astype(jnp.float32)
            q_ref[b : b + 8, span] = pixel_row * down_here + pixel_column * right_here - bins
        for g in range(GROUPS):
            for b in range(0, BLOCKS, 8):
                wide_ref[g, b : b + 8, span] = lookup(table_ref[b : b + 8], at + g * ANGLES)

    def turn(ur, carry):
        p_ref[TV_STEPS + ur, EXTRA : EXTRA + TILE, :] = to_pixels(x_ref, ur, across, slices) * (
            1.0 / descent_step
        )
        return carry

    lax.fori_loop(0, GROUP_ROWS, turn, jnp.int32(0), unroll=2)

    for quad in range(ANGLES // QUAD):
        parts = []
        for sub in range(QUAD // angles_here):
            at = quad * (QUAD // angles_here) + sub
            right = lax.rem(col - at + cols, cols)

            def arrived(down, carry, right=right):
                pl.when((down > 0) | (right > 0))(window_copy(down, right).wait_recv)
                return carry

            lax.fori_loop(0, rows, arrived, jnp.int32(0))
            for r in range(owners):
                message = returned[r * cols + at].astype(jnp.float32)
                for t in range(across):
                    parts.append(message[t * tile_rows : t * tile_rows + per_tile])
        flat = jnp.concatenate(parts, axis=0)
        turned = []
        for e in range(TILE // 8):
            keys = []
            for r in range(e * 8, e * 8 + 8):
                a = r // slices_here % angles_here
                t = r // (slices_here * angles_here) % across
                a = a + r // (slices_here * angles_here * across * owners) * angles_here
                start = starts_ref[row, col * across + t, quad * QUAD + a]
                keys.append(((a, t), start))
            shift = select_rows(keys)
            turned.append(lookup(flat[e * 8 : e * 8 + 8], (lanes + shift) & (TILE - 1)))
        bins_first = jnp.concatenate(turned, axis=0).T
        for b in range(TILE // 8):
            span = slice(MARGIN + b * 8, MARGIN + b * 8 + 8)
            value = lookup(bins_first[b * 8 : b * 8 + 8], order)
            for k in range(GROUPS):
                moved = pltpu.roll(value, width * k, 1) if k else value
                for a in range(QUAD):
                    g = (a + k) % GROUPS
                    store_ref[g * ANGLES + quad * QUAD + a, span, :] = jnp.where(
                        group == g, moved, 0.0
                    )

    def block(urb, vb):
        i = urb * RIGHT + vb
        top = urb * HIGH + TV_STEPS
        left = pl.multiple_of(vb * WIDE, WIDE) + EXTRA
        total = None
        for g in range(GROUPS):
            shadows = jnp.concatenate(
                [
                    store_ref[g * ANGLES + a, pl.ds(first_ref[i, g * ANGLES + a], BINS), :]
                    for a in range(ANGLES)
                ],
                axis=0,
            ).astype(jnp.bfloat16)
            weights = hat(q_ref[...] + wide_ref[g, pl.ds(i, 1), :])
            part = jnp.dot(weights, shadows, preferred_element_type=jnp.float32)
            total = part if total is None else total + part
        total = total * (relaxation * proj_scale / descent_step)
        for k in range(HIGH):
            p_ref[top + k, pl.ds(left, WIDE), :] = (
                p_ref[top + k, pl.ds(left, WIDE), :] + total[k * WIDE : (k + 1) * WIDE]
            )

    def outer_rows(i, carry):
        block((i // RIGHT) * (DOWN - 1), i % RIGHT)
        return carry

    def outer_columns(i, carry):
        block(1 + i // 2, (i % 2) * (RIGHT - 1))
        return carry

    def inner_blocks(i, carry):
        block(1 + i // (RIGHT - 2), 1 + i % (RIGHT - 2))
        return carry

    copies = []
    for k, (down, right, src, dst) in enumerate(routes):
        copy = pltpu.make_async_remote_copy(
            src_ref=src,
            dst_ref=dst,
            send_sem=edge_sems.at[0, k],
            recv_sem=edge_sems.at[1, k],
            device_id=(row + down, col + right),
            device_id_type=MESH,
        )
        copies.append((down, right, copy))
    lax.fori_loop(0, 2 * RIGHT, outer_rows, jnp.int32(0), unroll=8)
    pack_rows(p_ref, row_edge)
    for down, right, copy in copies:
        if down:
            pl.when(exists(down, right))(copy.start)
    lax.fori_loop(0, 2 * (DOWN - 2), outer_columns, jnp.int32(0), unroll=4)
    pack_columns(p_ref, col_edge, slices)
    for down, right, copy in copies:
        if not down:
            pl.when(exists(down, right))(copy.start)
    lax.fori_loop(0, (DOWN - 2) * (RIGHT - 2), inner_blocks, jnp.int32(0), unroll=6)
    for down, right, copy in copies:
        pl.when(exists(-down, -right))(copy.wait_recv)

    inner = slice(EXTRA, EXTRA + TILE)
    half_rows = GROUP_ROWS // 2

    def shift(value, by):
        by = by % TILE
        return pltpu.roll(value, by, 1) if by else value

    for i in range(TV_STEPS):
        for b in range(0, TILE, 16):
            above = row_halo[0, b : b + 16, :].astype(jnp.float32)
            below = row_halo[1, b : b + 16, :].astype(jnp.float32)
            for half in range(2):
                to = slice(EXTRA + b + half * 8, EXTRA + b + half * 8 + 8)
                piece = slice(half * 8, half * 8 + 8)
                p_ref[i, to, :] = jnp.where(
                    group == 0,
                    shift(above[piece], -width * i),
                    shift(p_ref[GROUP_ROWS + i, to, :], width),
                )
                p_ref[TV_STEPS + GROUP_ROWS + i, to, :] = jnp.where(
                    group == GROUPS - 1,
                    shift(below[piece], width * (GROUPS - 1 - i)),
                    shift(p_ref[TV_STEPS + i, to, :], -width),
                )

    left, right = [], []
    for j in range(half_rows):
        piece = slice((j % 2) * 8, (j % 2) * 8 + 8)
        left.append(col_halo[0, j // 2].astype(jnp.float32)[piece])
        right.append(col_halo[1, j // 2].astype(jnp.float32)[piece])

    def from_left(ur):
        return left[ur] if ur < half_rows else shift(left[ur - half_rows], -slices)

    def from_right(ur):
        return shift(right[ur], slices) if ur < half_rows else right[ur - half_rows]

    def corner_of(down, side):
        value = corner[down, side].astype(jnp.float32)
        return value[8:16] if side == 0 else value[0:8]

    for r in range(ROWS):
        ur = r - TV_STEPS
        if ur < 0:
            outer = [from_left(GROUP_ROWS + ur), from_right(GROUP_ROWS + ur)]
            edge = [
                shift(corner_of(0, 0), -width * r - slices),
                shift(corner_of(0, 1), -width * r + slices),
            ]
            outer = [jnp.where(group == 0, e, shift(o, width)) for e, o in zip(edge, outer)]
        elif ur >= GROUP_ROWS:
            i = ur - GROUP_ROWS
            outer = [from_left(i), from_right(i)]
            edge = [
                shift(corner_of(1, 0), width * (GROUPS - 1 - i) - slices),
                shift(corner_of(1, 1), width * (GROUPS - 1 - i) + slices),
            ]
            outer = [jnp.where(group == GROUPS - 1, e, shift(o, -width)) for e, o in zip(edge, outer)]
        else:
            outer = [from_left(ur), from_right(ur)]
        p_ref[r, 0:EXTRA, :] = jnp.where(
            first_tile, outer[0], shift(p_ref[r, TILE : TILE + EXTRA, :], slices)
        )
        p_ref[r, EXTRA + TILE :, :] = jnp.where(
            first_tile, shift(p_ref[r, EXTRA : 2 * EXTRA, :], -slices), outer[1]
        )

    for down, right, copy in copies:
        pl.when(exists(down, right))(copy.wait_send)
    def settle(down, right):
        shadow_copy(down, right).wait_send()
        window_copy(down, right).wait_send()

    all_peers(settle)
    for down in range(1, rows):
        scan_copy(down).wait_send()


def update(image, shadows, first, table, starts, measured, weight, x):
    rows = lax.axis_size("row")
    cols = lax.axis_size("col")
    slices, height, width = image.shape
    angles_here = ANGLES // cols
    slices_here = slices // rows
    tile_rows = tile_rows_of(angles_here, slices_here)
    count = rows * cols
    across = width // TILE
    message = pltpu.VMEM((count, across * tile_rows, TILE), jnp.bfloat16)
    kernel = lambda *refs: update_kernel(
        *refs, slices=slices, angles_here=angles_here, slices_here=slices_here,
        across=across, tile_rows=tile_rows,
    )
    dma = pltpu.SemaphoreType.DMA
    row_edge = pltpu.VMEM((2, TILE, TILE), jnp.bfloat16)
    col_edge = pltpu.VMEM((2, GROUP_ROWS // 4, 16, TILE), jnp.bfloat16)
    return pl.pallas_call(
        kernel,
        out_shape=pltpu.VMEM((ROWS, SPAN, TILE), jnp.float32),
        in_specs=[SMEM] * 2 + [VMEM] * 5,
        out_specs=VMEM,
        scratch_shapes=[
            message,
            pltpu.VMEM((rows, 2 * tile_rows, TILE), jnp.float32),
            pltpu.VMEM((GROUPS, BLOCKS, ANGLES * BINS), jnp.float32),
            pltpu.VMEM((2, 3 * TILE, TILE), jnp.bfloat16),
            message,
            pltpu.VMEM((rows, 2 * tile_rows, TILE), jnp.float32),
            pltpu.VMEM((rows, cols, across, tile_rows, TILE), jnp.int32),
            message,
            message,
            pltpu.VMEM((GROUPS * ANGLES, DEPTH, TILE), jnp.float32),
            pltpu.VMEM((TILE, ANGLES * BINS), jnp.float32),
            row_edge, col_edge, row_edge, col_edge,
            pltpu.VMEM((2, 2, 16, TILE), jnp.bfloat16),
            dma((2, count)),
            dma((2, rows)),
            dma((2, count)),
            dma((2, 8)),
        ],
        compiler_params=pltpu.CompilerParams(
            collective_id=0, has_side_effects=True, vmem_limit_bytes=40 << 20
        ),
        name="update",
    )(
        starts, first, shadows, measured, weight, table, x,
    )


def smooth_kernel(p_ref, out_ref, held_ref, z_ref, sems, *, slices, across):
    row = lax.axis_index("row")
    col = lax.axis_index("col")
    rows = lax.axis_size("row")
    cols = lax.axis_size("col")
    group = lane_iota() // (TILE // GROUPS)
    first_tile = lane_iota() % (TILE // GROUPS) < slices
    whole = z_ref.reshape(across, slices, GROUPS, GROUP_ROWS, TILE)
    writes = []
    one, nought = jnp.ones((8, TILE), jnp.float32), jnp.zeros((8, TILE), jnp.float32)

    def there(near, outside):
        return jnp.where(outside, jnp.where(near, one, nought), one)

    keep_above = there(row > 0, group == 0)[0:1]
    keep_below = there(row < rows - 1, group == GROUPS - 1)[0:1]
    keep_left = there(col > 0, first_tile)
    keep_right = there(col < cols - 1, jnp.logical_not(first_tile))

    limit = (smoothing / descent_step) ** 2
    columns = SPAN // 8
    sublanes = row_iota()
    last, head = sublanes == 7, sublanes == 0

    def sweep(source, r, above, emit, end):
        def at(r, j):
            return source[r, j * 8 : j * 8 + 8, :]

        below = []
        here, turned, left = at(r, 0), pltpu.roll(at(r, 0), 7, 0), None
        for j in range(end):
            k = min(j + 1, columns - 1)
            ahead = at(r, k)
            ahead_turned = pltpu.roll(ahead, 7, 0)
            down = at(r + 1, j) - here
            right = jnp.where(last, ahead_turned, turned) - here
            scale = lax.rsqrt(limit + (down * down + right * right))
            down, right = down * scale, right * scale
            if emit is not None:
                moved = pltpu.roll(right, 1, 0)
                before = moved if left is None else jnp.where(head, left, moved)
                emit(j, (here - above[j]) + (down - before) + right)
                left = moved
            below.append(down)
            here, turned = ahead, ahead_turned
        return tuple(below)

    for step in range(TV_STEPS):
        low, high = step + 1, ROWS - 1 - step
        source = p_ref if step == 0 else held_ref
        end = columns - 1 if step == TV_STEPS - 1 else columns
        above_flow = sweep(source, step, None, None, end)

        def one_row(r, above_flow, place, source=source, end=end):
            values = []

            def emit(j, value):
                if place == "out":
                    values.append(value)
                    return
                if j == 0:
                    value = value * keep_left
                if j == columns - 1:
                    value = value * keep_right
                if place == "above":
                    value = value * keep_above
                if place == "below":
                    value = value * keep_below
                held_ref[r, j * 8 : j * 8 + 8, :] = value

            below_flow = sweep(source, r, above_flow, emit, end)
            if place == "out":
                kept = jnp.concatenate(values[EXTRA // 8 :], axis=0) * descent_step
                flipped = kept.T
                for g in range(GROUPS):
                    for t in range(across):
                        for s in range(0, slices, 8):
                            lane = (g * across + t) * slices + s
                            start = s * TILE + g * GROUP_ROWS + r - TV_STEPS
                            z_ref[t, pl.ds(start, 8, stride=TILE), :] = flipped[lane : lane + 8]
            return below_flow

        if step == TV_STEPS - 1:
            for c in range(GROUP_ROWS // CHUNK):
                span = range(low + c * CHUNK, low + (c + 1) * CHUNK)
                above_flow = lax.fori_loop(
                    span.start, span.stop, lambda r, f: one_row(r, f, "out"), above_flow, unroll=CHUNK
                )
                here = pl.ds(c * CHUNK, CHUNK)
                for t in range(across):
                    copy = pltpu.make_async_copy(
                        whole.at[t, :, :, here],
                        out_ref.at[:, :, here, pl.ds(t * TILE, TILE)],
                        sems.at[t, c],
                    )
                    copy.start()
                    writes.append(copy)
        else:
            for r in range(low, TV_STEPS):
                above_flow = one_row(r, above_flow, "above")
            above_flow = lax.fori_loop(
                TV_STEPS, TV_STEPS + GROUP_ROWS, lambda r, f: one_row(r, f, ""), above_flow, unroll=8
            )
            for r in range(TV_STEPS + GROUP_ROWS, high):
                above_flow = one_row(r, above_flow, "below")
    for copy in writes:
        copy.wait()


def smooth(p, image):
    slices, height, width = image.shape
    across = width // TILE
    kernel = lambda *refs: smooth_kernel(*refs, slices=slices, across=across)
    return pl.pallas_call(
        kernel,
        out_shape=jax.ShapeDtypeStruct((slices, GROUPS, GROUP_ROWS, width), jnp.float32),
        in_specs=[VMEM],
        out_specs=HBM,
        scratch_shapes=[
            pltpu.VMEM(p.shape, jnp.float32),
            pltpu.VMEM((across, slices * height, TILE), jnp.float32),
            pltpu.SemaphoreType.DMA((across, GROUP_ROWS // CHUNK)),
        ],
        compiler_params=pltpu.CompilerParams(vmem_limit_bytes=40 << 20),
        name="smooth",
    )(p).reshape(image.shape)


def local(current_image, measured, ray_weight, angle_ids, shadow_start):
    measured, weight = measured.reshape(-1, TILE), ray_weight.reshape(-1, TILE)
    made = project(current_image, angle_ids, shadow_start, measured, weight)
    return smooth(update(current_image, *made), current_image)


def solution(mesh):
    return jax.shard_map(
        local,
        mesh=mesh,
        in_specs=(
            P(None, "row", "col"),
            P("col", "row", None, None),
            P("col", "row", None),
            P(),
            P(),
        ),
        out_specs=P(None, "row", "col"),
        check_vma=False,
    )
```

```python
import math

import jax
import jax.numpy as jnp
from jax import lax
from jax.experimental import pallas as pl
from jax.experimental.pallas import tpu as pltpu
from jax.sharding import PartitionSpec as P

TILE = 128
ANGLES = 16
ALL_ANGLES = 256
TV_STEPS = 4
PACK = TILE // TV_STEPS

HIGH = 8
WIDE = 16
BINS = 16
MARGIN = 8
DEPTH = MARGIN + TILE + BINS
GROUPS = 4
GROUP_ROWS = TILE // GROUPS
DOWN = GROUP_ROWS // HIGH
RIGHT = TILE // WIDE
QUAD = 4
CHUNK = 8

inverse_root = 0.7071067811865476
proj_scale = 0.03125
relaxation = 8.0
smoothing = 0.25
descent_step = 0.05

MESH = pl.DeviceIdType.MESH
SMEM = pl.BlockSpec(memory_space=pltpu.SMEM)
VMEM = pl.BlockSpec(memory_space=pltpu.VMEM)
HBM = pl.BlockSpec(memory_space=pltpu.HBM)


def lookup(table, index):
    return jnp.take_along_axis(table, index, axis=1, mode="promise_in_bounds")


def lane_iota():
    return lax.broadcasted_iota(jnp.int32, (8, TILE), 1)


def row_iota():
    return lax.broadcasted_iota(jnp.int32, (8, TILE), 0)


BLOCKS = DOWN * RIGHT
PAIR = 2


def geometry(angle_ref):
    lanes = lane_iota()
    ids = jnp.zeros((8, TILE), jnp.int32)
    for a in range(ANGLES):
        ids = jnp.where(lanes % ANGLES == a, angle_ref[a], ids)
    radians = ids.astype(jnp.float32) * (math.pi / ALL_ANGLES)
    down = jnp.cos(radians) * inverse_root
    right = jnp.sin(radians) * inverse_root
    centre = (TILE - 1) / 2.0
    firsts, offsets = [], []
    for b in range(0, BLOCKS, 8):
        block = row_iota() + b
        row = (block // RIGHT) * HIGH + (lanes // ANGLES % GROUPS) * GROUP_ROWS
        column = (block % RIGHT) * WIDE
        row = row.astype(jnp.float32) - centre
        column = column.astype(jnp.float32) - centre
        place = TILE / 2.0 + (row * down + column * right)
        lowest = place + jnp.minimum(0.0, (HIGH - 1) * down) + jnp.minimum(0.0, (WIDE - 1) * right)
        first = jnp.floor(lowest - 0.5)
        firsts.append(first.astype(jnp.int32) + MARGIN)
        offsets.append(place - first - 0.5)
    return down, right, jnp.concatenate(firsts, axis=0), jnp.concatenate(offsets, axis=0)


def pair_source(slices_here, slices, across):
    lanes = lane_iota()
    owners = slices // slices_here
    s = lanes % slices_here
    a = lanes // slices_here % PAIR
    t = lanes // (slices_here * PAIR) % across
    r = lanes // (slices_here * PAIR * across) % owners
    kind = lanes // (slices_here * PAIR * across * owners)
    return ((kind * PAIR + a) * across + t) * slices + r * slices_here + s


def quad_source(angles_here, slices_here, slices, across):
    lanes = lane_iota()
    slice_ = lanes % slices
    t = lanes // slices % across
    angle = lanes // (slices * across)
    sub, a = angle // angles_here, angle % angles_here
    r, s = slice_ // slices_here, slice_ % slices_here
    owner = sub * (slices // slices_here) + r
    return ((owner * across + t) * angles_here + a) * slices_here + s


def select_rows(values):
    rows = row_iota()
    result = jnp.full((8, TILE), values[0][1], jnp.int32)
    for r in range(1, 8):
        if values[r][0] != values[r - 1][0]:
            result = jnp.where(rows >= r, values[r][1], result)
    return result


def hat(distance):
    return jnp.maximum(1.0 - jnp.abs(distance), 0.0).astype(jnp.bfloat16)


def to_pixels(z_ref, ur, across, slices, mirrored=GROUPS):
    parts = []
    mirror = TILE - 1 - lane_iota()
    for g in range(GROUPS):
        row = ur if g < mirrored else GROUP_ROWS - 1 - ur
        for t in range(across):
            for s in range(0, slices, 8):
                start = s * TILE + g * GROUP_ROWS + row
                part = z_ref[t, pl.ds(start, 8, stride=TILE), :]
                parts.append(part if g < mirrored else lookup(part, mirror))
    pixels = jnp.concatenate(parts, axis=0)
    return pixels.T if mirrored == GROUPS else pixels.astype(jnp.bfloat16).T


def forward_kernel(
    angle_ref, x_ref, starts_ref, measured_ref, weight_ref,
    acc_ref, first_out, table_out, starts_out, measured_out, weight_out, z_ref,
    xb_ref, q_ref, first_ref, offset_ref, sems, read_sems,
    *, slices, across,
):
    half = GROUPS // 2
    slices = x_ref.shape[0]
    whole = z_ref.reshape(across, slices, GROUPS, GROUP_ROWS, TILE)
    chunks = GROUP_ROWS // CHUNK
    copies = []
    for c in range(chunks):
        for t in range(across):
            for h, k in ((0, c), (half, chunks - 1 - c)):
                groups, here = pl.ds(h, half), pl.ds(k * CHUNK, CHUNK)
                copies.append(
                    pltpu.make_async_copy(
                        x_ref.at[:, groups, here, pl.ds(t * TILE, TILE)],
                        whole.at[t, :, groups, here],
                        read_sems.at[c, t, h // half],
                    )
                )
                copies[-1].start()

    passed = [
        pltpu.make_async_copy(starts_ref, starts_out, sems.at[2]),
        pltpu.make_async_copy(measured_ref, measured_out, sems.at[3]),
        pltpu.make_async_copy(weight_ref, weight_out, sems.at[4]),
    ]
    for copy in passed:
        copy.start()
    down, right, first, offset = geometry(angle_ref)
    first_out[...] = first
    table_out[0:BLOCKS] = offset
    table_out[BLOCKS : BLOCKS + 8] = down
    table_out[BLOCKS + 8 :] = right
    scalars = [
        pltpu.make_async_copy(first_out, first_ref, sems.at[5]),
        pltpu.make_async_copy(table_out.at[0:BLOCKS], offset_ref, sems.at[1]),
    ]
    for copy in scalars:
        copy.start()
    pixel = lane_iota()
    pixel_row = (pixel // WIDE).astype(jnp.float32)
    pixel_column = (pixel % WIDE).astype(jnp.float32)
    bins = row_iota().astype(jnp.float32)
    for a in range(ANGLES):
        at = jnp.full((8, TILE), a, jnp.int32)
        place = pixel_row * lookup(down, at) + pixel_column * lookup(right, at)
        for b in range(0, BINS, 8):
            q_ref[a, b : b + 8, :] = place - (bins + b)

    def clear(k, carry):
        acc_ref[k] = jnp.zeros((DEPTH, TILE), jnp.float32)
        return carry

    lax.fori_loop(0, half * ANGLES, clear, jnp.int32(0))

    def turn(ur, carry):
        xb_ref[ur] = to_pixels(z_ref, ur, across, slices, half)
        return carry

    for c in range(chunks):
        for copy in copies[c * 2 * across : (c + 1) * 2 * across]:
            copy.wait()
        lax.fori_loop(c * CHUNK, (c + 1) * CHUNK, turn, jnp.int32(0), unroll=CHUNK)
    for copy in scalars:
        copy.wait()

    def block(i, carry):
        top = (i // RIGHT) * HIGH
        left = pl.multiple_of((i % RIGHT) * WIDE, WIDE)
        pixels = jnp.concatenate(
            [xb_ref[top + k, pl.ds(left, WIDE), :] for k in range(HIGH)], axis=0
        )
        for g in range(half):
            weights = jnp.concatenate(
                [hat(q_ref[a] + offset_ref[i, g * ANGLES + a]) for a in range(ANGLES)], axis=0
            )
            shadow = jnp.dot(weights, pixels, preferred_element_type=jnp.float32)
            spans = [pl.ds(first_ref[i, g * ANGLES + a], BINS) for a in range(ANGLES)]
            olds = [acc_ref[g * ANGLES + a, spans[a], :] for a in range(ANGLES)]
            for a in range(ANGLES):
                acc_ref[g * ANGLES + a, spans[a], :] = (
                    olds[a] + shadow[a * BINS : (a + 1) * BINS]
                )
        return carry

    lax.fori_loop(0, BLOCKS, block, jnp.int32(0), unroll=8)
    for copy in passed:
        copy.wait()


def tile_rows_of(angles_here, slices_here):
    return pl.cdiv(angles_here * slices_here, 8) * 8


def project(image, angle_ids, starts, measured, weight):
    slices, height, width = image.shape
    across = width // TILE
    kernel = lambda *refs: forward_kernel(*refs, slices=slices, across=across)
    return pl.pallas_call(
        kernel,
        out_shape=[
            pltpu.VMEM((GROUPS // 2 * ANGLES, DEPTH, TILE), jnp.float32),
            pltpu.VMEM((BLOCKS, TILE), jnp.int32),
            pltpu.VMEM((BLOCKS + 16, TILE), jnp.float32),
            pltpu.VMEM(starts.shape, starts.dtype),
            pltpu.VMEM(measured.shape, measured.dtype),
            pltpu.VMEM(weight.shape, weight.dtype),
            pltpu.VMEM((across, slices * height, TILE), jnp.float32),
        ],
        in_specs=[SMEM] + [HBM] * 4,
        out_specs=[VMEM] * 7,
        scratch_shapes=[
            pltpu.VMEM((GROUP_ROWS, TILE, TILE), jnp.bfloat16),
            pltpu.VMEM((ANGLES, BINS, TILE), jnp.float32),
            pltpu.SMEM((BLOCKS, TILE), jnp.int32),
            pltpu.SMEM((BLOCKS, TILE), jnp.float32),
            pltpu.SemaphoreType.DMA((6,)),
            pltpu.SemaphoreType.DMA((GROUP_ROWS // CHUNK, across, 2)),
        ],
        compiler_params=pltpu.CompilerParams(vmem_limit_bytes=58 << 20),
        name="project",
    )(
        angle_ids, image.reshape(slices, GROUPS, GROUP_ROWS, width), starts, measured, weight
    )


def ramp_table(n):
    gap = lax.broadcasted_iota(jnp.int32, (TILE, TILE), 1) - n * TILE
    gap = gap - lax.broadcasted_iota(jnp.int32, (TILE, TILE), 0)
    nonzero = jnp.where(gap == 0, 1, gap).astype(jnp.float32)
    value = -1.0 / (math.pi * math.pi * nonzero * nonzero)
    value = jnp.where((gap & 1) == 1, value, 0.0)
    value = jnp.where(gap == 0, 0.25, value)
    return jnp.where(jnp.abs(gap) < TILE, value, 0.0)


EXTRA = 8
SPAN = TILE + 2 * EXTRA
ROWS = GROUP_ROWS + 2 * TV_STEPS


def pack_rows(y_ref, row_edge_ref):
    width = TILE // GROUPS
    group = lane_iota() // width
    for b in range(0, TILE, 16):
        for side in range(2):
            halves = []
            for half in range(2):
                span = slice(EXTRA + b + half * 8, EXTRA + b + half * 8 + 8)
                packed = None
                for i in range(TV_STEPS):
                    row = i if side == 0 else GROUP_ROWS - TV_STEPS + i
                    home = 0 if side == 0 else GROUPS - 1
                    value = pltpu.roll(y_ref[TV_STEPS + row, span, :], (width * (i - home)) % TILE, 1)
                    packed = value if packed is None else jnp.where(group == i, value, packed)
                halves.append(packed)
            row_edge_ref[side, b : b + 16, :] = jnp.concatenate(halves, axis=0).astype(jnp.bfloat16)


def pack_columns(y_ref, col_edge_ref, slices):
    first_tile = lane_iota() % (TILE // GROUPS) < slices
    half_rows = GROUP_ROWS // 2
    for j in range(0, half_rows, 2):
        for side in range(2):
            start = EXTRA if side == 0 else TILE
            span = slice(start, start + 8)
            parts = []
            for k in (j, j + 1):
                near = y_ref[TV_STEPS + k, span, :]
                far = y_ref[TV_STEPS + k + half_rows, span, :]
                if side == 0:
                    far = pltpu.roll(far, slices, 1)
                else:
                    near = pltpu.roll(near, TILE - slices, 1)
                parts.append(jnp.where(first_tile, near, far))
            col_edge_ref[side, j // 2] = jnp.concatenate(parts, axis=0).astype(jnp.bfloat16)


def update_kernel(
    starts_ref, first_ref, acc_ref, measured_ref, weight_ref, table_ref, x_ref, p_ref,
    sent_ref, scan_out, wide_ref, ramp_ref, landed, scan, target_ref, outgoing, returned, store_ref, q_ref,
    row_edge, col_edge, row_halo, col_halo, corner,
    shadow_sems, scan_sems, window_sems, edge_sems,
    *, slices, angles_here, slices_here, across, tile_rows,
):
    rows = lax.axis_size("row")
    cols = lax.axis_size("col")
    row = lax.axis_index("row")
    col = lax.axis_index("col")
    count = rows * cols
    me = row * cols + col

    def send(src, dst, sems, k, to_row, to_col):
        return pltpu.make_async_remote_copy(
            src_ref=src, dst_ref=dst, send_sem=sems.at[0, k], recv_sem=sems.at[1, k],
            device_id=(to_row, to_col), device_id_type=MESH,
        )

    width = TILE // GROUPS
    lanes = lane_iota()
    group = lanes // width
    first_tile = lanes % width < slices
    order = quad_source(angles_here, slices_here, slices, across)
    per_tile = angles_here * slices_here
    owners = slices // slices_here
    low, high = pl.ds(0, 16), pl.ds(TILE - 16, 16)
    routes = (
        (-1, 0, row_edge.at[0], row_halo.at[1]),
        (1, 0, row_edge.at[1], row_halo.at[0]),
        (0, -1, col_edge.at[0], col_halo.at[1]),
        (0, 1, col_edge.at[1], col_halo.at[0]),
        (-1, -1, row_edge.at[0, low], corner.at[1, 1]),
        (-1, 1, row_edge.at[0, high], corner.at[1, 0]),
        (1, -1, row_edge.at[1, low], corner.at[0, 1]),
        (1, 1, row_edge.at[1, high], corner.at[0, 0]),
    )

    def exists(down, right):
        to_row, to_col = row + down, col + right
        return (to_row >= 0) & (to_row < rows) & (to_col >= 0) & (to_col < cols)

    for r in range(rows):
        for a in range(angles_here):
            to = a * slices_here
            scan_out[r, to : to + slices_here] = measured_ref[
                a * slices + r * slices_here : a * slices + (r + 1) * slices_here
            ]
            scan_out[r, tile_rows + to : tile_rows + to + slices_here] = jnp.broadcast_to(
                weight_ref[a : a + 1], (slices_here, TILE)
            )
        if tile_rows > per_tile:
            spare = jnp.zeros((tile_rows - per_tile, TILE), jnp.float32)
            scan_out[r, per_tile:tile_rows] = spare
            scan_out[r, tile_rows + per_tile :] = spare
    row_halo[...] = jnp.zeros(row_halo.shape, row_halo.dtype)
    col_halo[...] = jnp.zeros(col_halo.shape, col_halo.dtype)
    corner[...] = jnp.zeros(corner.shape, corner.dtype)
    barrier = pltpu.get_barrier_semaphore()

    def peer(down, right):
        to_row, to_col = row + down, col + right
        to_row = jnp.where(to_row >= rows, to_row - rows, to_row)
        return to_row, jnp.where(to_col >= cols, to_col - cols, to_col)

    def all_peers(body, first=0):
        def some(j, carry):
            down = lax.rem(j + first, rows)

            @pl.when(down > 0)
            def _():
                body(down, 0)

            for right in range(1, cols):
                body(down, right)
            return carry

        lax.fori_loop(0, rows, some, jnp.int32(0))

    def greet(down, right):
        pl.semaphore_signal(barrier, inc=1, device_id=peer(down, right), device_id_type=MESH)

    all_peers(greet, rows // 2)

    near = pair_source(slices_here, slices, across)
    far = near ^ width
    piece = PAIR * slices_here
    kind_rows = TILE // 2

    def pick(span, values):
        result = acc_ref[values[0], span, :]
        for g in range(1, GROUPS):
            result = jnp.where(group == g, acc_ref[values[g], span, :], result)
        return result

    def pair_shadows(pair):
        here, there = pair * PAIR, pair * PAIR + 1
        pieces = []
        for b in range(TILE // 8):
            span = slice(MARGIN + b * 8, MARGIN + b * 8 + 8)
            own = pick(span, (here, ANGLES + there, ANGLES + here, there))
            other = pick(span, (there, ANGLES + here, ANGLES + there, here))
            pieces.append(lookup(own, near) + lookup(other, far))
        rows = jnp.concatenate(pieces, axis=0).T
        sent = []
        for e in range(kind_rows // 8):
            keys = []
            for r in range(e * 8, e * 8 + 8):
                a = r // slices_here % PAIR
                t = r // (slices_here * PAIR) % across
                start = starts_ref[row, col * across + t, pair * PAIR + a]
                keys.append(((a, t), start))
            index = (lanes - select_rows(keys)) & (TILE - 1)
            value = lookup(rows[e * 8 : e * 8 + 8], index) + lookup(
                rows[kind_rows + e * 8 : kind_rows + e * 8 + 8], TILE - 1 - index
            )
            sent.append(value * proj_scale)
        return jnp.concatenate(sent, axis=0)

    for owner in range(cols):
        pairs = angles_here // PAIR
        shadows = [pair_shadows(owner * pairs + p) for p in range(pairs)]
        for r in range(owners):
            parts = []
            for t in range(across):
                at = (r * across + t) * piece
                parts += [shadow[at : at + piece] for shadow in shadows]
                if tile_rows > per_tile:
                    parts.append(jnp.zeros((tile_rows - per_tile, TILE), jnp.float32))
            message = jnp.concatenate(parts, axis=0)
            sent_ref[r * cols + owner] = message.astype(jnp.bfloat16)

    pl.semaphore_wait(barrier, count - 1)

    def shadow_copy(down, right):
        k = down * cols + right
        to_row, to_col = peer(down, right)
        src = sent_ref.at[to_row * cols + to_col]
        return send(src, landed.at[k], shadow_sems, k, to_row, to_col)

    def scan_copy(down):
        to_row, to_col = peer(down, 0)
        return send(scan_out.at[to_row], scan.at[down], scan_sems, down, to_row, to_col)

    all_peers(lambda down, right: shadow_copy(down, right).start(), rows // 2)
    for down in range(1, rows):
        scan_copy(down).start()
    landed[0] = sent_ref[me]
    scan[0] = scan_out[row]

    sublanes = row_iota()

    def aim(down, carry):
        for right in range(cols):
            to_row, to_col = peer(down, right)
            for t in range(across):
                start = jnp.full(
                    (8, TILE), starts_ref[to_row, to_col * across + t, col * angles_here], jnp.int32
                )
                for a in range(1, angles_here):
                    value = starts_ref[to_row, to_col * across + t, col * angles_here + a]
                    start = jnp.where(sublanes >= a * slices_here, value, start)
                block = (start >> 7) + jnp.where(lanes < (start & (TILE - 1)), 1, 0)
                target_ref[down, right, t] = block
        return carry

    lax.fori_loop(0, rows, aim, jnp.int32(0))

    for k in range(GROUPS * ANGLES):
        store_ref[k, 0:MARGIN, :] = jnp.zeros((MARGIN, TILE), jnp.float32)
        store_ref[k, MARGIN + TILE :, :] = jnp.zeros((DEPTH - MARGIN - TILE, TILE), jnp.float32)
    for n in (-1, 0, 1):
        taps = ramp_table(n)
        coarse = taps.astype(jnp.bfloat16)
        ramp_ref[0, (n + 1) * TILE : (n + 2) * TILE] = coarse
        ramp_ref[1, (n + 1) * TILE : (n + 2) * TILE] = (
            taps - coarse.astype(jnp.float32)
        ).astype(jnp.bfloat16)

    def add(down, right, sums):
        message = landed[down * cols + right].astype(jnp.float32)
        back = lax.rem(rows - down, rows)
        for t in range(across):
            value = message[t * tile_rows : (t + 1) * tile_rows]
            target = target_ref[back, (cols - right) % cols, t]
            sums = tuple(
                total + jnp.where(target == b, value, 0.0) for b, total in enumerate(sums)
            )
        return sums

    zero = jnp.zeros((tile_rows, TILE), jnp.float32)
    sums = add(0, 0, (zero,) * rows)
    for right in range(1, cols):
        shadow_copy(0, right).wait_recv()
        sums = add(0, right, sums)

    def add_row(down, sums):
        for right in range(cols):
            shadow_copy(down, right).wait_recv()
        for right in range(cols):
            sums = add(down, right, sums)
        return sums

    sums = lax.fori_loop(1, rows, add_row, sums)
    for down in range(1, rows):
        scan_copy(down).wait_recv()
    residual = []
    for b in range(rows):
        here = scan[lax.rem(row - b + rows, rows)]
        residual.append(here[tile_rows:] * (here[:tile_rows] - sums[b]))
    stacked = jnp.concatenate(
        [
            jnp.concatenate([zero] + residual[:-1], axis=0),
            jnp.concatenate(residual, axis=0),
            jnp.concatenate(residual[1:] + [zero], axis=0),
        ],
        axis=1,
    )
    coarse = stacked.astype(jnp.bfloat16)
    fine = (stacked - coarse.astype(jnp.float32)).astype(jnp.bfloat16)
    both = jnp.dot(
        jnp.concatenate([coarse, fine], axis=0), ramp_ref[0], preferred_element_type=jnp.float32
    )
    filtered = both[: rows * tile_rows] + (
        both[rows * tile_rows :]
        + jnp.dot(coarse, ramp_ref[1], preferred_element_type=jnp.float32)
    )
    blocks = tuple(filtered[b * tile_rows : (b + 1) * tile_rows] for b in range(rows))

    def window(down, right):
        parts = []
        for t in range(across):
            target = target_ref[down, right, t]
            value = zero
            for b in range(rows):
                value = jnp.where(target == b, blocks[b], value)
            parts.append(value)
        return jnp.concatenate(parts, axis=0).astype(jnp.bfloat16)

    def window_copy(down, right):
        k = down * cols + right
        return send(outgoing.at[k], returned.at[me], window_sems, k, *peer(down, right))

    def reply(j, carry):
        down = lax.rem(j + rows // 2, rows)
        for right in range(cols):
            outgoing[down * cols + right] = window(down, right)
        pl.when(down > 0)(window_copy(down, 0).start)
        for right in range(1, cols):
            window_copy(down, right).start()
        return carry

    lax.fori_loop(0, rows, reply, jnp.int32(0), unroll=2)
    returned[me] = outgoing[0]

    pixel = row_iota()
    bins = (lanes % BINS).astype(jnp.float32)
    down = table_ref[BLOCKS : BLOCKS + 8]
    right = table_ref[BLOCKS + 8 :]
    for h in range(ANGLES * BINS // TILE):
        at = lanes // BINS + h * (TILE // BINS)
        down_here, right_here = lookup(down, at), lookup(right, at)
        span = slice(h * TILE, (h + 1) * TILE)
        for b in range(0, TILE, 8):
            pixel_row = ((pixel + b) // WIDE).astype(jnp.float32)
            pixel_column = ((pixel + b) % WIDE).astype(jnp.float32)
            q_ref[b : b + 8, span] = pixel_row * down_here + pixel_column * right_here - bins
        for g in range(GROUPS):
            for b in range(0, BLOCKS, 8):
                wide_ref[g, b : b + 8, span] = lookup(table_ref[b : b + 8], at + g * ANGLES)

    def turn(ur, carry):
        p_ref[TV_STEPS + ur, EXTRA : EXTRA + TILE, :] = to_pixels(x_ref, ur, across, slices) * (
            1.0 / descent_step
        )
        return carry

    lax.fori_loop(0, GROUP_ROWS, turn, jnp.int32(0), unroll=2)

    for quad in range(ANGLES // QUAD):
        parts = []
        for sub in range(QUAD // angles_here):
            at = quad * (QUAD // angles_here) + sub
            right = lax.rem(col - at + cols, cols)

            def arrived(down, carry, right=right):
                pl.when((down > 0) | (right > 0))(window_copy(down, right).wait_recv)
                return carry

            lax.fori_loop(0, rows, arrived, jnp.int32(0))
            for r in range(owners):
                message = returned[r * cols + at].astype(jnp.float32)
                for t in range(across):
                    parts.append(message[t * tile_rows : t * tile_rows + per_tile])
        flat = jnp.concatenate(parts, axis=0)
        turned = []
        for e in range(TILE // 8):
            keys = []
            for r in range(e * 8, e * 8 + 8):
                a = r // slices_here % angles_here
                t = r // (slices_here * angles_here) % across
                a = a + r // (slices_here * angles_here * across * owners) * angles_here
                start = starts_ref[row, col * across + t, quad * QUAD + a]
                keys.append(((a, t), start))
            shift = select_rows(keys)
            turned.append(lookup(flat[e * 8 : e * 8 + 8], (lanes + shift) & (TILE - 1)))
        bins_first = jnp.concatenate(turned, axis=0).T
        for b in range(TILE // 8):
            span = slice(MARGIN + b * 8, MARGIN + b * 8 + 8)
            value = lookup(bins_first[b * 8 : b * 8 + 8], order)
            for k in range(GROUPS):
                moved = pltpu.roll(value, width * k, 1) if k else value
                for a in range(QUAD):
                    g = (a + k) % GROUPS
                    store_ref[g * ANGLES + quad * QUAD + a, span, :] = jnp.where(
                        group == g, moved, 0.0
                    )

    def block(urb, vb):
        i = urb * RIGHT + vb
        top = urb * HIGH + TV_STEPS
        left = pl.multiple_of(vb * WIDE, WIDE) + EXTRA
        total = None
        for g in range(GROUPS):
            shadows = jnp.concatenate(
                [
                    store_ref[g * ANGLES + a, pl.ds(first_ref[i, g * ANGLES + a], BINS), :]
                    for a in range(ANGLES)
                ],
                axis=0,
            ).astype(jnp.bfloat16)
            weights = hat(q_ref[...] + wide_ref[g, pl.ds(i, 1), :])
            part = jnp.dot(weights, shadows, preferred_element_type=jnp.float32)
            total = part if total is None else total + part
        total = total * (relaxation * proj_scale / descent_step)
        for k in range(HIGH):
            p_ref[top + k, pl.ds(left, WIDE), :] = (
                p_ref[top + k, pl.ds(left, WIDE), :] + total[k * WIDE : (k + 1) * WIDE]
            )

    def outer_rows(i, carry):
        block((i // RIGHT) * (DOWN - 1), i % RIGHT)
        return carry

    def outer_columns(i, carry):
        block(1 + i // 2, (i % 2) * (RIGHT - 1))
        return carry

    def inner_blocks(i, carry):
        block(1 + i // (RIGHT - 2), 1 + i % (RIGHT - 2))
        return carry

    copies = []
    for k, (down, right, src, dst) in enumerate(routes):
        copy = pltpu.make_async_remote_copy(
            src_ref=src,
            dst_ref=dst,
            send_sem=edge_sems.at[0, k],
            recv_sem=edge_sems.at[1, k],
            device_id=(row + down, col + right),
            device_id_type=MESH,
        )
        copies.append((down, right, copy))
    lax.fori_loop(0, 2 * RIGHT, outer_rows, jnp.int32(0), unroll=8)
    pack_rows(p_ref, row_edge)
    for down, right, copy in copies:
        if down:
            pl.when(exists(down, right))(copy.start)
    lax.fori_loop(0, 2 * (DOWN - 2), outer_columns, jnp.int32(0), unroll=4)
    pack_columns(p_ref, col_edge, slices)
    for down, right, copy in copies:
        if not down:
            pl.when(exists(down, right))(copy.start)
    lax.fori_loop(0, (DOWN - 2) * (RIGHT - 2), inner_blocks, jnp.int32(0), unroll=6)
    for down, right, copy in copies:
        pl.when(exists(-down, -right))(copy.wait_recv)

    inner = slice(EXTRA, EXTRA + TILE)
    half_rows = GROUP_ROWS // 2

    def shift(value, by):
        by = by % TILE
        return pltpu.roll(value, by, 1) if by else value

    for i in range(TV_STEPS):
        for b in range(0, TILE, 16):
            above = row_halo[0, b : b + 16, :].astype(jnp.float32)
            below = row_halo[1, b : b + 16, :].astype(jnp.float32)
            for half in range(2):
                to = slice(EXTRA + b + half * 8, EXTRA + b + half * 8 + 8)
                piece = slice(half * 8, half * 8 + 8)
                p_ref[i, to, :] = jnp.where(
                    group == 0,
                    shift(above[piece], -width * i),
                    shift(p_ref[GROUP_ROWS + i, to, :], width),
                )
                p_ref[TV_STEPS + GROUP_ROWS + i, to, :] = jnp.where(
                    group == GROUPS - 1,
                    shift(below[piece], width * (GROUPS - 1 - i)),
                    shift(p_ref[TV_STEPS + i, to, :], -width),
                )

    left, right = [], []
    for j in range(half_rows):
        piece = slice((j % 2) * 8, (j % 2) * 8 + 8)
        left.append(col_halo[0, j // 2].astype(jnp.float32)[piece])
        right.append(col_halo[1, j // 2].astype(jnp.float32)[piece])

    def from_left(ur):
        return left[ur] if ur < half_rows else shift(left[ur - half_rows], -slices)

    def from_right(ur):
        return shift(right[ur], slices) if ur < half_rows else right[ur - half_rows]

    def corner_of(down, side):
        value = corner[down, side].astype(jnp.float32)
        return value[8:16] if side == 0 else value[0:8]

    for r in range(ROWS):
        ur = r - TV_STEPS
        if ur < 0:
            outer = [from_left(GROUP_ROWS + ur), from_right(GROUP_ROWS + ur)]
            edge = [
                shift(corner_of(0, 0), -width * r - slices),
                shift(corner_of(0, 1), -width * r + slices),
            ]
            outer = [jnp.where(group == 0, e, shift(o, width)) for e, o in zip(edge, outer)]
        elif ur >= GROUP_ROWS:
            i = ur - GROUP_ROWS
            outer = [from_left(i), from_right(i)]
            edge = [
                shift(corner_of(1, 0), width * (GROUPS - 1 - i) - slices),
                shift(corner_of(1, 1), width * (GROUPS - 1 - i) + slices),
            ]
            outer = [jnp.where(group == GROUPS - 1, e, shift(o, -width)) for e, o in zip(edge, outer)]
        else:
            outer = [from_left(ur), from_right(ur)]
        p_ref[r, 0:EXTRA, :] = jnp.where(
            first_tile, outer[0], shift(p_ref[r, TILE : TILE + EXTRA, :], slices)
        )
        p_ref[r, EXTRA + TILE :, :] = jnp.where(
            first_tile, shift(p_ref[r, EXTRA : 2 * EXTRA, :], -slices), outer[1]
        )

    for down, right, copy in copies:
        pl.when(exists(down, right))(copy.wait_send)
    def settle(down, right):
        shadow_copy(down, right).wait_send()
        window_copy(down, right).wait_send()

    all_peers(settle)
    for down in range(1, rows):
        scan_copy(down).wait_send()


def update(image, shadows, first, table, starts, measured, weight, x):
    rows = lax.axis_size("row")
    cols = lax.axis_size("col")
    slices, height, width = image.shape
    angles_here = ANGLES // cols
    slices_here = slices // rows
    tile_rows = tile_rows_of(angles_here, slices_here)
    count = rows * cols
    across = width // TILE
    message = pltpu.VMEM((count, across * tile_rows, TILE), jnp.bfloat16)
    kernel = lambda *refs: update_kernel(
        *refs, slices=slices, angles_here=angles_here, slices_here=slices_here,
        across=across, tile_rows=tile_rows,
    )
    dma = pltpu.SemaphoreType.DMA
    row_edge = pltpu.VMEM((2, TILE, TILE), jnp.bfloat16)
    col_edge = pltpu.VMEM((2, GROUP_ROWS // 4, 16, TILE), jnp.bfloat16)
    return pl.pallas_call(
        kernel,
        out_shape=pltpu.VMEM((ROWS, SPAN, TILE), jnp.float32),
        in_specs=[SMEM] * 2 + [VMEM] * 5,
        out_specs=VMEM,
        scratch_shapes=[
            message,
            pltpu.VMEM((rows, 2 * tile_rows, TILE), jnp.float32),
            pltpu.VMEM((GROUPS, BLOCKS, ANGLES * BINS), jnp.float32),
            pltpu.VMEM((2, 3 * TILE, TILE), jnp.bfloat16),
            message,
            pltpu.VMEM((rows, 2 * tile_rows, TILE), jnp.float32),
            pltpu.VMEM((rows, cols, across, tile_rows, TILE), jnp.int32),
            message,
            message,
            pltpu.VMEM((GROUPS * ANGLES, DEPTH, TILE), jnp.float32),
            pltpu.VMEM((TILE, ANGLES * BINS), jnp.float32),
            row_edge, col_edge, row_edge, col_edge,
            pltpu.VMEM((2, 2, 16, TILE), jnp.bfloat16),
            dma((2, count)),
            dma((2, rows)),
            dma((2, count)),
            dma((2, 8)),
        ],
        compiler_params=pltpu.CompilerParams(
            collective_id=0, has_side_effects=True, vmem_limit_bytes=40 << 20
        ),
        name="update",
    )(
        starts, first, shadows, measured, weight, table, x,
    )


def smooth_kernel(p_ref, out_ref, held_ref, z_ref, sems, *, slices, across):
    row = lax.axis_index("row")
    col = lax.axis_index("col")
    rows = lax.axis_size("row")
    cols = lax.axis_size("col")
    group = lane_iota() // (TILE // GROUPS)
    first_tile = lane_iota() % (TILE // GROUPS) < slices
    whole = z_ref.reshape(across, slices, GROUPS, GROUP_ROWS, TILE)
    writes = []
    one, nought = jnp.ones((8, TILE), jnp.float32), jnp.zeros((8, TILE), jnp.float32)

    def there(near, outside):
        return jnp.where(outside, jnp.where(near, one, nought), one)

    keep_above = there(row > 0, group == 0)[0:1]
    keep_below = there(row < rows - 1, group == GROUPS - 1)[0:1]
    keep_left = there(col > 0, first_tile)
    keep_right = there(col < cols - 1, jnp.logical_not(first_tile))

    limit = (smoothing / descent_step) ** 2
    columns = SPAN // 8
    sublanes = row_iota()
    head = sublanes == 0


    def sweep(source, r, above, emit, end):
        def at(r, j):
            return source[r, j * 8 : j * 8 + 8, :]

        below = []
        here, left = at(r, 0), None
        for j in range(end):
            k = min(j + 1, columns - 1)
            ahead = at(r, k)
            down = at(r + 1, j) - here
            if j < columns - 1:
                right = source[r, j * 8 + 1 : j * 8 + 9, :] - here
            else:
                right = pltpu.roll(here, 7, 0) - here
            scale = lax.rsqrt(limit + (down * down + right * right))
            down, right = down * scale, right * scale
            if emit is not None:
                moved = pltpu.roll(right, 1, 0)
                before = moved if left is None else jnp.where(head, left, moved)
                emit(j, (here - above[j]) + (down - before) + right)
                left = moved
            below.append(down)
            here = ahead
        return tuple(below)

    for step in range(TV_STEPS):
        low, high = step + 1, ROWS - 1 - step
        source = p_ref if step == 0 else held_ref
        end = columns - 1 if step == TV_STEPS - 1 else columns
        above_flow = sweep(source, step, None, None, end)

        def one_row(r, above_flow, place, source=source, end=end):
            values = []

            def emit(j, value):
                if place == "out":
                    values.append(value)
                    return
                if j == 0:
                    value = value * keep_left
                if j == columns - 1:
                    value = value * keep_right
                if place == "above":
                    value = value * keep_above
                if place == "below":
                    value = value * keep_below
                held_ref[r, j * 8 : j * 8 + 8, :] = value

            below_flow = sweep(source, r, above_flow, emit, end)
            if place == "out":
                kept = jnp.concatenate(values[EXTRA // 8 :], axis=0) * descent_step
                flipped = kept.T
                for g in range(GROUPS):
                    for t in range(across):
                        for s in range(0, slices, 8):
                            lane = (g * across + t) * slices + s
                            start = s * TILE + g * GROUP_ROWS + r - TV_STEPS
                            z_ref[t, pl.ds(start, 8, stride=TILE), :] = flipped[lane : lane + 8]
            return below_flow

        if step == TV_STEPS - 1:
            for c in range(GROUP_ROWS // CHUNK):
                span = range(low + c * CHUNK, low + (c + 1) * CHUNK)
                above_flow = lax.fori_loop(
                    span.start, span.stop, lambda r, f: one_row(r, f, "out"), above_flow, unroll=CHUNK
                )
                here = pl.ds(c * CHUNK, CHUNK)
                for t in range(across):
                    copy = pltpu.make_async_copy(
                        whole.at[t, :, :, here],
                        out_ref.at[:, :, here, pl.ds(t * TILE, TILE)],
                        sems.at[t, c],
                    )
                    copy.start()
                    writes.append(copy)
        else:
            for r in range(low, TV_STEPS):
                above_flow = one_row(r, above_flow, "above")
            above_flow = lax.fori_loop(
                TV_STEPS, TV_STEPS + GROUP_ROWS, lambda r, f: one_row(r, f, ""), above_flow, unroll=8
            )
            for r in range(TV_STEPS + GROUP_ROWS, high):
                above_flow = one_row(r, above_flow, "below")
    for copy in writes:
        copy.wait()


def smooth(p, image):
    slices, height, width = image.shape
    across = width // TILE
    kernel = lambda *refs: smooth_kernel(*refs, slices=slices, across=across)
    return pl.pallas_call(
        kernel,
        out_shape=jax.ShapeDtypeStruct((slices, GROUPS, GROUP_ROWS, width), jnp.float32),
        in_specs=[VMEM],
        out_specs=HBM,
        scratch_shapes=[
            pltpu.VMEM(p.shape, jnp.float32),
            pltpu.VMEM((across, slices * height, TILE), jnp.float32),
            pltpu.SemaphoreType.DMA((across, GROUP_ROWS // CHUNK)),
        ],
        compiler_params=pltpu.CompilerParams(vmem_limit_bytes=40 << 20),
        name="smooth",
    )(p).reshape(image.shape)


def local(current_image, measured, ray_weight, angle_ids, shadow_start):
    measured, weight = measured.reshape(-1, TILE), ray_weight.reshape(-1, TILE)
    made = project(current_image, angle_ids, shadow_start, measured, weight)
    return smooth(update(current_image, *made), current_image)


def solution(mesh):
    return jax.shard_map(
        local,
        mesh=mesh,
        in_specs=(
            P(None, "row", "col"),
            P("col", "row", None, None),
            P("col", "row", None),
            P(),
            P(),
        ),
        out_specs=P(None, "row", "col"),
        check_vma=False,
    )
```

```python
import math

import jax
import jax.numpy as jnp
from jax import lax
from jax.experimental import pallas as pl
from jax.experimental.pallas import tpu as pltpu
from jax.sharding import PartitionSpec as P

TILE = 128
ANGLES = 16
ALL_ANGLES = 256
TV_STEPS = 4
PACK = TILE // TV_STEPS

HIGH = 8
WIDE = 16
BINS = 16
MARGIN = 8
DEPTH = MARGIN + TILE + BINS
GROUPS = 4
GROUP_ROWS = TILE // GROUPS
DOWN = GROUP_ROWS // HIGH
RIGHT = TILE // WIDE
QUAD = 4
CHUNK = 8

inverse_root = 0.7071067811865476
proj_scale = 0.03125
relaxation = 8.0
smoothing = 0.25
descent_step = 0.05

MESH = pl.DeviceIdType.MESH
SMEM = pl.BlockSpec(memory_space=pltpu.SMEM)
VMEM = pl.BlockSpec(memory_space=pltpu.VMEM)
HBM = pl.BlockSpec(memory_space=pltpu.HBM)


def lookup(table, index):
    return jnp.take_along_axis(table, index, axis=1, mode="promise_in_bounds")


def lane_iota():
    return lax.broadcasted_iota(jnp.int32, (8, TILE), 1)


def row_iota():
    return lax.broadcasted_iota(jnp.int32, (8, TILE), 0)


BLOCKS = DOWN * RIGHT
PAIR = 2


def geometry(angle_ref):
    lanes = lane_iota()
    ids = jnp.zeros((8, TILE), jnp.int32)
    for a in range(ANGLES):
        ids = jnp.where(lanes % ANGLES == a, angle_ref[a], ids)
    radians = ids.astype(jnp.float32) * (math.pi / ALL_ANGLES)
    down = jnp.cos(radians) * inverse_root
    right = jnp.sin(radians) * inverse_root
    centre = (TILE - 1) / 2.0
    firsts, offsets = [], []
    for b in range(0, BLOCKS, 8):
        block = row_iota() + b
        row = (block // RIGHT) * HIGH + (lanes // ANGLES % GROUPS) * GROUP_ROWS
        column = (block % RIGHT) * WIDE
        row = row.astype(jnp.float32) - centre
        column = column.astype(jnp.float32) - centre
        place = TILE / 2.0 + (row * down + column * right)
        lowest = place + jnp.minimum(0.0, (HIGH - 1) * down) + jnp.minimum(0.0, (WIDE - 1) * right)
        first = jnp.floor(lowest - 0.5)
        firsts.append(first.astype(jnp.int32) + MARGIN)
        offsets.append(place - first - 0.5)
    return down, right, jnp.concatenate(firsts, axis=0), jnp.concatenate(offsets, axis=0)


def pair_source(slices_here, slices, across):
    lanes = lane_iota()
    owners = slices // slices_here
    s = lanes % slices_here
    a = lanes // slices_here % PAIR
    t = lanes // (slices_here * PAIR) % across
    r = lanes // (slices_here * PAIR * across) % owners
    kind = lanes // (slices_here * PAIR * across * owners)
    return ((kind * PAIR + a) * across + t) * slices + r * slices_here + s


def quad_source(angles_here, slices_here, slices, across):
    lanes = lane_iota()
    slice_ = lanes % slices
    t = lanes // slices % across
    angle = lanes // (slices * across)
    sub, a = angle // angles_here, angle % angles_here
    r, s = slice_ // slices_here, slice_ % slices_here
    owner = sub * (slices // slices_here) + r
    return ((owner * across + t) * angles_here + a) * slices_here + s


def select_rows(values):
    rows = row_iota()
    result = jnp.full((8, TILE), values[0][1], jnp.int32)
    for r in range(1, 8):
        if values[r][0] != values[r - 1][0]:
            result = jnp.where(rows >= r, values[r][1], result)
    return result


def hat(distance):
    return jnp.maximum(1.0 - jnp.abs(distance), 0.0).astype(jnp.bfloat16)


def to_pixels(z_ref, ur, across, slices, mirrored=GROUPS):
    parts = []
    mirror = TILE - 1 - lane_iota()
    for g in range(GROUPS):
        row = ur if g < mirrored else GROUP_ROWS - 1 - ur
        for t in range(across):
            for s in range(0, slices, 8):
                start = s * TILE + g * GROUP_ROWS + row
                part = z_ref[t, pl.ds(start, 8, stride=TILE), :]
                parts.append(part if g < mirrored else lookup(part, mirror))
    pixels = jnp.concatenate(parts, axis=0)
    return pixels.T if mirrored == GROUPS else pixels.astype(jnp.bfloat16).T


def forward_kernel(
    angle_ref, x_ref, starts_ref, measured_ref, weight_ref,
    acc_ref, first_out, table_out, starts_out, measured_out, weight_out, z_ref,
    xb_ref, q_ref, first_ref, offset_ref, sems, read_sems,
    *, slices, across,
):
    half = GROUPS // 2
    slices = x_ref.shape[0]
    whole = z_ref.reshape(across, slices, GROUPS, GROUP_ROWS, TILE)
    chunks = GROUP_ROWS // CHUNK
    copies = []
    for c in range(chunks):
        for t in range(across):
            for h, k in ((0, c), (half, chunks - 1 - c)):
                groups, here = pl.ds(h, half), pl.ds(k * CHUNK, CHUNK)
                copies.append(
                    pltpu.make_async_copy(
                        x_ref.at[:, groups, here, pl.ds(t * TILE, TILE)],
                        whole.at[t, :, groups, here],
                        read_sems.at[c, t, h // half],
                    )
                )
                copies[-1].start()

    passed = [
        pltpu.make_async_copy(starts_ref, starts_out, sems.at[2]),
        pltpu.make_async_copy(measured_ref, measured_out, sems.at[3]),
        pltpu.make_async_copy(weight_ref, weight_out, sems.at[4]),
    ]
    for copy in passed:
        copy.start()
    down, right, first, offset = geometry(angle_ref)
    first_out[...] = first
    table_out[0:BLOCKS] = offset
    table_out[BLOCKS : BLOCKS + 8] = down
    table_out[BLOCKS + 8 :] = right
    scalars = [
        pltpu.make_async_copy(first_out, first_ref, sems.at[5]),
        pltpu.make_async_copy(table_out.at[0:BLOCKS], offset_ref, sems.at[1]),
    ]
    for copy in scalars:
        copy.start()
    pixel = lane_iota()
    pixel_row = (pixel // WIDE).astype(jnp.float32)
    pixel_column = (pixel % WIDE).astype(jnp.float32)
    bins = row_iota().astype(jnp.float32)
    for a in range(ANGLES):
        at = jnp.full((8, TILE), a, jnp.int32)
        place = pixel_row * lookup(down, at) + pixel_column * lookup(right, at)
        for b in range(0, BINS, 8):
            q_ref[a, b : b + 8, :] = place - (bins + b)

    def clear(k, carry):
        acc_ref[k] = jnp.zeros((DEPTH, TILE), jnp.float32)
        return carry

    lax.fori_loop(0, half * ANGLES, clear, jnp.int32(0))

    def turn(ur, carry):
        xb_ref[ur] = to_pixels(z_ref, ur, across, slices, half)
        return carry

    for c in range(chunks):
        for copy in copies[c * 2 * across : (c + 1) * 2 * across]:
            copy.wait()
        lax.fori_loop(c * CHUNK, (c + 1) * CHUNK, turn, jnp.int32(0), unroll=CHUNK)
    for copy in scalars:
        copy.wait()

    def block(i, carry):
        top = (i // RIGHT) * HIGH
        left = pl.multiple_of((i % RIGHT) * WIDE, WIDE)
        pixels = jnp.concatenate(
            [xb_ref[top + k, pl.ds(left, WIDE), :] for k in range(HIGH)], axis=0
        )
        for g in range(half):
            weights = jnp.concatenate(
                [hat(q_ref[a] + offset_ref[i, g * ANGLES + a]) for a in range(ANGLES)], axis=0
            )
            shadow = jnp.dot(weights, pixels, preferred_element_type=jnp.float32)
            spans = [pl.ds(first_ref[i, g * ANGLES + a], BINS) for a in range(ANGLES)]
            olds = [acc_ref[g * ANGLES + a, spans[a], :] for a in range(ANGLES)]
            for a in range(ANGLES):
                acc_ref[g * ANGLES + a, spans[a], :] = (
                    olds[a] + shadow[a * BINS : (a + 1) * BINS]
                )
        return carry

    lax.fori_loop(0, BLOCKS, block, jnp.int32(0), unroll=8)
    for copy in passed:
        copy.wait()


def tile_rows_of(angles_here, slices_here):
    return pl.cdiv(angles_here * slices_here, 8) * 8


def project(image, angle_ids, starts, measured, weight):
    slices, height, width = image.shape
    across = width // TILE
    kernel = lambda *refs: forward_kernel(*refs, slices=slices, across=across)
    return pl.pallas_call(
        kernel,
        out_shape=[
            pltpu.VMEM((GROUPS // 2 * ANGLES, DEPTH, TILE), jnp.float32),
            pltpu.VMEM((BLOCKS, TILE), jnp.int32),
            pltpu.VMEM((BLOCKS + 16, TILE), jnp.float32),
            pltpu.VMEM(starts.shape, starts.dtype),
            pltpu.VMEM(measured.shape, measured.dtype),
            pltpu.VMEM(weight.shape, weight.dtype),
            pltpu.VMEM((across, slices * height, TILE), jnp.float32),
        ],
        in_specs=[SMEM] + [HBM] * 4,
        out_specs=[VMEM] * 7,
        scratch_shapes=[
            pltpu.VMEM((GROUP_ROWS, TILE, TILE), jnp.bfloat16),
            pltpu.VMEM((ANGLES, BINS, TILE), jnp.float32),
            pltpu.SMEM((BLOCKS, TILE), jnp.int32),
            pltpu.SMEM((BLOCKS, TILE), jnp.float32),
            pltpu.SemaphoreType.DMA((6,)),
            pltpu.SemaphoreType.DMA((GROUP_ROWS // CHUNK, across, 2)),
        ],
        compiler_params=pltpu.CompilerParams(vmem_limit_bytes=58 << 20),
        name="project",
    )(
        angle_ids, image.reshape(slices, GROUPS, GROUP_ROWS, width), starts, measured, weight
    )


def ramp_table(n):
    gap = lax.broadcasted_iota(jnp.int32, (TILE, TILE), 1) - n * TILE
    gap = gap - lax.broadcasted_iota(jnp.int32, (TILE, TILE), 0)
    nonzero = jnp.where(gap == 0, 1, gap).astype(jnp.float32)
    value = -1.0 / (math.pi * math.pi * nonzero * nonzero)
    value = jnp.where((gap & 1) == 1, value, 0.0)
    value = jnp.where(gap == 0, 0.25, value)
    return jnp.where(jnp.abs(gap) < TILE, value, 0.0)


EXTRA = 8
SPAN = TILE + 2 * EXTRA
ROWS = GROUP_ROWS + 2 * TV_STEPS


def pack_rows(y_ref, row_edge_ref):
    width = TILE // GROUPS
    group = lane_iota() // width
    for b in range(0, TILE, 16):
        for side in range(2):
            halves = []
            for half in range(2):
                span = slice(EXTRA + b + half * 8, EXTRA + b + half * 8 + 8)
                packed = None
                for i in range(TV_STEPS):
                    row = i if side == 0 else GROUP_ROWS - TV_STEPS + i
                    home = 0 if side == 0 else GROUPS - 1
                    value = pltpu.roll(y_ref[TV_STEPS + row, span, :], (width * (i - home)) % TILE, 1)
                    packed = value if packed is None else jnp.where(group == i, value, packed)
                halves.append(packed)
            row_edge_ref[side, b : b + 16, :] = jnp.concatenate(halves, axis=0).astype(jnp.bfloat16)


def pack_columns(y_ref, col_edge_ref, slices):
    first_tile = lane_iota() % (TILE // GROUPS) < slices
    half_rows = GROUP_ROWS // 2
    for j in range(0, half_rows, 2):
        for side in range(2):
            start = EXTRA if side == 0 else TILE
            span = slice(start, start + 8)
            parts = []
            for k in (j, j + 1):
                near = y_ref[TV_STEPS + k, span, :]
                far = y_ref[TV_STEPS + k + half_rows, span, :]
                if side == 0:
                    far = pltpu.roll(far, slices, 1)
                else:
                    near = pltpu.roll(near, TILE - slices, 1)
                parts.append(jnp.where(first_tile, near, far))
            col_edge_ref[side, j // 2] = jnp.concatenate(parts, axis=0).astype(jnp.bfloat16)


def update_kernel(
    starts_ref, first_ref, acc_ref, measured_ref, weight_ref, table_ref, x_ref, p_ref,
    sent_ref, scan_out, wide_ref, ramp_ref, landed, scan, target_ref, outgoing, returned, store_ref, q_ref,
    row_edge, col_edge, row_halo, col_halo, corner,
    shadow_sems, scan_sems, window_sems, edge_sems,
    *, slices, angles_here, slices_here, across, tile_rows,
):
    rows = lax.axis_size("row")
    cols = lax.axis_size("col")
    row = lax.axis_index("row")
    col = lax.axis_index("col")
    count = rows * cols
    me = row * cols + col

    def send(src, dst, sems, k, to_row, to_col):
        return pltpu.make_async_remote_copy(
            src_ref=src, dst_ref=dst, send_sem=sems.at[0, k], recv_sem=sems.at[1, k],
            device_id=(to_row, to_col), device_id_type=MESH,
        )

    width = TILE // GROUPS
    lanes = lane_iota()
    group = lanes // width
    first_tile = lanes % width < slices
    order = quad_source(angles_here, slices_here, slices, across)
    per_tile = angles_here * slices_here
    owners = slices // slices_here
    low, high = pl.ds(0, 16), pl.ds(TILE - 16, 16)
    routes = (
        (-1, 0, row_edge.at[0], row_halo.at[1]),
        (1, 0, row_edge.at[1], row_halo.at[0]),
        (0, -1, col_edge.at[0], col_halo.at[1]),
        (0, 1, col_edge.at[1], col_halo.at[0]),
        (-1, -1, row_edge.at[0, low], corner.at[1, 1]),
        (-1, 1, row_edge.at[0, high], corner.at[1, 0]),
        (1, -1, row_edge.at[1, low], corner.at[0, 1]),
        (1, 1, row_edge.at[1, high], corner.at[0, 0]),
    )

    def exists(down, right):
        to_row, to_col = row + down, col + right
        return (to_row >= 0) & (to_row < rows) & (to_col >= 0) & (to_col < cols)

    for r in range(rows):
        for a in range(angles_here):
            to = a * slices_here
            scan_out[r, to : to + slices_here] = measured_ref[
                a * slices + r * slices_here : a * slices + (r + 1) * slices_here
            ]
            scan_out[r, tile_rows + to : tile_rows + to + slices_here] = jnp.broadcast_to(
                weight_ref[a : a + 1], (slices_here, TILE)
            )
        if tile_rows > per_tile:
            spare = jnp.zeros((tile_rows - per_tile, TILE), jnp.float32)
            scan_out[r, per_tile:tile_rows] = spare
            scan_out[r, tile_rows + per_tile :] = spare
    row_halo[...] = jnp.zeros(row_halo.shape, row_halo.dtype)
    col_halo[...] = jnp.zeros(col_halo.shape, col_halo.dtype)
    corner[...] = jnp.zeros(corner.shape, corner.dtype)
    barrier = pltpu.get_barrier_semaphore()

    def peer(down, right):
        to_row, to_col = row + down, col + right
        to_row = jnp.where(to_row >= rows, to_row - rows, to_row)
        return to_row, jnp.where(to_col >= cols, to_col - cols, to_col)

    def all_peers(body, first=0):
        def some(j, carry):
            down = lax.rem(j + first, rows)

            @pl.when(down > 0)
            def _():
                body(down, 0)

            for right in range(1, cols):
                body(down, right)
            return carry

        lax.fori_loop(0, rows, some, jnp.int32(0))

    def greet(down, right):
        pl.semaphore_signal(barrier, inc=1, device_id=peer(down, right), device_id_type=MESH)

    all_peers(greet, rows // 2)

    near = pair_source(slices_here, slices, across)
    far = near ^ width
    piece = PAIR * slices_here
    kind_rows = TILE // 2

    def pick(span, values):
        result = acc_ref[values[0], span, :]
        for g in range(1, GROUPS):
            result = jnp.where(group == g, acc_ref[values[g], span, :], result)
        return result

    def pair_shadows(pair):
        here, there = pair * PAIR, pair * PAIR + 1
        pieces = []
        for b in range(TILE // 8):
            span = slice(MARGIN + b * 8, MARGIN + b * 8 + 8)
            own = pick(span, (here, ANGLES + there, ANGLES + here, there))
            other = pick(span, (there, ANGLES + here, ANGLES + there, here))
            pieces.append(lookup(own, near) + lookup(other, far))
        rows = jnp.concatenate(pieces, axis=0).T
        sent = []
        for e in range(kind_rows // 8):
            keys = []
            for r in range(e * 8, e * 8 + 8):
                a = r // slices_here % PAIR
                t = r // (slices_here * PAIR) % across
                start = starts_ref[row, col * across + t, pair * PAIR + a]
                keys.append(((a, t), start))
            index = (lanes - select_rows(keys)) & (TILE - 1)
            value = lookup(rows[e * 8 : e * 8 + 8], index) + lookup(
                rows[kind_rows + e * 8 : kind_rows + e * 8 + 8], TILE - 1 - index
            )
            sent.append(value * proj_scale)
        return jnp.concatenate(sent, axis=0)

    for owner in range(cols):
        pairs = angles_here // PAIR
        shadows = [pair_shadows(owner * pairs + p) for p in range(pairs)]
        for r in range(owners):
            parts = []
            for t in range(across):
                at = (r * across + t) * piece
                parts += [shadow[at : at + piece] for shadow in shadows]
                if tile_rows > per_tile:
                    parts.append(jnp.zeros((tile_rows - per_tile, TILE), jnp.float32))
            message = jnp.concatenate(parts, axis=0)
            sent_ref[r * cols + owner] = message.astype(jnp.bfloat16)

    pl.semaphore_wait(barrier, count - 1)

    def shadow_copy(down, right):
        k = down * cols + right
        to_row, to_col = peer(down, right)
        src = sent_ref.at[to_row * cols + to_col]
        return send(src, landed.at[k], shadow_sems, k, to_row, to_col)

    def scan_copy(down):
        to_row, to_col = peer(down, 0)
        return send(scan_out.at[to_row], scan.at[down], scan_sems, down, to_row, to_col)

    all_peers(lambda down, right: shadow_copy(down, right).start(), 1)
    for down in range(1, rows):
        scan_copy(down).start()
    landed[0] = sent_ref[me]
    scan[0] = scan_out[row]

    sublanes = row_iota()

    def aim(down, carry):
        for right in range(cols):
            to_row, to_col = peer(down, right)
            for t in range(across):
                start = jnp.full(
                    (8, TILE), starts_ref[to_row, to_col * across + t, col * angles_here], jnp.int32
                )
                for a in range(1, angles_here):
                    value = starts_ref[to_row, to_col * across + t, col * angles_here + a]
                    start = jnp.where(sublanes >= a * slices_here, value, start)
                block = (start >> 7) + jnp.where(lanes < (start & (TILE - 1)), 1, 0)
                target_ref[down, right, t] = block
        return carry

    lax.fori_loop(0, rows, aim, jnp.int32(0))

    for k in range(GROUPS * ANGLES):
        store_ref[k, 0:MARGIN, :] = jnp.zeros((MARGIN, TILE), jnp.float32)
        store_ref[k, MARGIN + TILE :, :] = jnp.zeros((DEPTH - MARGIN - TILE, TILE), jnp.float32)
    for n in (-1, 0, 1):
        taps = ramp_table(n)
        coarse = taps.astype(jnp.bfloat16)
        ramp_ref[0, (n + 1) * TILE : (n + 2) * TILE] = coarse
        ramp_ref[1, (n + 1) * TILE : (n + 2) * TILE] = (
            taps - coarse.astype(jnp.float32)
        ).astype(jnp.bfloat16)

    def add(down, right, sums):
        message = landed[down * cols + right].astype(jnp.float32)
        back = lax.rem(rows - down, rows)
        for t in range(across):
            value = message[t * tile_rows : (t + 1) * tile_rows]
            target = target_ref[back, (cols - right) % cols, t]
            sums = tuple(
                total + jnp.where(target == b, value, 0.0) for b, total in enumerate(sums)
            )
        return sums

    zero = jnp.zeros((tile_rows, TILE), jnp.float32)
    sums = add(0, 0, (zero,) * rows)
    for right in range(1, cols):
        shadow_copy(0, right).wait_recv()
        sums = add(0, right, sums)

    def add_row(down, sums):
        for right in range(cols):
            shadow_copy(down, right).wait_recv()
        for right in range(cols):
            sums = add(down, right, sums)
        return sums

    sums = lax.fori_loop(1, rows, add_row, sums)
    for down in range(1, rows):
        scan_copy(down).wait_recv()
    residual = []
    for b in range(rows):
        here = scan[lax.rem(row - b + rows, rows)]
        residual.append(here[tile_rows:] * (here[:tile_rows] - sums[b]))
    stacked = jnp.concatenate(
        [
            jnp.concatenate([zero] + residual[:-1], axis=0),
            jnp.concatenate(residual, axis=0),
            jnp.concatenate(residual[1:] + [zero], axis=0),
        ],
        axis=1,
    )
    coarse = stacked.astype(jnp.bfloat16)
    fine = (stacked - coarse.astype(jnp.float32)).astype(jnp.bfloat16)
    both = jnp.dot(
        jnp.concatenate([coarse, fine], axis=0), ramp_ref[0], preferred_element_type=jnp.float32
    )
    filtered = both[: rows * tile_rows] + (
        both[rows * tile_rows :]
        + jnp.dot(coarse, ramp_ref[1], preferred_element_type=jnp.float32)
    )
    blocks = tuple(filtered[b * tile_rows : (b + 1) * tile_rows] for b in range(rows))

    def window(down, right):
        parts = []
        for t in range(across):
            target = target_ref[down, right, t]
            value = zero
            for b in range(rows):
                value = jnp.where(target == b, blocks[b], value)
            parts.append(value)
        return jnp.concatenate(parts, axis=0).astype(jnp.bfloat16)

    def window_copy(down, right):
        k = down * cols + right
        return send(outgoing.at[k], returned.at[me], window_sems, k, *peer(down, right))

    def reply(j, carry):
        down = lax.rem(j + rows // 2, rows)
        for right in range(cols):
            outgoing[down * cols + right] = window(down, right)
        pl.when(down > 0)(window_copy(down, 0).start)
        for right in range(1, cols):
            window_copy(down, right).start()
        return carry

    lax.fori_loop(0, rows, reply, jnp.int32(0), unroll=2)
    returned[me] = outgoing[0]

    pixel = row_iota()
    bins = (lanes % BINS).astype(jnp.float32)
    down = table_ref[BLOCKS : BLOCKS + 8]
    right = table_ref[BLOCKS + 8 :]
    for h in range(ANGLES * BINS // TILE):
        at = lanes // BINS + h * (TILE // BINS)
        down_here, right_here = lookup(down, at), lookup(right, at)
        span = slice(h * TILE, (h + 1) * TILE)
        for b in range(0, TILE, 8):
            pixel_row = ((pixel + b) // WIDE).astype(jnp.float32)
            pixel_column = ((pixel + b) % WIDE).astype(jnp.float32)
            q_ref[b : b + 8, span] = pixel_row * down_here + pixel_column * right_here - bins
        for g in range(GROUPS):
            for b in range(0, BLOCKS, 8):
                wide_ref[g, b : b + 8, span] = lookup(table_ref[b : b + 8], at + g * ANGLES)

    def turn(ur, carry):
        p_ref[TV_STEPS + ur, EXTRA : EXTRA + TILE, :] = to_pixels(x_ref, ur, across, slices) * (
            1.0 / descent_step
        )
        return carry

    lax.fori_loop(0, GROUP_ROWS, turn, jnp.int32(0), unroll=2)

    for quad in range(ANGLES // QUAD):
        parts = []
        for sub in range(QUAD // angles_here):
            at = quad * (QUAD // angles_here) + sub
            right = lax.rem(col - at + cols, cols)

            def arrived(down, carry, right=right):
                pl.when((down > 0) | (right > 0))(window_copy(down, right).wait_recv)
                return carry

            lax.fori_loop(0, rows, arrived, jnp.int32(0))
            for r in range(owners):
                message = returned[r * cols + at].astype(jnp.float32)
                for t in range(across):
                    parts.append(message[t * tile_rows : t * tile_rows + per_tile])
        flat = jnp.concatenate(parts, axis=0)
        turned = []
        for e in range(TILE // 8):
            keys = []
            for r in range(e * 8, e * 8 + 8):
                a = r // slices_here % angles_here
                t = r // (slices_here * angles_here) % across
                a = a + r // (slices_here * angles_here * across * owners) * angles_here
                start = starts_ref[row, col * across + t, quad * QUAD + a]
                keys.append(((a, t), start))
            shift = select_rows(keys)
            turned.append(lookup(flat[e * 8 : e * 8 + 8], (lanes + shift) & (TILE - 1)))
        bins_first = jnp.concatenate(turned, axis=0).T
        for b in range(TILE // 8):
            span = slice(MARGIN + b * 8, MARGIN + b * 8 + 8)
            value = lookup(bins_first[b * 8 : b * 8 + 8], order)
            for k in range(GROUPS):
                moved = pltpu.roll(value, width * k, 1) if k else value
                for a in range(QUAD):
                    g = (a + k) % GROUPS
                    store_ref[g * ANGLES + quad * QUAD + a, span, :] = jnp.where(
                        group == g, moved, 0.0
                    )

    def block(urb, vb):
        i = urb * RIGHT + vb
        top = urb * HIGH + TV_STEPS
        left = pl.multiple_of(vb * WIDE, WIDE) + EXTRA
        total = None
        for g in range(GROUPS):
            shadows = jnp.concatenate(
                [
                    store_ref[g * ANGLES + a, pl.ds(first_ref[i, g * ANGLES + a], BINS), :]
                    for a in range(ANGLES)
                ],
                axis=0,
            ).astype(jnp.bfloat16)
            weights = hat(q_ref[...] + wide_ref[g, pl.ds(i, 1), :])
            part = jnp.dot(weights, shadows, preferred_element_type=jnp.float32)
            total = part if total is None else total + part
        total = total * (relaxation * proj_scale / descent_step)
        for k in range(HIGH):
            p_ref[top + k, pl.ds(left, WIDE), :] = (
                p_ref[top + k, pl.ds(left, WIDE), :] + total[k * WIDE : (k + 1) * WIDE]
            )

    def outer_rows(i, carry):
        block((i // RIGHT) * (DOWN - 1), i % RIGHT)
        return carry

    def outer_columns(i, carry):
        block(1 + i // 2, (i % 2) * (RIGHT - 1))
        return carry

    def inner_blocks(i, carry):
        block(1 + i // (RIGHT - 2), 1 + i % (RIGHT - 2))
        return carry

    copies = []
    for k, (down, right, src, dst) in enumerate(routes):
        copy = pltpu.make_async_remote_copy(
            src_ref=src,
            dst_ref=dst,
            send_sem=edge_sems.at[0, k],
            recv_sem=edge_sems.at[1, k],
            device_id=(row + down, col + right),
            device_id_type=MESH,
        )
        copies.append((down, right, copy))
    lax.fori_loop(0, 2 * RIGHT, outer_rows, jnp.int32(0), unroll=8)
    pack_rows(p_ref, row_edge)
    for down, right, copy in copies:
        if down:
            pl.when(exists(down, right))(copy.start)
    lax.fori_loop(0, 2 * (DOWN - 2), outer_columns, jnp.int32(0), unroll=4)
    pack_columns(p_ref, col_edge, slices)
    for down, right, copy in copies:
        if not down:
            pl.when(exists(down, right))(copy.start)
    lax.fori_loop(0, (DOWN - 2) * (RIGHT - 2), inner_blocks, jnp.int32(0), unroll=6)
    for down, right, copy in copies:
        pl.when(exists(-down, -right))(copy.wait_recv)

    inner = slice(EXTRA, EXTRA + TILE)
    half_rows = GROUP_ROWS // 2

    def shift(value, by):
        by = by % TILE
        return pltpu.roll(value, by, 1) if by else value

    for i in range(TV_STEPS):
        for b in range(0, TILE, 16):
            above = row_halo[0, b : b + 16, :].astype(jnp.float32)
            below = row_halo[1, b : b + 16, :].astype(jnp.float32)
            for half in range(2):
                to = slice(EXTRA + b + half * 8, EXTRA + b + half * 8 + 8)
                piece = slice(half * 8, half * 8 + 8)
                p_ref[i, to, :] = jnp.where(
                    group == 0,
                    shift(above[piece], -width * i),
                    shift(p_ref[GROUP_ROWS + i, to, :], width),
                )
                p_ref[TV_STEPS + GROUP_ROWS + i, to, :] = jnp.where(
                    group == GROUPS - 1,
                    shift(below[piece], width * (GROUPS - 1 - i)),
                    shift(p_ref[TV_STEPS + i, to, :], -width),
                )

    left, right = [], []
    for j in range(half_rows):
        piece = slice((j % 2) * 8, (j % 2) * 8 + 8)
        left.append(col_halo[0, j // 2].astype(jnp.float32)[piece])
        right.append(col_halo[1, j // 2].astype(jnp.float32)[piece])

    def from_left(ur):
        return left[ur] if ur < half_rows else shift(left[ur - half_rows], -slices)

    def from_right(ur):
        return shift(right[ur], slices) if ur < half_rows else right[ur - half_rows]

    def corner_of(down, side):
        value = corner[down, side].astype(jnp.float32)
        return value[8:16] if side == 0 else value[0:8]

    for r in range(ROWS):
        ur = r - TV_STEPS
        if ur < 0:
            outer = [from_left(GROUP_ROWS + ur), from_right(GROUP_ROWS + ur)]
            edge = [
                shift(corner_of(0, 0), -width * r - slices),
                shift(corner_of(0, 1), -width * r + slices),
            ]
            outer = [jnp.where(group == 0, e, shift(o, width)) for e, o in zip(edge, outer)]
        elif ur >= GROUP_ROWS:
            i = ur - GROUP_ROWS
            outer = [from_left(i), from_right(i)]
            edge = [
                shift(corner_of(1, 0), width * (GROUPS - 1 - i) - slices),
                shift(corner_of(1, 1), width * (GROUPS - 1 - i) + slices),
            ]
            outer = [jnp.where(group == GROUPS - 1, e, shift(o, -width)) for e, o in zip(edge, outer)]
        else:
            outer = [from_left(ur), from_right(ur)]
        p_ref[r, 0:EXTRA, :] = jnp.where(
            first_tile, outer[0], shift(p_ref[r, TILE : TILE + EXTRA, :], slices)
        )
        p_ref[r, EXTRA + TILE :, :] = jnp.where(
            first_tile, shift(p_ref[r, EXTRA : 2 * EXTRA, :], -slices), outer[1]
        )

    for down, right, copy in copies:
        pl.when(exists(down, right))(copy.wait_send)
    def settle(down, right):
        shadow_copy(down, right).wait_send()
        window_copy(down, right).wait_send()

    all_peers(settle)
    for down in range(1, rows):
        scan_copy(down).wait_send()


def update(image, shadows, first, table, starts, measured, weight, x):
    rows = lax.axis_size("row")
    cols = lax.axis_size("col")
    slices, height, width = image.shape
    angles_here = ANGLES // cols
    slices_here = slices // rows
    tile_rows = tile_rows_of(angles_here, slices_here)
    count = rows * cols
    across = width // TILE
    message = pltpu.VMEM((count, across * tile_rows, TILE), jnp.bfloat16)
    kernel = lambda *refs: update_kernel(
        *refs, slices=slices, angles_here=angles_here, slices_here=slices_here,
        across=across, tile_rows=tile_rows,
    )
    dma = pltpu.SemaphoreType.DMA
    row_edge = pltpu.VMEM((2, TILE, TILE), jnp.bfloat16)
    col_edge = pltpu.VMEM((2, GROUP_ROWS // 4, 16, TILE), jnp.bfloat16)
    return pl.pallas_call(
        kernel,
        out_shape=pltpu.VMEM((ROWS, SPAN, TILE), jnp.float32),
        in_specs=[SMEM] * 2 + [VMEM] * 5,
        out_specs=VMEM,
        scratch_shapes=[
            message,
            pltpu.VMEM((rows, 2 * tile_rows, TILE), jnp.float32),
            pltpu.VMEM((GROUPS, BLOCKS, ANGLES * BINS), jnp.float32),
            pltpu.VMEM((2, 3 * TILE, TILE), jnp.bfloat16),
            message,
            pltpu.VMEM((rows, 2 * tile_rows, TILE), jnp.float32),
            pltpu.VMEM((rows, cols, across, tile_rows, TILE), jnp.int32),
            message,
            message,
            pltpu.VMEM((GROUPS * ANGLES, DEPTH, TILE), jnp.float32),
            pltpu.VMEM((TILE, ANGLES * BINS), jnp.float32),
            row_edge, col_edge, row_edge, col_edge,
            pltpu.VMEM((2, 2, 16, TILE), jnp.bfloat16),
            dma((2, count)),
            dma((2, rows)),
            dma((2, count)),
            dma((2, 8)),
        ],
        compiler_params=pltpu.CompilerParams(
            collective_id=0, has_side_effects=True, vmem_limit_bytes=40 << 20
        ),
        name="update",
    )(
        starts, first, shadows, measured, weight, table, x,
    )


def smooth_kernel(p_ref, out_ref, held_ref, z_ref, sems, *, slices, across):
    row = lax.axis_index("row")
    col = lax.axis_index("col")
    rows = lax.axis_size("row")
    cols = lax.axis_size("col")
    group = lane_iota() // (TILE // GROUPS)
    first_tile = lane_iota() % (TILE // GROUPS) < slices
    whole = z_ref.reshape(across, slices, GROUPS, GROUP_ROWS, TILE)
    writes = []
    one, nought = jnp.ones((8, TILE), jnp.float32), jnp.zeros((8, TILE), jnp.float32)

    def there(near, outside):
        return jnp.where(outside, jnp.where(near, one, nought), one)

    keep_above = there(row > 0, group == 0)[0:1]
    keep_below = there(row < rows - 1, group == GROUPS - 1)[0:1]
    keep_left = there(col > 0, first_tile)
    keep_right = there(col < cols - 1, jnp.logical_not(first_tile))

    limit = (smoothing / descent_step) ** 2
    columns = SPAN // 8
    sublanes = row_iota()
    head = sublanes == 0


    def sweep(source, r, above, emit, end):
        def at(r, j):
            return source[r, j * 8 : j * 8 + 8, :]

        below = []
        here, left = at(r, 0), None
        for j in range(end):
            k = min(j + 1, columns - 1)
            ahead = at(r, k)
            down = at(r + 1, j) - here
            if j < columns - 1:
                right = source[r, j * 8 + 1 : j * 8 + 9, :] - here
            else:
                right = pltpu.roll(here, 7, 0) - here
            scale = lax.rsqrt(limit + (down * down + right * right))
            down, right = down * scale, right * scale
            if emit is not None:
                moved = pltpu.roll(right, 1, 0)
                before = moved if left is None else jnp.where(head, left, moved)
                emit(j, (here - above[j]) + (down - before) + right)
                left = moved
            below.append(down)
            here = ahead
        return tuple(below)

    for step in range(TV_STEPS):
        low, high = step + 1, ROWS - 1 - step
        source = p_ref if step == 0 else held_ref
        end = columns - 1 if step == TV_STEPS - 1 else columns
        above_flow = sweep(source, step, None, None, end)

        def one_row(r, above_flow, place, source=source, end=end):
            values = []

            def emit(j, value):
                if place == "out":
                    values.append(value)
                    return
                if j == 0:
                    value = value * keep_left
                if j == columns - 1:
                    value = value * keep_right
                if place == "above":
                    value = value * keep_above
                if place == "below":
                    value = value * keep_below
                held_ref[r, j * 8 : j * 8 + 8, :] = value

            below_flow = sweep(source, r, above_flow, emit, end)
            if place == "out":
                kept = jnp.concatenate(values[EXTRA // 8 :], axis=0) * descent_step
                flipped = kept.T
                for g in range(GROUPS):
                    for t in range(across):
                        for s in range(0, slices, 8):
                            lane = (g * across + t) * slices + s
                            start = s * TILE + g * GROUP_ROWS + r - TV_STEPS
                            z_ref[t, pl.ds(start, 8, stride=TILE), :] = flipped[lane : lane + 8]
            return below_flow

        if step == TV_STEPS - 1:
            for c in range(GROUP_ROWS // CHUNK):
                span = range(low + c * CHUNK, low + (c + 1) * CHUNK)
                above_flow = lax.fori_loop(
                    span.start, span.stop, lambda r, f: one_row(r, f, "out"), above_flow, unroll=CHUNK
                )
                here = pl.ds(c * CHUNK, CHUNK)
                for t in range(across):
                    copy = pltpu.make_async_copy(
                        whole.at[t, :, :, here],
                        out_ref.at[:, :, here, pl.ds(t * TILE, TILE)],
                        sems.at[t, c],
                    )
                    copy.start()
                    writes.append(copy)
        else:
            for r in range(low, TV_STEPS):
                above_flow = one_row(r, above_flow, "above")
            above_flow = lax.fori_loop(
                TV_STEPS, TV_STEPS + GROUP_ROWS, lambda r, f: one_row(r, f, ""), above_flow, unroll=8
            )
            for r in range(TV_STEPS + GROUP_ROWS, high):
                above_flow = one_row(r, above_flow, "below")
    for copy in writes:
        copy.wait()


def smooth(p, image):
    slices, height, width = image.shape
    across = width // TILE
    kernel = lambda *refs: smooth_kernel(*refs, slices=slices, across=across)
    return pl.pallas_call(
        kernel,
        out_shape=jax.ShapeDtypeStruct((slices, GROUPS, GROUP_ROWS, width), jnp.float32),
        in_specs=[VMEM],
        out_specs=HBM,
        scratch_shapes=[
            pltpu.VMEM(p.shape, jnp.float32),
            pltpu.VMEM((across, slices * height, TILE), jnp.float32),
            pltpu.SemaphoreType.DMA((across, GROUP_ROWS // CHUNK)),
        ],
        compiler_params=pltpu.CompilerParams(vmem_limit_bytes=40 << 20),
        name="smooth",
    )(p).reshape(image.shape)


def local(current_image, measured, ray_weight, angle_ids, shadow_start):
    measured, weight = measured.reshape(-1, TILE), ray_weight.reshape(-1, TILE)
    made = project(current_image, angle_ids, shadow_start, measured, weight)
    return smooth(update(current_image, *made), current_image)


def solution(mesh):
    return jax.shard_map(
        local,
        mesh=mesh,
        in_specs=(
            P(None, "row", "col"),
            P("col", "row", None, None),
            P("col", "row", None),
            P(),
            P(),
        ),
        out_specs=P(None, "row", "col"),
        check_vma=False,
    )
```
